128 devices in a mesh: gx: 8 (over y, core), gy: 16 (over z, x).
Axes of the slice: x: 4, y: 4, z: 4, core: 2. Of those that a mesh axis runs over, the one named last changes fastest.
Arguments:
- source_mass: float32 [4, 2048, 2048], P(None, 'gx', 'gy'), may hold values from 0.1 to 2
- target_density: float32 [4, 2048, 2048], P(None, 'gx', 'gy'), may hold values from 0.25 to 4
- potential: float32 [4, 2048, 2048], P(None, 'gx', 'gy'), may hold values from -6 to 6
- dest_device: int32 [8, 16, 128, 4], P('gx', 'gy'), may hold values from 0 to 127, all different within a row; in each aligned block of 128 rows (0 to 127, 128 to 255, ..., all dimensions but the last counted through in order) at most 6 rows name the same one
- dest_tile: int32 [8, 16, 128, 4], P('gx', 'gy'), may hold values from 0 to 127
- mass_counts: int32 [8, 16, 128, 4], P('gx', 'gy'), may hold values from 1 to 8
- reach: float32 [4], replicated, may hold values from 2 to 16384
Outputs:
- pushed: float32 [4, 2048, 2048], P(None, 'gx', 'gy')
- potential_next: float32 [4, 2048, 2048], P(None, 'gx', 'gy')
The draws below stay inside these ranges and needn't reach their ends.
Inputs may be any that keep to these rules, and one draw needn't show every extreme that they name: `dest_device`: within one block's 128 x 4 entries no destination block is named more than 6 times, and in some blocks one is named exactly 6 times; the 4 entries of one source tile name different blocks.
All inputs are finite; a program needn't handle non-finite values.
Results may differ from the reference program's by a relative error of at most 0.0001.
Values sent between devices are 32-bit elements; how exact they have to be, the bound alone decides.
A program may use at most 64 MiB of HBM per device.

```python
import math
import jax
import jax.numpy as jnp
import numpy as np
from jax import lax

NZ = 4
CX = 256
CY = 128
TS = 16
K = 4
TILES_DEV = 128
SLOTS = 6
NX = 2048
NY = 2048
N_GX = 8
N_GY = 16


def draw_reach(key, part):
    key_order = jax.random.fold_in(key, 11)
    key_short = jax.random.fold_in(key, 12)
    key_long = jax.random.fold_in(key, 13)
    order = jax.random.permutation(key_order, NZ)
    slow = order < NZ // 2
    short_reach = jnp.exp(jax.random.uniform(key_short, (NZ,), jnp.float32, jnp.log(2.0), jnp.log(40.0)))
    long_reach = jnp.exp(jax.random.uniform(key_long, (NZ,), jnp.float32, jnp.log(0.5 * NX), jnp.log(8.0 * NX)))
    return jnp.where(slow, long_reach, short_reach).astype(jnp.float32)


def touch_ends(result, own_key, low, top_value):
    longest = result.shape.index(max(result.shape))
    spots = []
    for shift in (0, 1):
        where = [jax.random.randint(jax.random.fold_in(own_key, axis), (), 0, length) for axis, length in enumerate(result.shape)]
        where[longest] = (where[longest] + shift) % result.shape[longest]
        spots.append(tuple(where))
    return result.at[spots[0]].set(low).at[spots[1]].set(top_value)


def levels(own_key, dims, cuts, smallest, top_value):
    loudness = 1.0
    for position, parts in cuts:
        heights = jax.random.uniform(jax.random.fold_in(jax.random.fold_in(own_key, 6), position), (parts,), jnp.float32, smallest / len(cuts), top_value / len(cuts))
        loudness = loudness * jnp.repeat(jnp.exp(heights), dims[position] // parts).reshape((-1,) + (1,) * (len(dims) - 1 - position))
    return loudness


def shared_out(key, own, number, rows, count, top, most, slope):
    sequence = jax.random.permutation(key, count)
    crowded, common = load_shares(count, rows * top, most, slope, True), load_shares(count, rows * top, most, slope, False)
    places = jnp.arange(count)

    def named(sizes, offset_by):
        used = int((sizes > 0).sum())
        fixed = max(1, used // 4)
        moved = fixed + (places - fixed + offset_by * (used - fixed)) % max(1, count - fixed)
        return jnp.zeros((count,), jnp.int32).at[sequence[jnp.where(places < fixed, places, moved)]].set(jnp.asarray(sizes, jnp.int32))

    sizes = jnp.where(number % 4 == 0, named(crowded, number // 4), named(common, number - number // 4 - 1))
    mixed = jax.random.permutation(jax.random.fold_in(own, 3), count)
    giver, receiver = mixed[0:count // 2 * 2:2], mixed[1:count // 2 * 2:2]
    margin = jnp.minimum(sizes[giver] - 1, most - sizes[receiver]) // 2
    margin = jnp.where((giver == sequence[0]) | (receiver == sequence[0]) | (sizes[receiver] == 0), 0, jnp.maximum(margin, 0))
    moved = jax.random.randint(jax.random.fold_in(own, 4), (count // 2,), 0, 1 << 20) % (margin + 1)
    sizes = sizes.at[giver].add(-moved).at[receiver].add(moved)
    items = jnp.searchsorted(jnp.cumsum(sizes), jnp.arange(rows * top), side="right").astype(jnp.int32)
    listing = items.reshape(top, rows).T
    listing = listing[jax.random.permutation(jax.random.fold_in(own, 1), rows)]
    offset_by = jax.random.randint(jax.random.fold_in(own, 2), (rows, 1), 0, top)
    return jnp.take_along_axis(listing, (jnp.arange(top)[None, :] + offset_by) % top, axis=1)


def load_shares(amount, total, most, lean, full):
    loads = [(1 << 20) // math.isqrt(standing ** lean) + 1 for standing in range(1, amount + 1)]
    largest = most if full else min(most, max(-(-total // amount), total * loads[0] // sum(loads)))
    least = 1 if total - largest >= amount - 1 else 0
    holding, rest = [largest] + [least] * (amount - 1), total - largest - least * (amount - 1)
    while rest > 0:
        movable = [i for i in range(1, amount) if holding[i] < largest] or [i for i in range(1, amount) if holding[i] < most]
        whole, remaining = sum([loads[i] for i in movable]), rest
        for i in movable:
            extra = min(most - holding[i], max(1, remaining * loads[i] // whole), rest)
            holding[i] = holding[i] + extra
            rest = rest - extra
    return np.array(holding)


def normal_values(rng, extent, width, most, pieces=(), dtype=jnp.bfloat16):
    entries = jax.random.normal(rng, extent, jnp.float32) * width
    if len(pieces) > 0:
        entries = levels(rng, extent, pieces, -0.22, 0.18) * entries
    return jnp.clip(entries, min=-most, max=most).astype(dtype)


def setup_inputs(seed: int = 0) -> dict:
    key_list = jax.random.split(jax.random.key(seed), 8)
    source_mass = jnp.clip(jnp.exp(math.log(2.0) - 2.9957323 * jax.random.uniform(key_list[0], (NZ, NX, NY), jnp.float32) ** levels(key_list[0], (NZ, NX, NY), ((1, 8), (2, 16)), -0.2, 0.2)), 0.1, 2.0)
    target_density = jnp.clip(jnp.exp(math.log(4.0) - 2.7725887 * jax.random.uniform(key_list[1], (NZ, NX, NY), jnp.float32) ** levels(key_list[1], (NZ, NX, NY), ((1, 8), (2, 16)), -0.2, 0.2)), 0.25, 4.0)
    potential = normal_values(key_list[2], (NZ, NX, NY), 1.0, 6.0, ((1, 8), (2, 16)), jnp.float32)
    dest_device_keys = jax.random.split(jax.random.fold_in(key_list[3], 1), N_GX * N_GY * TILES_DEV // TILES_DEV)
    dest_device_turns = jax.random.permutation(jax.random.fold_in(key_list[3], 3), N_GX * N_GY * TILES_DEV // TILES_DEV)
    dest_device = jax.vmap(lambda own, number: shared_out(jax.random.fold_in(key_list[3], 2), own, number, TILES_DEV, N_GX * N_GY, K, SLOTS, 2))(dest_device_keys, dest_device_turns).reshape((N_GX, N_GY, TILES_DEV, K))
    dest_tile = touch_ends(jax.random.randint(key_list[4], (N_GX, N_GY, TILES_DEV, K), 0, TILES_DEV), jax.random.fold_in(key_list[4], 1), 0, TILES_DEV - 1).astype(jnp.int32)
    mass_counts = touch_ends(jax.random.randint(key_list[5], (N_GX, N_GY, TILES_DEV, K), 1, 9), jax.random.fold_in(key_list[5], 1), 1, 8).astype(jnp.int32)
    reach = draw_reach(jax.random.fold_in(key_list[7], 71), 0)
    return {"source_mass": source_mass, "target_density": target_density, "potential": potential, "dest_device": dest_device, "dest_tile": dest_tile, "mass_counts": mass_counts, "reach": reach}


def line_pass(lines, decay):
    scale = (1.0 - decay) ** 2

    def ahead(carry, value):
        fresh = value + decay * carry
        return fresh, fresh

    def behind(carry, value):
        fresh = scale * value + decay * carry
        return fresh, fresh

    _, forward = lax.scan(ahead, jnp.zeros_like(lines[0]), lines)
    _, backward = lax.scan(behind, jnp.zeros_like(lines[0]), forward, reverse=True)
    return backward


def reference(source_mass, target_density, potential, dest_device, dest_tile, mass_counts, reach):
    tiles_x = CX // TS
    tiles_y = CY // TS
    total_tiles = N_GX * N_GY * TILES_DEV
    tiles = source_mass.reshape(NZ, N_GX, tiles_x, TS, N_GY, tiles_y, TS)
    tiles = tiles.transpose(1, 4, 2, 5, 0, 3, 6).reshape(total_tiles, NZ * TS * TS)
    counts = mass_counts.astype(jnp.float32)
    shares = (counts / jnp.sum(counts, axis=-1, keepdims=True)).reshape(total_tiles, K)
    target_index = (dest_device * TILES_DEV + dest_tile).reshape(total_tiles, K).astype(jnp.int32)
    pushed_tiles = jnp.zeros_like(tiles)
    for entry in range(K):
        pushed_tiles = pushed_tiles + jax.ops.segment_sum(tiles * shares[:, entry:entry + 1], target_index[:, entry], num_segments=total_tiles)
    pushed = pushed_tiles.reshape(N_GX, N_GY, tiles_x, tiles_y, NZ, TS, TS)
    pushed = pushed.transpose(4, 0, 2, 5, 1, 3, 6).reshape(NZ, NX, NY)
    mismatch = target_density - pushed
    decay = (1.0 - 1.0 / reach)[:, None]
    smoothed_x = line_pass(mismatch.transpose(1, 0, 2), decay).transpose(1, 0, 2)
    correction = line_pass(smoothed_x.transpose(2, 0, 1), decay).transpose(1, 2, 0)
    return pushed, potential + correction
```

```python
import functools
import jax
import jax.numpy as jnp
from jax import lax
from jax.experimental import pallas as pl
from jax.experimental.pallas import tpu as pltpu
from jax.sharding import PartitionSpec as P

MESH = pl.DeviceIdType.MESH
TS = 16
SLOTS = 6
LANES = 128
STEP = 37
CHUNKS = 4
F32 = jnp.float32
BF16 = jnp.bfloat16


def split2(a):
    hi = a.astype(BF16)
    return hi, (a - hi.astype(F32)).astype(BF16)


def split3(a):
    hi = a.astype(BF16)
    rest = a - hi.astype(F32)
    mid = rest.astype(BF16)
    return hi, mid, (rest - mid.astype(F32)).astype(BF16)


def dot(a, b, dims=((1,), (0,))):
    return lax.dot_general(a, b, (dims, ((), ())), preferred_element_type=F32)


def dot3(a, b, dims=((1,), (0,))):
    ah, al = a
    bh, bl = b
    return dot(ah, bh, dims) + (dot(ah, bl, dims) + dot(al, bh, dims))


def dot_f32(a, b, dims=((1,), (0,))):
    return lax.dot_general(
        a, b, (dims, ((), ())), precision=lax.Precision.HIGHEST, preferred_element_type=F32
    )


def iota(shape, axis):
    return lax.broadcasted_iota(jnp.int32, shape, axis)


def block_transpose(vectors):
    lane_block = iota((8, LANES), 1) // TS
    vectors = list(vectors)
    for bit in (4, 2, 1):
        low = (lane_block & bit) == 0
        result = [None] * 8
        for a in range(8):
            if a & bit:
                continue
            b = a | bit
            up, down = vectors[a], vectors[b]
            result[a] = jnp.where(low, up, pltpu.roll(down, bit * TS, 1))
            result[b] = jnp.where(low, pltpu.roll(up, LANES - bit * TS, 1), down)
        vectors = result
    return vectors


def displaced(p, q, row):
    shift = (row * STEP) & 127
    dp, dq = shift >> 4, shift & 15
    tp = ((((p >> 1) + (dp >> 1)) & 3) << 1) + (((p & 1) + (dp & 1)) & 1)
    tq = ((((q >> 2) + (dq >> 2)) & 3) << 2) + (((q & 3) + (dq & 3)) & 3)
    return tp, tq


def powers(logs, exponent):
    return jnp.exp(exponent.astype(F32) * logs)


def kernel(
    source_ref, target_ref, potential_ref, device_ref, tile_ref, count_ref, reach_ref,
    pushed_ref, next_ref,
    natural, tiles, packed, packed_labels, arrived, arrived_labels, gathered,
    target, potential, xtab_hi, xtab_lo, ytab_hi, ytab_lo, xmsg, xall, ymsg, yall, smooth,
    load_sem, self_sem, send_sem, recv_sem, label_send, label_recv, store_sem,
    x_send, x_recv, y_send, y_recv,
):
    p, q = lax.axis_index("gx"), lax.axis_index("gy")
    devices, n_gx, n_gy = 128, 8, 16
    planes, cx, cy = source_ref.shape
    tile_rows, tile_cols = cx // TS, cy // TS
    rows_per = SLOTS * 8

    load = pltpu.make_async_copy(source_ref, natural, load_sem.at[0])
    load.start()
    load_target = pltpu.make_async_copy(target_ref, target, load_sem.at[1])
    load_target.start()
    load_potential = pltpu.make_async_copy(potential_ref, potential, load_sem.at[2])
    load_potential.start()

    barrier = pltpu.get_barrier_semaphore()

    def greet(row, carry):
        pl.semaphore_signal(barrier, inc=1, device_id=displaced(p, q, row), device_id_type=MESH)
        return carry

    lax.fori_loop(1, devices, greet, 0)

    names = device_ref[...]
    places = tile_ref[...].astype(F32)
    counts = count_ref[...].astype(F32)
    shares = counts / jnp.sum(counts, axis=0, keepdims=True)
    row_p, row_q = displaced(p, q, iota((devices, LANES), 0))
    owner = row_p * n_gy + row_q
    named = jnp.zeros((devices, LANES), F32)
    share = jnp.zeros((devices, LANES), F32)
    place = jnp.zeros((devices, LANES), F32)
    for j in range(names.shape[0]):
        match = (owner == names[j : j + 1, :]).astype(F32)
        named += match
        share += match * shares[j : j + 1, :]
        place += match * places[j : j + 1, :]
    earlier = (iota((LANES, LANES), 0) < iota((LANES, LANES), 1)).astype(BF16)
    rank = dot(named.astype(BF16), earlier)
    lane = iota((devices, LANES), 1)
    labels = jnp.zeros((devices, LANES), F32)
    picks, weights = [], []
    for k in range(SLOTS):
        pick = jnp.where(rank == float(k), named, 0.0)
        picks.append(pick.astype(BF16))
        weights.append(jnp.sum(pick * share, axis=1, keepdims=True))
        label = jnp.sum(pick * place, axis=1, keepdims=True)
        labels = jnp.where(lane == k, label, labels)
    packed_labels[...] = labels[:, None, :]

    load.wait()
    for xo in range(tile_rows):
        parts = [
            natural[g // 2, pl.ds(xo * TS + (g % 2) * 8, 8), :] for g in range(2 * planes)
        ]
        for yo, value in enumerate(block_transpose(parts)):
            tiles[pl.ds((xo * tile_cols + yo) * 8, 8), :] = value
    parts = []
    for c in range(8):
        parts.append(split3(tiles[pl.ds(c, LANES, stride=8), :]))

    chunk = devices // CHUNKS
    for g in range(CHUNKS):
        pick = jnp.concatenate([a[g * chunk : (g + 1) * chunk] for a in picks], axis=0)
        pick3 = jnp.concatenate([pick, pick, pick], axis=1)
        for c in range(8):
            value = dot(pick3, jnp.concatenate(parts[c], axis=0))
            for k in range(SLOTS):
                packed[pl.ds(g * chunk * rows_per + k * 8 + c, chunk, stride=rows_per), :] = (
                    value[k * chunk : (k + 1) * chunk] * weights[k][g * chunk : (g + 1) * chunk]
                )
        if g == 0:
            pl.semaphore_wait(barrier, devices - 1)

        def send(row, carry):
            to = displaced(p, q, row)
            start = pl.multiple_of(row * rows_per, 8)
            pltpu.make_async_remote_copy(
                src_ref=packed.at[pl.ds(start, rows_per)],
                dst_ref=arrived.at[pl.ds(start, rows_per)],
                send_sem=send_sem,
                recv_sem=recv_sem.at[g],
                device_id=to,
                device_id_type=MESH,
            ).start()
            pltpu.make_async_remote_copy(
                src_ref=packed_labels.at[row],
                dst_ref=arrived_labels.at[row],
                send_sem=label_send,
                recv_sem=label_recv,
                device_id=to,
                device_id_type=MESH,
            ).start()
            return carry

        lax.fori_loop(max(g * chunk, 1), (g + 1) * chunk, send, 0)
    own = pltpu.make_async_copy(
        packed.at[pl.ds(0, rows_per)], arrived.at[pl.ds(0, rows_per)], self_sem.at[0]
    )
    own.start()
    own_label = pltpu.make_async_copy(packed_labels.at[0], arrived_labels.at[0], self_sem.at[1])
    own_label.start()

    decay = [1.0 - 1.0 / reach_ref[z] for z in range(planes)]
    decay = [jnp.full((1, 1), d, F32) for d in decay]
    logs = [jnp.log(d) for d in decay]
    scale = [(1.0 - d) ** 2 for d in decay]

    def tables(z, n):
        gap = iota((n, n), 0) - iota((n, n), 1)
        lower = jnp.where(gap >= 0, powers(logs[z], jnp.maximum(gap, 0)), 0.0)
        both = scale[z] * dot_f32(lower, lower, ((0,), (0,)))
        return both

    for z in range(planes):
        hi, lo = split2(tables(z, cx))
        xtab_hi[z], xtab_lo[z] = hi, lo
        hi, lo = split2(tables(z, cy))
        ytab_hi[z], ytab_lo[z] = hi, lo

    def edges(z, n):
        at = iota((1, n), 1)
        last = powers(logs[z], n - 1 - at)
        rise = powers(logs[z], at + 1)
        fall = powers(logs[z], n - at)
        gap = iota((n, n), 0) - iota((n, n), 1)
        lower = jnp.where(gap >= 0, powers(logs[z], jnp.maximum(gap, 0)), 0.0)
        swept = scale[z] * dot_f32(jnp.broadcast_to(rise, (8, n)), lower)[0:1]
        return last, swept, fall

    x_edges = [edges(z, cx) for z in range(planes)]
    y_edges = [edges(z, cy) for z in range(planes)]

    def whole(ref, first, count, sem):
        part = ref.at[pl.ds(first, count)]
        pltpu.make_async_copy(part, part, sem).wait()

    own.wait()
    own_label.wait()
    whole(arrived_labels, 1, devices - 1, label_recv)
    label_lanes = jnp.transpose(arrived_labels[...].reshape(devices, LANES))
    tile_index = iota((LANES, LANES), 0).astype(F32)
    wanted = [(label_lanes[k : k + 1, :] == tile_index).astype(BF16) for k in range(SLOTS)]
    sums = [jnp.zeros((LANES, LANES), F32) for _ in range(8)]
    for g in range(CHUNKS):
        first = 1 if g == 0 else g * chunk
        whole(arrived, first * rows_per, ((g + 1) * chunk - first) * rows_per, recv_sem.at[g])
        select = jnp.concatenate([w[:, g * chunk : (g + 1) * chunk] for w in wanted], axis=1)
        for c in range(8):
            rows = jnp.concatenate(
                [
                    arrived[pl.ds(g * chunk * rows_per + k * 8 + c, chunk, stride=rows_per), :]
                    for k in range(SLOTS)
                ],
                axis=0,
            )
            hi, mid, lo = split3(rows)
            sums[c] = sums[c] + (dot(select, hi) + (dot(select, mid) + dot(select, lo)))
    for c in range(8):
        tiles[pl.ds(c, LANES, stride=8), :] = sums[c]
    for xo in range(tile_rows):
        parts = [tiles[pl.ds((xo * tile_cols + yo) * 8, 8), :] for yo in range(tile_cols)]
        for g, value in enumerate(block_transpose(parts)):
            gathered[g // 2, pl.ds(xo * TS + (g % 2) * 8, 8), :] = value
    store_pushed = pltpu.make_async_copy(gathered, pushed_ref, store_sem.at[0])
    store_pushed.start()

    load_target.wait()
    row8 = iota((8, 1), 0)
    ends = jnp.zeros((8, cy), F32)
    for z in range(planes):
        mismatch = target[z] - gathered[z]
        m2 = split2(mismatch)
        base = dot3((xtab_hi[z], xtab_lo[z]), m2)
        smooth[z] = base
        weights8 = jnp.where(row8 == z, x_edges[z][0], 0.0)
        ends += dot_f32(weights8, mismatch)
        ends += jnp.where(row8 == planes + z, base[0:1], 0.0)
    xmsg[...] = ends

    def line_peer(i):
        return ((((p >> 1) + (i >> 1)) & 3) << 1) + (((p & 1) + (i & 1)) & 1)

    def send_x(i, carry):
        pltpu.make_async_remote_copy(
            src_ref=xmsg, dst_ref=xall.at[p], send_sem=x_send, recv_sem=x_recv,
            device_id=(line_peer(i), q), device_id_type=MESH,
        ).start()
        return carry

    lax.fori_loop(1, n_gx, send_x, 0)
    xall[p] = ends
    xmsg_done = pltpu.make_async_copy(
        xall.at[pl.ds(0, n_gx - 1)], xall.at[pl.ds(0, n_gx - 1)], x_recv
    )
    xmsg_done.wait()

    def boundary(all_ref, count, here, across, first_swept, width):
        low = row8 < planes
        entering = jnp.zeros((8, width), F32)
        entry, picked = [], jnp.zeros((8, width), F32)
        for i in range(count):
            entry.append(entering)
            picked = jnp.where(here == i, entering, picked)
            entering = jnp.where(low, across * entering + all_ref[i], 0.0)
        leaving = jnp.zeros((8, width), F32)
        out = jnp.zeros((8, width), F32)
        for i in reversed(range(count)):
            out = jnp.where(here == i, leaving, out)
            begun = all_ref[i] + pltpu.roll(first_swept * entry[i], planes, 0)
            leaving = jnp.where(low, 0.0, across * leaving + begun)
        return picked + out

    def column8(values):
        result = jnp.zeros((8, 1), F32)
        for z, v in enumerate(values):
            result = jnp.where((row8 == z) | (row8 == planes + z), v, result)
        return result

    across_x = column8([powers(logs[z], jnp.full((1, 1), cx, jnp.int32)) for z in range(planes)])
    across_y = column8([powers(logs[z], jnp.full((1, 1), cy, jnp.int32)) for z in range(planes)])
    swept_x = column8([x_edges[z][1][:, 0:1] for z in range(planes)])
    swept_y = column8([y_edges[z][1][:, 0:1] for z in range(planes)])

    def spread(z, edge):
        return jnp.where(row8 == z, edge[1], 0.0) + jnp.where(row8 == planes + z, edge[2], 0.0)

    inflow = boundary(xall, n_gx, p, across_x, swept_x, cy)
    ends = jnp.zeros((8, cx), F32)
    for z in range(planes):
        value = smooth[z] + dot_f32(spread(z, x_edges[z]), inflow, ((0,), (0,)))
        smooth[z] = value
        start_row = ytab_hi[z][0:1].astype(F32) + ytab_lo[z][0:1].astype(F32)
        weights8 = jnp.where(row8 == z, y_edges[z][0], 0.0) + jnp.where(
            row8 == planes + z, start_row, 0.0
        )
        ends += dot_f32(weights8, value, ((1,), (1,)))
    ymsg[...] = ends

    def send_y(i, carry):
        to = ((((q >> 2) + (i >> 2)) & 3) << 2) + (((q & 3) + (i & 3)) & 3)
        pltpu.make_async_remote_copy(
            src_ref=ymsg, dst_ref=yall.at[q], send_sem=y_send, recv_sem=y_recv,
            device_id=(p, to), device_id_type=MESH,
        ).start()
        return carry

    lax.fori_loop(1, n_gy, send_y, 0)
    yall[q] = ends
    load_potential.wait()
    for z in range(planes):
        potential[z] = potential[z] + dot3(split2(smooth[z]), (ytab_hi[z], ytab_lo[z]))
    part = yall.at[pl.ds(0, n_gy - 1)]
    pltpu.make_async_copy(part, part, y_recv).wait()
    inflow = boundary(yall, n_gy, q, across_y, swept_y, cx)
    for z in range(planes):
        potential[z] = potential[z] + dot_f32(inflow, spread(z, y_edges[z]), ((0,), (0,)))
    store_next = pltpu.make_async_copy(potential, next_ref, store_sem.at[1])
    store_next.start()

    whole(packed, rows_per, (devices - 1) * rows_per, send_sem)
    whole(packed_labels, 1, devices - 1, label_send)
    whole(xall, 0, n_gx - 1, x_send)
    whole(yall, 0, n_gy - 1, y_send)
    store_pushed.wait()
    store_next.wait()


def per_device(source_mass, target_density, potential, dest_device, dest_tile, mass_counts, reach):
    planes, cx, cy = source_mass.shape

    def lanes(a):
        return jnp.swapaxes(a.reshape(a.shape[2:]), 0, 1)

    rows = LANES * SLOTS * 8
    hbm = pl.BlockSpec(memory_space=pl.ANY)
    vmem = pl.BlockSpec(memory_space=pltpu.VMEM)
    dma = pltpu.SemaphoreType.DMA
    grid = jax.ShapeDtypeStruct((planes, cx, cy), F32)
    return pl.pallas_call(
        kernel,
        out_shape=(grid, grid),
        in_specs=[hbm, hbm, hbm, vmem, vmem, vmem, pl.BlockSpec(memory_space=pltpu.SMEM)],
        out_specs=(hbm, hbm),
        scratch_shapes=[
            pltpu.VMEM((planes, cx, cy), F32),
            pltpu.VMEM((LANES * 8, LANES), F32),
            pltpu.VMEM((rows, LANES), F32),
            pltpu.VMEM((LANES, 1, LANES), F32),
            pltpu.VMEM((rows, LANES), F32),
            pltpu.VMEM((LANES, 1, LANES), F32),
            pltpu.VMEM((planes, cx, cy), F32),
            pltpu.VMEM((planes, cx, cy), F32),
            pltpu.VMEM((planes, cx, cy), F32),
            pltpu.VMEM((planes, cx, cx), BF16),
            pltpu.VMEM((planes, cx, cx), BF16),
            pltpu.VMEM((planes, cy, cy), BF16),
            pltpu.VMEM((planes, cy, cy), BF16),
            pltpu.VMEM((8, cy), F32),
            pltpu.VMEM((8, 8, cy), F32),
            pltpu.VMEM((8, cx), F32),
            pltpu.VMEM((16, 8, cx), F32),
            pltpu.VMEM((planes, cx, cy), F32),
            dma((3,)),
            dma((2,)),
            dma,
            dma((CHUNKS,)),
            dma,
            dma,
            dma((2,)),
            dma,
            dma,
            dma,
            dma,
        ],
        compiler_params=pltpu.CompilerParams(
            collective_id=0, has_side_effects=True, vmem_limit_bytes=48 * 1024 * 1024
        ),
        name="dual_step",
    )(
        source_mass, target_density, potential,
        lanes(dest_device), lanes(dest_tile), lanes(mass_counts), reach,
    )


def solution(mesh):
    in_specs = (
        P(None, "gx", "gy"),
        P(None, "gx", "gy"),
        P(None, "gx", "gy"),
        P("gx", "gy", None, None),
        P("gx", "gy", None, None),
        P("gx", "gy", None, None),
        P(),
    )
    out_specs = (P(None, "gx", "gy"), P(None, "gx", "gy"))
    return jax.shard_map(
        per_device, mesh=mesh, in_specs=in_specs, out_specs=out_specs, check_vma=False
    )
```

```python
import jax
import jax.numpy as jnp
from jax import lax
from jax.experimental import pallas as pl
from jax.experimental.pallas import tpu as pltpu
from jax.sharding import PartitionSpec as P

MESH = pl.DeviceIdType.MESH
TS = 16
SLOTS = 6
LANES = 128
UNITS = 8
AXES = ((0, 1, 2), (1, 2, 0), (2, 0, 1))
GROUP = SLOTS * 4
BLOCK = 4 * GROUP
F32 = jnp.float32
BF16 = jnp.bfloat16


def split2(a):
    hi = a.astype(BF16)
    return hi, (a - hi.astype(F32)).astype(BF16)


def dot(a, b, dims=((1,), (0,))):
    return lax.dot_general(a, b, (dims, ((), ())), preferred_element_type=F32)


def dot3(a, b, dims=((1,), (0,))):
    ah, al = a
    bh, bl = b
    return dot(ah, bh, dims) + (dot(ah, bl, dims) + dot(al, bh, dims))


def dot_f32(a, b, dims=((1,), (0,))):
    return lax.dot_general(
        a, b, (dims, ((), ())), precision=lax.Precision.HIGHEST, preferred_element_type=F32
    )


def iota(shape, axis):
    return lax.broadcasted_iota(jnp.int32, shape, axis)


def block_transpose(vectors):
    lane_block = iota((8, LANES), 1) // TS
    vectors = list(vectors)
    for bit in (4, 2, 1):
        low = (lane_block & bit) == 0
        result = [None] * 8
        for a in range(8):
            if a & bit:
                continue
            b = a | bit
            up, down = vectors[a], vectors[b]
            result[a] = jnp.where(low, up, pltpu.roll(down, bit * TS, 1))
            result[b] = jnp.where(low, pltpu.roll(up, LANES - bit * TS, 1), down)
        vectors = result
    return vectors


def powers(logs, exponent):
    return jnp.exp(exponent.astype(F32) * logs)


def whole(ref, first, count, sem):
    part = ref.at[pl.ds(first, count)]
    pltpu.make_async_copy(part, part, sem).wait()


def kernel(
    source_ref, target_ref, potential_ref, device_ref, tile_ref, count_ref, reach_hbm,
    pushed_ref, next_ref,
    natural, target, potential, gathered, smooth, reach_ref,
    meta, metas, tiles, spread_in, picks, weights, places,
    slots_out, slots_in, labels_out, labels_in, partial_out, partial_in, own_sum,
    xtab_hi, xtab_lo, ytab_hi, ytab_lo, xmsg, xall, ymsg, yall,
    load_sem, store_sem, meta_send, meta_recv, spread_send, spread_recv,
    slot_send, slot_recv, label_send, label_recv, partial_send, partial_recv,
    x_send, x_recv, y_send, y_recv,
):
    p, q = lax.axis_index("gx"), lax.axis_index("gy")
    n_gx, n_gy = 8, 16
    planes, cx, cy = source_ref.shape
    tile_rows, tile_cols = cx // TS, cy // TS
    here = (q & 3, p >> 1, q >> 2)
    core = p & 1
    stride = (1, 2 * n_gy, 4)

    def device(moves, other):
        x, y, z = [(here[axis] + moves.get(axis, 0)) & 3 for axis in range(3)]
        return y * 2 + (core ^ other), z * 4 + x

    def remote(src, dst, send, recv, to):
        pltpu.make_async_remote_copy(
            src_ref=src, dst_ref=dst, send_sem=send, recv_sem=recv,
            device_id=to, device_id_type=MESH,
        ).start()

    loads = [
        pltpu.make_async_copy(a, b, load_sem.at[i])
        for i, (a, b) in enumerate([
            (device_ref, meta.at[0]), (tile_ref, meta.at[1]), (count_ref, meta.at[2]),
            (source_ref, natural), (target_ref, target), (potential_ref, potential),
            (reach_hbm, reach_ref),
        ])
    ]
    for load in loads:
        load.start()

    barrier = pltpu.get_barrier_semaphore()
    peers = [({axis: s}, h) for axis in range(3) for s in range(1, 4) for h in range(2)]
    peers.append(({}, 1))
    for moves, other in peers:
        pl.semaphore_signal(
            barrier, inc=1, device_id=device(moves, other), device_id_type=MESH
        )

    for load in loads[:4]:
        load.wait()
    for xo in range(tile_rows):
        parts = [
            natural[g // 2, pl.ds(xo * TS + (g % 2) * 8, 8), :] for g in range(2 * planes)
        ]
        for yo, value in enumerate(block_transpose(parts)):
            tiles[pl.ds(xo * tile_cols + yo, UNITS, stride=LANES), :] = value
    pl.semaphore_wait(barrier, len(peers))

    for g, (a, _, _) in enumerate(AXES):
        for s in range(1, 4):
            remote(meta, metas.at[g * 3 + s - 1], meta_send, meta_recv.at[g], device({a: s}, 0))
    for c in range(UNITS):
        for s in range(1, 4):
            remote(
                tiles.at[pl.ds(c * LANES, LANES)],
                spread_in.at[pl.ds((c * 3 + s - 1) * LANES, LANES)],
                spread_send, spread_recv.at[c], device({AXES[c % 3][0]: s}, 0),
            )

    earlier = (iota((LANES, LANES), 0) < iota((LANES, LANES), 1)).astype(BF16)
    row = iota((GROUP, LANES), 0)
    row_k, row_j = (row >> 2).astype(F32), row & 3

    def find_slots(g, s, info):
        a, b, e = AXES[g]
        names, spots, counts = info[0], info[1].astype(F32), info[2].astype(F32)
        shares = counts / jnp.sum(counts, axis=0, keepdims=True)
        along = ((here[e] + row_j) & 3) * stride[e]
        masks = []
        for ih in range(8):
            number = (
                here[a] * stride[a] + ((here[b] + ih // 2) & 3) * stride[b]
                + (core ^ (ih % 2)) * n_gy + along
            )
            share = jnp.zeros((GROUP, LANES), F32)
            spot = jnp.zeros((GROUP, LANES), F32)
            for f in range(4):
                match = number == names[f : f + 1, :]
                share = jnp.where(match, shares[f : f + 1, :], share)
                spot = jnp.where(match, spots[f : f + 1, :], spot)
            masks.append((share, spot))
        share = jnp.concatenate([m[0] for m in masks], axis=0)
        named = jnp.where(share > 0.0, 1.0, 0.0)
        rank = dot(named.astype(BF16), earlier)
        wanted = jnp.concatenate([row_k] * 8, axis=0)
        pick = jnp.where(rank == wanted, named, 0.0)
        picks[g * 4 + s] = pick.astype(BF16)
        weights[g * 4 + s] = jnp.broadcast_to(
            jnp.sum(pick * share, axis=1, keepdims=True), (8 * GROUP, LANES)
        )
        for ih in range(8):
            places[g, pl.ds(ih * LANES + s * GROUP, GROUP), :] = (
                pick[ih * GROUP : (ih + 1) * GROUP] * masks[ih][1]
            )

    for g, (a, b, _) in enumerate(AXES):
        whole(metas, g * 3, 3, meta_recv.at[g])
        for s in range(4):
            find_slots(g, s, meta[...] if s == 0 else metas[g * 3 + s - 1])
        for ih in range(8):
            places[g, pl.ds(ih * LANES + BLOCK, LANES - BLOCK), :] = jnp.zeros(
                (LANES - BLOCK, LANES), F32
            )
        found = dot(jnp.ones((8, LANES), BF16), places[g].astype(BF16), ((1,), (1,)))
        for ih in range(8):
            line = found[0:1, ih * LANES : (ih + 1) * LANES]
            if ih == 0:
                labels_in[g * 8] = line
            else:
                labels_out[g * 8 + ih] = line
        for ih in range(1, 8):
            remote(
                labels_out.at[g * 8 + ih], labels_in.at[g * 8 + ih],
                label_send, label_recv.at[g], device({b: ih // 2}, ih % 2),
            )

    for c in range(UNITS):
        g = c % 3
        b = AXES[g][1]
        for s in range(4):
            if s == 1:
                whole(spread_in, c * 3 * LANES, 3 * LANES, spread_recv.at[c])
            if s == 0:
                value = tiles[pl.ds(c * LANES, LANES), :]
            else:
                value = spread_in[pl.ds((c * 3 + s - 1) * LANES, LANES), :]
            pick = picks[g * 4 + s]
            value = dot(
                jnp.concatenate([pick, pick], axis=1), jnp.concatenate(split2(value), axis=0)
            )
            value = value * weights[g * 4 + s]
            for ih in range(8):
                piece = value[ih * GROUP : (ih + 1) * GROUP]
                if ih == 0:
                    slots_in[pl.ds(c * 8 * BLOCK + s * GROUP, GROUP), :] = piece
                else:
                    slots_out[pl.ds((c * 7 + ih - 1) * BLOCK + s * GROUP, GROUP), :] = piece
        for ih in range(1, 8):
            remote(
                slots_out.at[pl.ds((c * 7 + ih - 1) * BLOCK, BLOCK)],
                slots_in.at[pl.ds((c * 8 + ih) * BLOCK, BLOCK)],
                slot_send, slot_recv.at[c], device({b: ih // 2}, ih % 2),
            )

    loads[6].wait()
    decay = [jnp.full((1, 1), 1.0 - 1.0 / reach_ref[z], F32) for z in range(planes)]
    logs = [jnp.log(d) for d in decay]
    scale = [(1.0 - d) ** 2 for d in decay]

    def tables(z, n):
        at = iota((1, n), 1)
        gap = iota((n, n), 0) - iota((n, n), 1)
        lower = jnp.where(gap >= 0, powers(logs[z], jnp.maximum(gap, 0)), 0.0)
        both = scale[z] * dot_f32(lower, lower, ((0,), (0,)))
        last = powers(logs[z], n - 1 - at)
        rise = powers(logs[z], at + 1)
        fall = powers(logs[z], n - at)
        swept = scale[z] * dot_f32(jnp.broadcast_to(rise, (8, n)), lower)[0:1]
        return both, (last, swept, fall, both[0:1])

    x_edges, y_edges = [], []
    for z in range(planes):
        both, edge = tables(z, cx)
        xtab_hi[z], xtab_lo[z] = split2(both)
        x_edges.append(edge)
        both, edge = tables(z, cy)
        ytab_hi[z], ytab_lo[z] = split2(both)
        y_edges.append(edge)

    wide = 8 * SLOTS * 4
    out_lane = iota((1, wide), 1)
    sender = jnp.zeros((1, wide), jnp.int32)
    for m in range(1, 8):
        sender += (out_lane >= m * GROUP).astype(jnp.int32)
    within = out_lane - sender * GROUP
    in_lane = iota((LANES, wide), 0)
    sender_row = iota((8, wide), 0) == sender
    tile_index = iota((LANES, wide), 0).astype(F32)
    selects = []
    for g in range(3):
        whole(labels_in, g * 8 + 1, 7, label_recv.at[g])
        lines = labels_in[pl.ds(g * 8, 8)].reshape(8, LANES).astype(BF16)
        row_of = []
        for j in range(4):
            choose = ((in_lane >> 2) == within) & ((in_lane & 3) == j)
            named = dot(lines, choose.astype(BF16))
            named = jnp.sum(jnp.where(sender_row, named, 0.0), axis=0, keepdims=True)
            row_of.append((tile_index == named).astype(BF16))
        selects.append(row_of)

    for c in range(UNITS):
        g = c % 3
        whole(slots_in, (c * 8 + 1) * BLOCK, 7 * BLOCK, slot_recv.at[c])
        for j in range(4):
            rows = slots_in[pl.ds(c * 8 * BLOCK + j, wide, stride=4), :]
            value = dot(selects[g][j], jnp.concatenate(split2(rows), axis=1))
            value = value[:, :LANES] + value[:, LANES:]
            if j == 0:
                own_sum[pl.ds(c * LANES, LANES), :] = value
            else:
                at = pl.ds((c * 3 + j - 1) * LANES, LANES)
                partial_out[at, :] = value
                remote(
                    partial_out.at[at], partial_in.at[at],
                    partial_send, partial_recv.at[c], device({AXES[g][2]: j}, 0),
                )

    for c in range(UNITS):
        whole(partial_in, c * 3 * LANES, 3 * LANES, partial_recv.at[c])
        at = pl.ds(c * LANES, LANES)
        total = own_sum[at, :]
        for j in range(3):
            total += partial_in[pl.ds((c * 3 + j) * LANES, LANES), :]
        own_sum[at, :] = total
    for xo in range(tile_rows):
        parts = [
            own_sum[pl.ds(xo * tile_cols + yo, UNITS, stride=LANES), :]
            for yo in range(tile_cols)
        ]
        for g, value in enumerate(block_transpose(parts)):
            gathered[g // 2, pl.ds(xo * TS + (g % 2) * 8, 8), :] = value
    store_pushed = pltpu.make_async_copy(gathered, pushed_ref, store_sem.at[0])
    store_pushed.start()

    loads[4].wait()
    row8 = iota((8, 1), 0)
    ends = jnp.zeros((8, cy), F32)
    for z in range(planes):
        mismatch = target[z] - gathered[z]
        base = dot3((xtab_hi[z], xtab_lo[z]), split2(mismatch))
        smooth[z] = base
        ends += dot_f32(jnp.where(row8 == z, x_edges[z][0], 0.0), mismatch)
        ends += jnp.where(row8 == planes + z, base[0:1], 0.0)
    xmsg[...] = ends
    for s in range(4):
        for h in range(2):
            if s + h:
                remote(xmsg, xall.at[p], x_send, x_recv, device({1: s}, h))
    xall[p] = ends
    whole(xall, 0, n_gx - 1, x_recv)

    def boundary(all_ref, count, at, across, first_swept, width):
        low = row8 < planes
        entering = jnp.zeros((8, width), F32)
        entry, picked = [], jnp.zeros((8, width), F32)
        for i in range(count):
            entry.append(entering)
            picked = jnp.where(at == i, entering, picked)
            entering = jnp.where(low, across * entering + all_ref[i], 0.0)
        leaving = jnp.zeros((8, width), F32)
        out = jnp.zeros((8, width), F32)
        for i in reversed(range(count)):
            out = jnp.where(at == i, leaving, out)
            begun = all_ref[i] + pltpu.roll(first_swept * entry[i], planes, 0)
            leaving = jnp.where(low, 0.0, across * leaving + begun)
        return picked + out

    def column8(values):
        result = jnp.zeros((8, 1), F32)
        for z, v in enumerate(values):
            result = jnp.where((row8 == z) | (row8 == planes + z), v, result)
        return result

    across_x = column8([powers(logs[z], jnp.full((1, 1), cx, jnp.int32)) for z in range(planes)])
    across_y = column8([powers(logs[z], jnp.full((1, 1), cy, jnp.int32)) for z in range(planes)])
    swept_x = column8([x_edges[z][1][:, 0:1] for z in range(planes)])
    swept_y = column8([y_edges[z][1][:, 0:1] for z in range(planes)])

    def spread(z, edge):
        return jnp.where(row8 == z, edge[1], 0.0) + jnp.where(row8 == planes + z, edge[2], 0.0)

    inflow = boundary(xall, n_gx, p, across_x, swept_x, cy)
    ends = jnp.zeros((8, cx), F32)
    for z in range(planes):
        value = smooth[z] + dot_f32(spread(z, x_edges[z]), inflow, ((0,), (0,)))
        smooth[z] = value
        weights8 = jnp.where(row8 == z, y_edges[z][0], 0.0) + jnp.where(
            row8 == planes + z, y_edges[z][3], 0.0
        )
        ends += dot_f32(weights8, value, ((1,), (1,)))
    ymsg[...] = ends
    for dz in range(4):
        for dx in range(4):
            if dz + dx:
                remote(ymsg, yall.at[q], y_send, y_recv, device({2: dz, 0: dx}, 0))
    yall[q] = ends
    loads[5].wait()
    for z in range(planes):
        potential[z] = potential[z] + dot3(split2(smooth[z]), (ytab_hi[z], ytab_lo[z]))
    whole(yall, 0, n_gy - 1, y_recv)
    inflow = boundary(yall, n_gy, q, across_y, swept_y, cx)
    for z in range(planes):
        potential[z] = potential[z] + dot_f32(inflow, spread(z, y_edges[z]), ((0,), (0,)))
    store_next = pltpu.make_async_copy(potential, next_ref, store_sem.at[1])
    store_next.start()

    whole(metas, 0, 9, meta_send)
    whole(spread_in, 0, 3 * UNITS * LANES, spread_send)
    whole(slots_out, 0, 7 * UNITS * BLOCK, slot_send)
    whole(labels_out, 0, 21, label_send)
    whole(partial_out, 0, 3 * UNITS * LANES, partial_send)
    whole(xall, 0, n_gx - 1, x_send)
    whole(yall, 0, n_gy - 1, y_send)
    store_pushed.wait()
    store_next.wait()


def per_device(source_mass, target_density, potential, dest_device, dest_tile, mass_counts, reach):
    planes, cx, cy = source_mass.shape

    def lanes(a):
        return jnp.swapaxes(a.reshape(a.shape[2:]), 0, 1)

    hbm = pl.BlockSpec(memory_space=pl.ANY)
    dma = pltpu.SemaphoreType.DMA
    vmem = pltpu.VMEM
    grid = jax.ShapeDtypeStruct((planes, cx, cy), F32)
    field = vmem((planes, cx, cy), F32)
    return pl.pallas_call(
        kernel,
        out_shape=(grid, grid),
        in_specs=[hbm] * 7,
        out_specs=(hbm, hbm),
        scratch_shapes=[
            field, field, field, field, field,
            pltpu.SMEM((planes,), F32),
            vmem((3, 4, LANES), jnp.int32),
            vmem((9, 3, 4, LANES), jnp.int32),
            vmem((UNITS * LANES, LANES), F32),
            vmem((3 * UNITS * LANES, LANES), F32),
            vmem((12, 8 * GROUP, LANES), BF16),
            vmem((12, 8 * GROUP, LANES), F32),
            vmem((3, 8 * LANES, LANES), F32),
            vmem((7 * UNITS * BLOCK, LANES), F32),
            vmem((8 * UNITS * BLOCK, LANES), F32),
            vmem((24, 1, LANES), F32),
            vmem((24, 1, LANES), F32),
            vmem((3 * UNITS * LANES, LANES), F32),
            vmem((3 * UNITS * LANES, LANES), F32),
            vmem((UNITS * LANES, LANES), F32),
            vmem((planes, cx, cx), BF16),
            vmem((planes, cx, cx), BF16),
            vmem((planes, cy, cy), BF16),
            vmem((planes, cy, cy), BF16),
            vmem((8, cy), F32),
            vmem((8, 8, cy), F32),
            vmem((8, cx), F32),
            vmem((16, 8, cx), F32),
            dma((7,)), dma((2,)), dma, dma((3,)), dma, dma((UNITS,)),
            dma, dma((UNITS,)), dma, dma((3,)), dma, dma((UNITS,)),
            dma, dma, dma, dma,
        ],
        compiler_params=pltpu.CompilerParams(collective_id=0, has_side_effects=True),
        name="dual_step",
    )(
        source_mass, target_density, potential,
        lanes(dest_device), lanes(dest_tile), lanes(mass_counts), reach,
    )


def solution(mesh):
    in_specs = (
        P(None, "gx", "gy"),
        P(None, "gx", "gy"),
        P(None, "gx", "gy"),
        P("gx", "gy", None, None),
        P("gx", "gy", None, None),
        P("gx", "gy", None, None),
        P(),
    )
    out_specs = (P(None, "gx", "gy"), P(None, "gx", "gy"))
    return jax.shard_map(
        per_device, mesh=mesh, in_specs=in_specs, out_specs=out_specs, check_vma=False
    )
```

```python
import jax
import jax.numpy as jnp
from jax import lax
from jax.experimental import pallas as pl
from jax.experimental.pallas import tpu as pltpu
from jax.sharding import PartitionSpec as P

MESH = pl.DeviceIdType.MESH
TS = 16
SLOTS = 6
LANES = 128
UNITS = 8
AXES = ((0, 1, 2), (1, 2, 0), (2, 0, 1))
GROUP = SLOTS * 4
BLOCK = 4 * GROUP
PITCH = 9
F32 = jnp.float32
BF16 = jnp.bfloat16


def split2(a):
    hi = a.astype(BF16)
    return hi, (a - hi.astype(F32)).astype(BF16)


def dot(a, b, dims=((1,), (0,))):
    return lax.dot_general(a, b, (dims, ((), ())), preferred_element_type=F32)


def dot3(a, b, dims=((1,), (0,))):
    ah, al = a
    bh, bl = b
    return dot(ah, bh, dims) + (dot(ah, bl, dims) + dot(al, bh, dims))


def dot_f32(a, b, dims=((1,), (0,))):
    return lax.dot_general(
        a, b, (dims, ((), ())), precision=lax.Precision.HIGHEST, preferred_element_type=F32
    )


def iota(shape, axis):
    return lax.broadcasted_iota(jnp.int32, shape, axis)


def block_transpose(vectors):
    lane_block = iota((8, LANES), 1) // TS
    vectors = list(vectors)
    for bit in (4, 2, 1):
        low = (lane_block & bit) == 0
        result = [None] * 8
        for a in range(8):
            if a & bit:
                continue
            b = a | bit
            up, down = vectors[a], vectors[b]
            result[a] = jnp.where(low, up, pltpu.roll(down, bit * TS, 1))
            result[b] = jnp.where(low, pltpu.roll(up, LANES - bit * TS, 1), down)
        vectors = result
    return vectors


def powers(logs, exponent):
    return jnp.exp(exponent.astype(F32) * logs)


def whole(ref, first, count, sem):
    part = ref.at[pl.ds(first, count)]
    pltpu.make_async_copy(part, part, sem).wait()


def kernel(
    source_ref, target_ref, potential_ref, device_ref, tile_ref, count_ref, reach_hbm,
    pushed_ref, next_ref,
    natural, target, potential, smooth, reach_ref,
    meta, metas, tiles, regroup, spread_in, picks, weights, places,
    slots_out, slots_in, labels_out, labels_in,
    far_out, far_in, partial_out, partial_in, own_sum,
    xtab_hi, xtab_lo, ytab_hi, ytab_lo, xends_tab, yends_tab, xfill, yfill_tab,
    coef, edge_rows, halves, xmsg, xall, ymsg, yall,
    load_sem, meta_send, meta_recv, spread_send, spread_recv, relay_recv,
    slot_send, slot_recv, label_send, label_recv, far_send, far_recv,
    partial_send, partial_recv, x_send, x_recv, y_send, y_recv,
):
    p, q = lax.axis_index("gx"), lax.axis_index("gy")
    n_gx, n_gy = 8, 16
    planes, cx, cy = source_ref.shape
    tile_rows, tile_cols = cx // TS, cy // TS
    half = LANES // 2
    here = (q & 3, p >> 1, q >> 2)
    core = p & 1
    stride = (1, 2 * n_gy, 4)

    def device(moves, other):
        x, y, z = [(here[axis] + moves.get(axis, 0)) & 3 for axis in range(3)]
        return y * 2 + (core ^ other), z * 4 + x

    def remote(src, dst, send, recv, to):
        pltpu.make_async_remote_copy(
            src_ref=src, dst_ref=dst, send_sem=send, recv_sem=recv,
            device_id=to, device_id_type=MESH,
        ).start()

    loads = [
        pltpu.make_async_copy(a, b, load_sem.at[i])
        for i, (a, b) in enumerate([
            (device_ref, meta.at[0]), (tile_ref, meta.at[1]), (count_ref, meta.at[2]),
            (source_ref, natural), (target_ref, target), (potential_ref, potential),
            (reach_hbm, reach_ref),
        ])
    ]
    for load in loads:
        load.start()

    barrier = pltpu.get_barrier_semaphore()
    peers = [({axis: s}, h) for axis in range(3) for s in range(1, 4) for h in range(2)]
    peers.append(({}, 1))
    for moves, other in peers:
        pl.semaphore_signal(
            barrier, inc=1, device_id=device(moves, other), device_id_type=MESH
        )

    for load in loads[:4]:
        load.wait()
    for xo in range(tile_rows):
        parts = [
            natural[g // 2, pl.ds(xo * TS + (g % 2) * 8, 8), :] for g in range(2 * planes)
        ]
        for yo, value in enumerate(block_transpose(parts)):
            regroup[pl.ds((xo * tile_cols + yo) * PITCH, UNITS), :] = value
    for c in range(UNITS):
        tiles[pl.ds(c * LANES, LANES), :] = regroup[pl.ds(c, LANES, stride=PITCH), :]
    pl.semaphore_wait(barrier, len(peers))

    def spread_row(c, s):
        return (c * 3 + s) * LANES

    for g, (a, _, _) in enumerate(AXES):
        for s in range(1, 4):
            remote(meta, metas.at[g * 3 + s - 1], meta_send, meta_recv.at[g], device({a: s}, 0))
    for c in range(UNITS):
        for s, move in enumerate((1, 3)):
            remote(
                tiles.at[pl.ds(c * LANES, LANES)],
                spread_in.at[pl.ds(spread_row(c, s), LANES)],
                spread_send, spread_recv.at[c], device({AXES[c % 3][0]: move}, 0),
            )

    def relay_tiles(c):
        whole(spread_in, spread_row(c, 0), 2 * LANES, spread_recv.at[c])
        for s, move in enumerate((1, 3)):
            remote(
                spread_in.at[pl.ds(spread_row(c, s) + s * half, half)],
                spread_in.at[pl.ds(spread_row(c, 2) + s * half, half)],
                spread_send, relay_recv.at[c], device({AXES[c % 3][0]: move}, 0),
            )

    earlier = (iota((LANES, LANES), 0) < iota((LANES, LANES), 1)).astype(BF16)
    row = iota((32, LANES), 0)
    row_target, row_j = row >> 2, row & 3
    order = iota((8, LANES), 0).astype(F32)

    def find_slots(g, s, info):
        a, b, e = AXES[g]
        names, spots, counts = info[0], info[1].astype(F32), info[2].astype(F32)
        shares = counts / jnp.sum(counts, axis=0, keepdims=True)
        number = (
            here[a] * stride[a] + ((here[b] + (row_target >> 1)) & 3) * stride[b]
            + (core ^ (row_target & 1)) * n_gy + ((here[e] + row_j) & 3) * stride[e]
        )
        share = jnp.zeros((32, LANES), F32)
        spot = jnp.zeros((32, LANES), F32)
        for f in range(4):
            match = number == names[f : f + 1, :]
            share = jnp.where(match, shares[f : f + 1, :], share)
            spot = jnp.where(match, spots[f : f + 1, :], spot)
        named = share > 0.0
        rank = dot(jnp.where(named, 1.0, 0.0).astype(BF16), earlier)
        rank = jnp.where(named, rank, -1.0)
        found = []
        for r in range(32):
            mine = rank[r : r + 1, :] == order
            found.append(jnp.where(mine, 1.0, 0.0))
            part = jnp.where(mine, share[r : r + 1, :], 0.0)
            weights[g * 4 + s, pl.ds(r * 8, 8), :] = jnp.broadcast_to(
                jnp.sum(part, axis=1, keepdims=True), (8, LANES)
            )
            places[g, pl.ds((r // 4) * LANES + (r % 4) * GROUP + s * SLOTS, SLOTS), :] = (
                jnp.where(mine, spot[r : r + 1, :], 0.0)[:SLOTS]
            )
        picks[g * 4 + s] = jnp.concatenate(found, axis=0).astype(BF16)

    source_meta = (None, 0, 2, 1)

    def find_labels(g):
        b = AXES[g][1]
        for ih in range(8):
            places[g, pl.ds(ih * LANES + BLOCK, LANES - BLOCK), :] = jnp.zeros(
                (LANES - BLOCK, LANES), F32
            )
        found = dot(jnp.ones((8, LANES), BF16), places[g].astype(BF16), ((1,), (1,)))
        for ih in range(8):
            line = found[0:1, ih * LANES : (ih + 1) * LANES]
            if ih == 0:
                labels_in[g * 8] = line
            else:
                labels_out[g * 8 + ih - 1] = line
        for ih in range(1, 8):
            remote(
                labels_out.at[g * 8 + ih - 1], labels_in.at[g * 8 + ih],
                label_send, label_recv.at[g], device({b: ih // 2}, ih % 2),
            )

    for g in range(3):
        find_slots(g, 0, meta[...])
    for g in range(3):
        whole(metas, g * 3, 3, meta_recv.at[g])
        for s in range(1, 4):
            find_slots(g, s, metas[g * 3 + source_meta[s]])
        for c in range(g, UNITS, 3)[:1]:
            relay_tiles(c)
    for g in range(3):
        find_labels(g)
    for c in range(3, UNITS):
        relay_tiles(c)

    def pack(c):
        g = c % 3
        b = AXES[g][1]
        for s in range(4):
            if s == 3:
                whole(spread_in, spread_row(c, 2), LANES, relay_recv.at[c])
            if s == 0:
                value = tiles[pl.ds(c * LANES, LANES), :]
            else:
                value = spread_in[pl.ds(spread_row(c, s - 1), LANES), :]
            pick = picks[g * 4 + s]
            value = dot(
                jnp.concatenate([pick, pick], axis=1), jnp.concatenate(split2(value), axis=0)
            )
            value = value * weights[g * 4 + s]
            for r in range(32):
                ih, j = r // 4, r % 4
                piece = value[r * 8 : r * 8 + SLOTS]
                within = j * GROUP + s * SLOTS
                if ih == 0:
                    slots_in[pl.ds(c * 8 * BLOCK + within, SLOTS), :] = piece
                else:
                    slots_out[pl.ds((c * 7 + ih - 1) * BLOCK + within, SLOTS), :] = piece
        for ih in range(1, 8):
            remote(
                slots_out.at[pl.ds((c * 7 + ih - 1) * BLOCK, BLOCK)],
                slots_in.at[pl.ds((c * 8 + ih) * BLOCK, BLOCK)],
                slot_send, slot_recv.at[c], device({b: ih // 2}, ih % 2),
            )

    for c in range(UNITS):
        pack(c)

    loads[6].wait()
    decay = [jnp.full((1, 1), 1.0 - 1.0 / reach_ref[z], F32) for z in range(planes)]
    logs = [jnp.log(d) for d in decay]
    scale = [(1.0 - d) ** 2 for d in decay]
    row8 = iota((8, 1), 0)

    def both_rows(values):
        result = jnp.zeros((8, values[0].shape[1]), F32)
        for z, v in enumerate(values):
            result = jnp.where((row8 == z) | (row8 == planes + z), v, result)
        return result

    def stacked(a):
        hi = a.astype(BF16).astype(F32)
        return jnp.concatenate([hi, a - hi], axis=0).astype(BF16)

    swept_first, last_rows, first_rows = {}, {}, {}
    for axis, n in (("x", cx), ("y", cy)):
        at = iota((1, n), 1)
        gap = iota((n, n), 0) - iota((n, n), 1)
        lasts, firsts, swepts, falls = [], [], [], []
        for z in range(planes):
            lower = jnp.where(gap >= 0, powers(logs[z], jnp.maximum(gap, 0)), 0.0)
            both = scale[z] * dot_f32(lower, lower, ((0,), (0,)))
            last = powers(logs[z], n - 1 - at)
            rise = powers(logs[z], at + 1)
            fall = powers(logs[z], n - at)
            swept = scale[z] * dot_f32(jnp.broadcast_to(rise, (8, n)), lower)[0:1]
            lasts.append(last)
            firsts.append(both[0:1])
            swepts.append(swept)
            falls.append(fall)
            ends = jnp.where(row8 == z, last, 0.0) + jnp.where(
                row8 == planes + z, both[0:1], 0.0
            )
            if axis == "x":
                xtab_hi[z], xtab_lo[z] = split2(both)
                xends_tab[z] = stacked(ends)
                down = iota((n, LANES), 0)
                xfill[z] = scale[z] * dot_f32(lower, powers(logs[z], down + 1), ((0,), (0,)))
                xfill[planes + z] = powers(logs[z], n - down)
            else:
                ytab_hi[z], ytab_lo[z] = split2(both)
                yends_tab[z] = stacked(ends)
                fill = jnp.where(row8 == z, swept, 0.0) + jnp.where(
                    row8 == planes + z, fall, 0.0
                )
                hi = fill.astype(BF16).astype(F32)
                yfill_tab[z] = jnp.concatenate([hi, hi, fill - hi, fill - hi], axis=0).astype(
                    BF16
                )
        swept_first[axis] = both_rows([v[:, 0:1] for v in swepts])
        if axis == "x":
            edge_rows[0] = both_rows(swepts)
            edge_rows[1] = both_rows(falls)
        else:
            last_rows, first_rows = both_rows(lasts), both_rows(firsts)

    def coefficients(base, count, at, n, first):
        across = both_rows([powers(logs[z], jnp.full((1, 1), n, jnp.int32)) for z in range(planes)])
        powers_of = [jnp.ones((8, 1), F32)]
        for _ in range(count - 1):
            powers_of.append(powers_of[-1] * across)
        low = row8 < planes
        before, after = [], []
        for i in range(count):
            coming = jnp.zeros((8, 1), F32)
            going = jnp.zeros((8, 1), F32)
            for m in range(count - 1):
                coming = jnp.where(at - 1 - i == m, powers_of[m], coming)
                going = jnp.where(i - at - 1 == m, powers_of[m], going)
            before.append(coming)
            after.append(going)
        through = jnp.zeros((8, 1), F32)
        crossing = [None] * count
        for i in reversed(range(count)):
            crossing[i] = first * through
            through = after[i] + across * through
        for i in range(count):
            coef[base + i] = jnp.broadcast_to(jnp.where(low, before[i], after[i]), (8, LANES))
            coef[base + count + i] = jnp.broadcast_to(
                jnp.where(low, crossing[i], 0.0), (8, LANES)
            )

    coefficients(0, n_gx, p, cx, swept_first["x"])
    coefficients(2 * n_gx, n_gy, q, cy, swept_first["y"])

    def inflow(base, count, all_ref, width):
        columns = []
        for w in range(width // LANES):
            direct, through = [], []
            for i in range(count):
                value = all_ref[i, :, pl.ds(w * LANES, LANES)]
                direct.append(coef[base + i] * value)
                through.append(coef[base + count + i] * value)
            while len(direct) > 1:
                direct = [a + b for a, b in zip(direct[::2], direct[1::2])]
                through = [a + b for a, b in zip(through[::2], through[1::2])]
            columns.append(direct[0] + pltpu.roll(through[0], planes, 0))
        return columns[0] if len(columns) == 1 else jnp.concatenate(columns, axis=1)

    wide = 8 * GROUP
    out_lane = iota((1, wide), 1)
    sender = jnp.zeros((1, wide), jnp.int32)
    for m in range(1, 8):
        sender += (out_lane >= m * GROUP).astype(jnp.int32)
    within = out_lane - sender * GROUP
    in_lane = iota((LANES, wide), 0)
    sender_row = iota((8, wide), 0) == sender
    tile_index = iota((LANES, wide), 0).astype(F32)
    selects = []
    for g in range(3):
        whole(labels_in, g * 8 + 1, 7, label_recv.at[g])
        lines = labels_in[pl.ds(g * 8, 8)].reshape(8, LANES).astype(BF16)
        row_of = []
        for j in range(4):
            choose = in_lane == within + j * GROUP
            named = dot(lines, choose.astype(BF16))
            named = jnp.sum(jnp.where(sender_row, named, 0.0), axis=0, keepdims=True)
            row_of.append((tile_index == named).astype(BF16))
        selects.append(row_of)

    def partial_row(c, s):
        return (c * 2 + s) * LANES

    def unpack(c):
        g = c % 3
        e = AXES[g][2]
        whole(slots_in, (c * 8 + 1) * BLOCK, 7 * BLOCK, slot_recv.at[c])
        for j in (2, 1, 3, 0):
            rows = jnp.concatenate(
                [
                    slots_in[pl.ds((c * 8 + ih) * BLOCK + j * GROUP, GROUP), :]
                    for ih in range(8)
                ],
                axis=0,
            )
            value = dot(selects[g][j], jnp.concatenate(split2(rows), axis=1))
            value = value[:, :LANES] + value[:, LANES:]
            if j == 0:
                own_sum[pl.ds(c * LANES, LANES), :] = value
            elif j == 2:
                far_out[pl.ds(c * LANES, LANES), :] = value
                for s, move in enumerate((1, 3)):
                    remote(
                        far_out.at[pl.ds(c * LANES + s * half, half)],
                        far_in.at[pl.ds(c * LANES + s * half, half)],
                        far_send, far_recv.at[c], device({e: move}, 0),
                    )
            else:
                s, move = (0, 1) if j == 1 else (1, 3)
                partial_out[pl.ds(partial_row(c, s), LANES), :] = value
                at = pl.ds(partial_row(c, s) + (1 - s) * half, half)
                remote(
                    partial_out.at[at], partial_in.at[at],
                    partial_send, partial_recv.at[c], device({e: move}, 0),
                )

    def relay_partials(c):
        whole(far_in, c * LANES, LANES, far_recv.at[c])
        for s, move in enumerate((1, 3)):
            at = pl.ds(partial_row(c, s) + s * half, half)
            partial_out[at, :] = partial_out[at, :] + far_in[pl.ds(c * LANES + s * half, half), :]
            remote(
                partial_out.at[at], partial_in.at[at],
                partial_send, partial_recv.at[c], device({AXES[c % 3][2]: move}, 0),
            )

    for c in range(UNITS):
        unpack(c)
        if c >= 3:
            relay_partials(c - 3)
    for c in range(UNITS - 3, UNITS):
        relay_partials(c)
    for c in range(UNITS):
        whole(partial_in, partial_row(c, 0), 2 * LANES, partial_recv.at[c])
        regroup[pl.ds(c, LANES, stride=PITCH), :] = (
            own_sum[pl.ds(c * LANES, LANES), :]
            + partial_in[pl.ds(partial_row(c, 0), LANES), :]
            + partial_in[pl.ds(partial_row(c, 1), LANES), :]
        )
    loads[4].wait()
    for xo in range(tile_rows):
        parts = [
            regroup[pl.ds((xo * tile_cols + yo) * PITCH, UNITS), :] for yo in range(tile_cols)
        ]
        for g, value in enumerate(block_transpose(parts)):
            pushed_ref[g // 2, pl.ds(xo * TS + (g % 2) * 8, 8), :] = value

    ends = jnp.zeros((8, cy), F32)
    for z in range(planes):
        both = jnp.concatenate(split2(target[z] - pushed_ref[z]), axis=1)
        halves[z] = both
        value = dot(xends_tab[z], both)
        ends += value[:8, :cy] + (value[:8, cy:] + value[8:, :cy])
    xmsg[...] = ends
    for s in range(4):
        for h in range(2):
            if s + h:
                remote(xmsg, xall.at[p], x_send, x_recv, device({1: s}, h))
    xall[p] = ends
    y_ends = jnp.zeros((8, cx), F32)
    for z in range(planes):
        both = halves[z]
        value = dot(xtab_hi[z], both)
        value = value[:, :cy] + (value[:, cy:] + dot(xtab_lo[z], both[:, :cy]))
        smooth[z] = value
        value = dot(yends_tab[z], jnp.concatenate(split2(value), axis=0), ((1,), (1,)))
        y_ends += value[:8, :cx] + (value[:8, cx:] + value[8:, :cx])
    whole(xall, 0, n_gx - 1, x_recv)
    flow = inflow(0, n_gx, xall, cy)
    at_last = jnp.sum(flow * last_rows, axis=1, keepdims=True)
    at_first = jnp.sum(flow * first_rows, axis=1, keepdims=True)
    upper = row8 < planes
    entered = jnp.where(upper, at_last, pltpu.roll(jnp.broadcast_to(at_first, (8, LANES)), 4, 0)[:, 0:1])
    left = jnp.where(upper, pltpu.roll(jnp.broadcast_to(at_last, (8, LANES)), 4, 0)[:, 0:1], at_first)
    y_ends += edge_rows[0] * entered + edge_rows[1] * left
    ymsg[...] = y_ends
    for dz in range(4):
        for dx in range(4):
            if dz + dx:
                remote(ymsg, yall.at[q], y_send, y_recv, device({2: dz, 0: dx}, 0))
    yall[q] = y_ends

    loads[5].wait()
    for z in range(planes):
        value = smooth[z] + (
            xfill[z] * flow[z : z + 1] + xfill[planes + z] * flow[planes + z : planes + z + 1]
        )
        potential[z] = potential[z] + dot3(split2(value), (ytab_hi[z], ytab_lo[z]))
    whole(yall, 0, n_gy - 1, y_recv)
    flow = inflow(2 * n_gx, n_gy, yall, cx)
    hi = flow.astype(BF16).astype(F32)
    flow = jnp.concatenate([hi, flow - hi, hi, flow - hi], axis=0).astype(BF16)
    for z in range(planes):
        next_ref[z] = potential[z] + dot(flow, yfill_tab[z], ((0,), (0,)))

    whole(metas, 0, 9, meta_send)
    whole(spread_in, 0, 3 * UNITS * LANES, spread_send)
    whole(slots_out, 0, 7 * UNITS * BLOCK, slot_send)
    whole(labels_out, 0, 21, label_send)
    whole(far_out, 0, UNITS * LANES, far_send)
    whole(partial_out, 0, 2 * UNITS * LANES, partial_send)
    whole(xall, 0, n_gx - 1, x_send)
    whole(yall, 0, n_gy - 1, y_send)


def per_device(source_mass, target_density, potential, dest_device, dest_tile, mass_counts, reach):
    planes, cx, cy = source_mass.shape

    def lanes(a):
        return jnp.swapaxes(a.reshape(a.shape[2:]), 0, 1)

    hbm = pl.BlockSpec(memory_space=pl.ANY)
    dma = pltpu.SemaphoreType.DMA
    vmem = pltpu.VMEM
    grid = jax.ShapeDtypeStruct((planes, cx, cy), F32)
    field = vmem((planes, cx, cy), F32)

    def rows(count):
        return vmem((count, LANES), F32)

    return pl.pallas_call(
        kernel,
        out_shape=(grid, grid),
        in_specs=[hbm] * 7,
        out_specs=(pl.BlockSpec(memory_space=vmem), pl.BlockSpec(memory_space=vmem)),
        scratch_shapes=[
            field, field, field, field,
            pltpu.SMEM((planes,), F32),
            vmem((3, 4, LANES), jnp.int32),
            vmem((9, 3, 4, LANES), jnp.int32),
            rows(UNITS * LANES), rows(LANES * PITCH + 16), rows(3 * UNITS * LANES),
            vmem((12, 256, LANES), BF16),
            vmem((12, 256, LANES), F32),
            vmem((3, 8 * LANES, LANES), F32),
            rows(7 * UNITS * BLOCK + 8), rows(8 * UNITS * BLOCK + 8),
            vmem((24, 1, LANES), F32),
            vmem((24, 1, LANES), F32),
            rows(UNITS * LANES), rows(UNITS * LANES),
            rows(2 * UNITS * LANES), rows(2 * UNITS * LANES), rows(UNITS * LANES),
            vmem((planes, cx, cx), BF16),
            vmem((planes, cx, cx), BF16),
            vmem((planes, cy, cy), BF16),
            vmem((planes, cy, cy), BF16),
            vmem((planes, 16, cx), BF16),
            vmem((planes, 16, cy), BF16),
            vmem((2 * planes, cx, LANES), F32),
            vmem((planes, 32, cy), BF16),
            vmem((48, 8, LANES), F32),
            vmem((2, 8, cx), F32),
            vmem((planes, cx, 2 * cy), BF16),
            vmem((8, cy), F32),
            vmem((8, 8, cy), F32),
            vmem((8, cx), F32),
            vmem((16, 8, cx), F32),
            dma((7,)), dma, dma((3,)), dma, dma((UNITS,)), dma((UNITS,)),
            dma, dma((UNITS,)), dma, dma((3,)), dma, dma((UNITS,)),
            dma, dma((UNITS,)), dma, dma, dma, dma,
        ],
        compiler_params=pltpu.CompilerParams(collective_id=0, has_side_effects=True),
        name="dual_step",
    )(
        source_mass, target_density, potential,
        lanes(dest_device), lanes(dest_tile), lanes(mass_counts), reach,
    )


def solution(mesh):
    in_specs = (
        P(None, "gx", "gy"),
        P(None, "gx", "gy"),
        P(None, "gx", "gy"),
        P("gx", "gy", None, None),
        P("gx", "gy", None, None),
        P("gx", "gy", None, None),
        P(),
    )
    out_specs = (P(None, "gx", "gy"), P(None, "gx", "gy"))
    return jax.shard_map(
        per_device, mesh=mesh, in_specs=in_specs, out_specs=out_specs, check_vma=False
    )
```

```python
import jax
import jax.numpy as jnp
from jax import lax
from jax.experimental import pallas as pl
from jax.experimental.pallas import tpu as pltpu
from jax.sharding import PartitionSpec as P

MESH = pl.DeviceIdType.MESH
TS = 16
SLOTS = 6
LANES = 128
UNITS = 8
AXES = ((0, 1, 2), (1, 2, 0), (2, 0, 1))
GROUP = SLOTS * 4
BLOCK = 4 * GROUP
PITCH = 9
F32 = jnp.float32
BF16 = jnp.bfloat16


def split2(a):
    hi = a.astype(BF16)
    return hi, (a - hi.astype(F32)).astype(BF16)


def dot(a, b, dims=((1,), (0,))):
    return lax.dot_general(a, b, (dims, ((), ())), preferred_element_type=F32)


def dot3(a, b, dims=((1,), (0,))):
    ah, al = a
    bh, bl = b
    return dot(ah, bh, dims) + (dot(ah, bl, dims) + dot(al, bh, dims))


def dot_f32(a, b, dims=((1,), (0,))):
    return lax.dot_general(
        a, b, (dims, ((), ())), precision=lax.Precision.HIGHEST, preferred_element_type=F32
    )


def iota(shape, axis):
    return lax.broadcasted_iota(jnp.int32, shape, axis)


def block_transpose(vectors):
    lane_block = iota((8, LANES), 1) // TS
    vectors = list(vectors)
    for bit in (4, 2, 1):
        low = (lane_block & bit) == 0
        result = [None] * 8
        for a in range(8):
            if a & bit:
                continue
            b = a | bit
            up, down = vectors[a], vectors[b]
            result[a] = jnp.where(low, up, pltpu.roll(down, bit * TS, 1))
            result[b] = jnp.where(low, pltpu.roll(up, LANES - bit * TS, 1), down)
        vectors = result
    return vectors


def powers(logs, exponent):
    return jnp.exp(exponent.astype(F32) * logs)


def whole(ref, first, count, sem):
    part = ref.at[pl.ds(first, count)]
    pltpu.make_async_copy(part, part, sem).wait()


def kernel(
    source_ref, target_ref, potential_ref, device_ref, tile_ref, count_ref, reach_hbm,
    pushed_ref, next_ref,
    natural, target, potential, smooth, reach_ref,
    meta, metas, tiles, regroup, spread_in, picks, weights, places,
    slots_out, slots_in, labels_out, labels_in,
    partial_out, partial_in, own_sum,
    xtab_hi, xtab_lo, ytab_hi, ytab_lo, xends_tab, yends_tab, xfill, yfill_tab,
    coef, edge_rows, halves, xmsg, xall, ymsg, yall,
    load_sem, meta_send, meta_recv, spread_send, spread_recv,
    slot_send, slot_recv, label_send, label_recv,
    partial_send, partial_recv, x_send, x_recv, y_send, y_recv,
):
    p, q = lax.axis_index("gx"), lax.axis_index("gy")
    n_gx, n_gy = 8, 16
    planes, cx, cy = source_ref.shape
    tile_rows, tile_cols = cx // TS, cy // TS
    here = (q & 3, p >> 1, q >> 2)
    core = p & 1
    stride = (1, 2 * n_gy, 4)

    def device(moves, other):
        x, y, z = [(here[axis] + moves.get(axis, 0)) & 3 for axis in range(3)]
        return y * 2 + (core ^ other), z * 4 + x

    def remote(src, dst, send, recv, to):
        pltpu.make_async_remote_copy(
            src_ref=src, dst_ref=dst, send_sem=send, recv_sem=recv,
            device_id=to, device_id_type=MESH,
        ).start()

    loads = [
        pltpu.make_async_copy(a, b, load_sem.at[i])
        for i, (a, b) in enumerate([
            (device_ref, meta.at[0]), (tile_ref, meta.at[1]), (count_ref, meta.at[2]),
            (source_ref, natural), (target_ref, target), (potential_ref, potential),
            (reach_hbm, reach_ref),
        ])
    ]
    for load in loads:
        load.start()

    barrier = pltpu.get_barrier_semaphore()
    peers = [({axis: s}, h) for axis in range(3) for s in range(1, 4) for h in range(2)]
    peers.append(({}, 1))
    for moves, other in peers:
        pl.semaphore_signal(
            barrier, inc=1, device_id=device(moves, other), device_id_type=MESH
        )

    for load in loads[:4]:
        load.wait()
    for xo in range(tile_rows):
        parts = [
            natural[g // 2, pl.ds(xo * TS + (g % 2) * 8, 8), :] for g in range(2 * planes)
        ]
        for yo, value in enumerate(block_transpose(parts)):
            regroup[pl.ds((xo * tile_cols + yo) * PITCH, UNITS), :] = value
    for c in range(UNITS):
        tiles[pl.ds(c * LANES, LANES), :] = regroup[pl.ds(c, LANES, stride=PITCH), :]
    pl.semaphore_wait(barrier, len(peers))

    for g, (a, _, _) in enumerate(AXES):
        for s in range(1, 4):
            remote(meta, metas.at[g * 3 + s - 1], meta_send, meta_recv.at[g], device({a: s}, 0))
    for c in range(UNITS):
        for s in range(1, 4):
            remote(
                tiles.at[pl.ds(c * LANES, LANES)],
                spread_in.at[pl.ds((c * 3 + s - 1) * LANES, LANES)],
                spread_send, spread_recv.at[c], device({AXES[c % 3][0]: s}, 0),
            )

    loads[6].wait()
    decay = [jnp.full((1, 1), 1.0 - 1.0 / reach_ref[z], F32) for z in range(planes)]
    logs = [jnp.log(d) for d in decay]
    scale = [(1.0 - d) ** 2 for d in decay]
    row8 = iota((8, 1), 0)

    def both_rows(values):
        result = jnp.zeros((8, values[0].shape[1]), F32)
        for z, v in enumerate(values):
            result = jnp.where((row8 == z) | (row8 == planes + z), v, result)
        return result

    def stacked(a):
        hi = a.astype(BF16).astype(F32)
        return jnp.concatenate([hi, a - hi], axis=0).astype(BF16)

    logs8, scale8 = both_rows(logs), both_rows(scale)

    def rows_of(n):
        at = iota((8, n), 1)
        squares = powers(2.0 * logs8, at)
        hi = squares.astype(BF16).astype(F32)
        mid = (squares - hi).astype(BF16).astype(F32)
        parts = jnp.concatenate([hi, mid, squares - hi - mid, jnp.zeros_like(hi)], axis=0)
        inside = (iota((n, n), 0) + iota((n, n), 1) < n).astype(BF16)
        sums = dot(parts.astype(BF16), inside)
        sums = sums[0:8] + (sums[8:16] + sums[16:24])
        last = powers(logs8, n - 1 - at)
        fall = powers(logs8, n - at)
        first = scale8 * powers(logs8, at) * sums
        swept = scale8 * powers(logs8, at + 1) * sums
        return sums, last, first, swept, fall

    upper = row8 < planes
    sums_x, last_x, first_x, swept_x, fall_x = rows_of(cx)
    sums_y, last_rows, first_rows, swept_y, fall_y = rows_of(cy)
    edge_rows[0], edge_rows[1] = swept_x, fall_x
    spare = jnp.zeros((cy - 24, cx), F32)
    columns = jnp.transpose(
        jnp.concatenate(
            [sums_x, jnp.where(upper, swept_x, fall_x),
             jnp.concatenate([sums_y, sums_y], axis=1), spare],
            axis=0,
        )
    )
    across_row = iota((cy, cy), 0)
    gap = across_row - iota((cy, cy), 1)
    for z in range(planes):
        near = powers(logs[z], jnp.abs(gap)) * scale[z]
        below = powers(logs[z], gap + cy) * scale[z]
        above = powers(logs[z], cy - gap) * scale[z]

        def column(i, first, count):
            return jnp.broadcast_to(columns[first : first + count, i : i + 1], (count, cy))

        low = gap >= 0
        g0, g1, gy = column(z, 0, cy), column(z, cy, cy), column(16 + z, 0, cy)
        r0, r1, ry = sums_x[z : z + 1, :cy], sums_x[z : z + 1, cy:], sums_y[z : z + 1]
        for r, (left_part, right_part) in enumerate([
            (near * jnp.where(low, g0, r0), above * r1),
            (below * g1, near * jnp.where(low, g1, r1)),
        ]):
            at = pl.ds(r * cy, cy)
            for w, part in enumerate((left_part, right_part)):
                hi, lo = split2(part)
                xtab_hi[z, at, pl.ds(w * cy, cy)] = hi
                xtab_lo[z, at, pl.ds(w * cy, cy)] = lo
        ytab_hi[z], ytab_lo[z] = split2(near * jnp.where(low, gy, ry))
        xfill[z] = jnp.broadcast_to(columns[:, 8 + z : 9 + z], (cx, LANES))
        xfill[planes + z] = jnp.broadcast_to(
            columns[:, 8 + planes + z : 9 + planes + z], (cx, LANES)
        )
        one, two = row8 == z, row8 == planes + z
        xends_tab[z] = stacked(jnp.where(one, last_x, 0.0) + jnp.where(two, first_x, 0.0))
        yends_tab[z] = stacked(jnp.where(one, last_rows, 0.0) + jnp.where(two, first_rows, 0.0))
        fill = jnp.where(one, swept_y, 0.0) + jnp.where(two, fall_y, 0.0)
        hi = fill.astype(BF16).astype(F32)
        yfill_tab[z] = jnp.concatenate([hi, hi, fill - hi, fill - hi], axis=0).astype(BF16)

    def coefficients(base, count, at, n, first):
        across = jnp.exp(float(n) * logs8)
        powers_of = [jnp.ones((8, 1), F32)]
        for _ in range(count - 1):
            powers_of.append(powers_of[-1] * across)
        low = row8 < planes
        before, after = [], []
        for i in range(count):
            coming = jnp.zeros((8, 1), F32)
            going = jnp.zeros((8, 1), F32)
            for m in range(count - 1):
                coming = jnp.where(at - 1 - i == m, powers_of[m], coming)
                going = jnp.where(i - at - 1 == m, powers_of[m], going)
            before.append(coming)
            after.append(going)
        through = jnp.zeros((8, 1), F32)
        crossing = [None] * count
        for i in reversed(range(count)):
            crossing[i] = first * through
            through = after[i] + across * through
        for i in range(count):
            coef[base + i] = jnp.broadcast_to(jnp.where(low, before[i], after[i]), (8, LANES))
            coef[base + count + i] = jnp.broadcast_to(
                jnp.where(low, crossing[i], 0.0), (8, LANES)
            )

    coefficients(0, n_gx, p, cx, swept_x[:, 0:1])
    coefficients(2 * n_gx, n_gy, q, cy, swept_y[:, 0:1])

    earlier = (iota((LANES, LANES), 0) < iota((LANES, LANES), 1)).astype(BF16)
    row = iota((32, LANES), 0)
    row_target, row_j = row >> 2, row & 3
    order = iota((8, LANES), 0).astype(F32)

    def find_slots(g, s, info):
        a, b, e = AXES[g]
        names, spots, counts = info[0], info[1].astype(F32), info[2].astype(F32)
        shares = counts / jnp.sum(counts, axis=0, keepdims=True)
        number = (
            here[a] * stride[a] + ((here[b] + (row_target >> 1)) & 3) * stride[b]
            + (core ^ (row_target & 1)) * n_gy + ((here[e] + row_j) & 3) * stride[e]
        )
        share = jnp.zeros((32, LANES), F32)
        spot = jnp.zeros((32, LANES), F32)
        for f in range(4):
            match = number == names[f : f + 1, :]
            share = jnp.where(match, shares[f : f + 1, :], share)
            spot = jnp.where(match, spots[f : f + 1, :], spot)
        named = share > 0.0
        rank = dot(jnp.where(named, 1.0, 0.0).astype(BF16), earlier)
        rank = jnp.where(named, rank, -1.0)
        found = []
        for r in range(32):
            mine = rank[r : r + 1, :] == order
            found.append(jnp.where(mine, 1.0, 0.0))
            part = jnp.where(mine, share[r : r + 1, :], 0.0)
            weights[g * 4 + s, pl.ds(r * 8, 8), :] = jnp.broadcast_to(
                jnp.sum(part, axis=1, keepdims=True), (8, LANES)
            )
            places[g, pl.ds((r // 4) * LANES + (r % 4) * GROUP + s * SLOTS, SLOTS), :] = (
                jnp.where(mine, spot[r : r + 1, :], 0.0)[:SLOTS]
            )
        picks[g * 4 + s] = jnp.concatenate(found, axis=0).astype(BF16)

    def find_labels(g):
        b = AXES[g][1]
        for ih in range(8):
            places[g, pl.ds(ih * LANES + BLOCK, LANES - BLOCK), :] = jnp.zeros(
                (LANES - BLOCK, LANES), F32
            )
        found = dot(jnp.ones((8, LANES), BF16), places[g].astype(BF16), ((1,), (1,)))
        for ih in range(8):
            line = found[0:1, ih * LANES : (ih + 1) * LANES]
            if ih == 0:
                labels_in[g * 8] = line
            else:
                labels_out[g * 8 + ih - 1] = line
        for ih in range(1, 8):
            remote(
                labels_out.at[g * 8 + ih - 1], labels_in.at[g * 8 + ih],
                label_send, label_recv.at[g], device({b: ih // 2}, ih % 2),
            )

    for g in range(3):
        find_slots(g, 0, meta[...])
    for g in range(3):
        whole(metas, g * 3, 3, meta_recv.at[g])
        for s in range(1, 4):
            find_slots(g, s, metas[g * 3 + s - 1])
        find_labels(g)

    def pack(c):
        g = c % 3
        b = AXES[g][1]
        for s in range(4):
            if s == 1:
                whole(spread_in, c * 3 * LANES, 3 * LANES, spread_recv.at[c])
            if s == 0:
                value = tiles[pl.ds(c * LANES, LANES), :]
            else:
                value = spread_in[pl.ds((c * 3 + s - 1) * LANES, LANES), :]
            pick = picks[g * 4 + s]
            value = dot(
                jnp.concatenate([pick, pick], axis=1), jnp.concatenate(split2(value), axis=0)
            )
            value = value * weights[g * 4 + s]
            for r in range(32):
                ih, j = r // 4, r % 4
                piece = value[r * 8 : r * 8 + SLOTS]
                within = j * GROUP + s * SLOTS
                if ih == 0:
                    slots_in[pl.ds(c * 8 * BLOCK + within, SLOTS), :] = piece
                else:
                    slots_out[pl.ds((c * 7 + ih - 1) * BLOCK + within, SLOTS), :] = piece
        for ih in range(1, 8):
            remote(
                slots_out.at[pl.ds((c * 7 + ih - 1) * BLOCK, BLOCK)],
                slots_in.at[pl.ds((c * 8 + ih) * BLOCK, BLOCK)],
                slot_send, slot_recv.at[c], device({b: ih // 2}, ih % 2),
            )

    for c in range(UNITS):
        pack(c)

    def inflow(base, count, all_ref, width):
        columns = []
        for w in range(width // LANES):
            direct, through = [], []
            for i in range(count):
                value = all_ref[i, :, pl.ds(w * LANES, LANES)]
                direct.append(coef[base + i] * value)
                through.append(coef[base + count + i] * value)
            while len(direct) > 1:
                direct = [a + b for a, b in zip(direct[::2], direct[1::2])]
                through = [a + b for a, b in zip(through[::2], through[1::2])]
            columns.append(direct[0] + pltpu.roll(through[0], planes, 0))
        return columns[0] if len(columns) == 1 else jnp.concatenate(columns, axis=1)

    wide = 8 * GROUP
    out_lane = iota((1, wide), 1)
    sender = jnp.zeros((1, wide), jnp.int32)
    for m in range(1, 8):
        sender += (out_lane >= m * GROUP).astype(jnp.int32)
    within = out_lane - sender * GROUP
    in_lane = iota((LANES, wide), 0)
    sender_row = iota((8, wide), 0) == sender
    tile_index = iota((LANES, wide), 0).astype(F32)
    selects = []
    for g in range(3):
        whole(labels_in, g * 8 + 1, 7, label_recv.at[g])
        lines = labels_in[pl.ds(g * 8, 8)].reshape(8, LANES).astype(BF16)
        row_of = []
        for j in range(4):
            choose = in_lane == within + j * GROUP
            named = dot(lines, choose.astype(BF16))
            named = jnp.sum(jnp.where(sender_row, named, 0.0), axis=0, keepdims=True)
            row_of.append((tile_index == named).astype(BF16))
        selects.append(row_of)

    def unpack(c):
        g = c % 3
        e = AXES[g][2]
        whole(slots_in, (c * 8 + 1) * BLOCK, 7 * BLOCK, slot_recv.at[c])
        for j in (2, 1, 3, 0):
            rows = jnp.concatenate(
                [
                    slots_in[pl.ds((c * 8 + ih) * BLOCK + j * GROUP, GROUP), :]
                    for ih in range(8)
                ],
                axis=0,
            )
            value = dot(selects[g][j], jnp.concatenate(split2(rows), axis=1))
            value = value[:, :LANES] + value[:, LANES:]
            if j == 0:
                own_sum[pl.ds(c * LANES, LANES), :] = value
            else:
                at = pl.ds((c * 3 + j - 1) * LANES, LANES)
                partial_out[at, :] = value
                remote(
                    partial_out.at[at], partial_in.at[at],
                    partial_send, partial_recv.at[c], device({e: j}, 0),
                )

    for c in range(UNITS):
        unpack(c)
    for c in range(UNITS):
        whole(partial_in, c * 3 * LANES, 3 * LANES, partial_recv.at[c])
        total = own_sum[pl.ds(c * LANES, LANES), :]
        for j in range(3):
            total += partial_in[pl.ds((c * 3 + j) * LANES, LANES), :]
        regroup[pl.ds(c, LANES, stride=PITCH), :] = total
    loads[4].wait()
    for xo in range(tile_rows):
        parts = [
            regroup[pl.ds((xo * tile_cols + yo) * PITCH, UNITS), :] for yo in range(tile_cols)
        ]
        for g, value in enumerate(block_transpose(parts)):
            pushed_ref[g // 2, pl.ds(xo * TS + (g % 2) * 8, 8), :] = value

    ends = jnp.zeros((8, cy), F32)
    for z in range(planes):
        both = jnp.concatenate(split2(target[z] - pushed_ref[z]), axis=1)
        halves[z] = both
        value = dot(xends_tab[z], both)
        ends += value[:8, :cy] + (value[:8, cy:] + value[8:, :cy])
    xmsg[...] = ends
    for s in range(4):
        for h in range(2):
            if s + h:
                remote(xmsg, xall.at[p], x_send, x_recv, device({1: s}, h))
    xall[p] = ends
    y_ends = jnp.zeros((8, cx), F32)
    for z in range(planes):
        both = halves[z]
        value = dot(xtab_hi[z], both)
        value = value[:, :cy] + (value[:, cy:] + dot(xtab_lo[z], both[:, :cy]))
        smooth[z] = value
        value = dot(yends_tab[z], jnp.concatenate(split2(value), axis=0), ((1,), (1,)))
        y_ends += value[:8, :cx] + (value[:8, cx:] + value[8:, :cx])
    whole(xall, 0, n_gx - 1, x_recv)
    flow = inflow(0, n_gx, xall, cy)
    at_last = jnp.sum(flow * last_rows, axis=1, keepdims=True)
    at_first = jnp.sum(flow * first_rows, axis=1, keepdims=True)
    entered = jnp.where(upper, at_last, pltpu.roll(jnp.broadcast_to(at_first, (8, LANES)), 4, 0)[:, 0:1])
    left = jnp.where(upper, pltpu.roll(jnp.broadcast_to(at_last, (8, LANES)), 4, 0)[:, 0:1], at_first)
    y_ends += edge_rows[0] * entered + edge_rows[1] * left
    ymsg[...] = y_ends
    for dz in range(4):
        for dx in range(4):
            if dz + dx:
                remote(ymsg, yall.at[q], y_send, y_recv, device({2: dz, 0: dx}, 0))
    yall[q] = y_ends

    loads[5].wait()
    for z in range(planes):
        value = smooth[z] + (
            xfill[z] * flow[z : z + 1] + xfill[planes + z] * flow[planes + z : planes + z + 1]
        )
        potential[z] = potential[z] + dot3(split2(value), (ytab_hi[z], ytab_lo[z]))
    whole(yall, 0, n_gy - 1, y_recv)
    flow = inflow(2 * n_gx, n_gy, yall, cx)
    hi = flow.astype(BF16).astype(F32)
    flow = jnp.concatenate([hi, flow - hi, hi, flow - hi], axis=0).astype(BF16)
    for z in range(planes):
        next_ref[z] = potential[z] + dot(flow, yfill_tab[z], ((0,), (0,)))

    whole(metas, 0, 9, meta_send)
    whole(spread_in, 0, 3 * UNITS * LANES, spread_send)
    whole(slots_out, 0, 7 * UNITS * BLOCK, slot_send)
    whole(labels_out, 0, 21, label_send)
    whole(partial_out, 0, 3 * UNITS * LANES, partial_send)
    whole(xall, 0, n_gx - 1, x_send)
    whole(yall, 0, n_gy - 1, y_send)


def per_device(source_mass, target_density, potential, dest_device, dest_tile, mass_counts, reach):
    planes, cx, cy = source_mass.shape

    def lanes(a):
        return jnp.swapaxes(a.reshape(a.shape[2:]), 0, 1)

    hbm = pl.BlockSpec(memory_space=pl.ANY)
    dma = pltpu.SemaphoreType.DMA
    vmem = pltpu.VMEM
    grid = jax.ShapeDtypeStruct((planes, cx, cy), F32)
    field = vmem((planes, cx, cy), F32)

    def rows(count):
        return vmem((count, LANES), F32)

    return pl.pallas_call(
        kernel,
        out_shape=(grid, grid),
        in_specs=[hbm] * 7,
        out_specs=(pl.BlockSpec(memory_space=vmem), pl.BlockSpec(memory_space=vmem)),
        scratch_shapes=[
            field, field, field, field,
            pltpu.SMEM((planes,), F32),
            vmem((3, 4, LANES), jnp.int32),
            vmem((9, 3, 4, LANES), jnp.int32),
            rows(UNITS * LANES), rows(LANES * PITCH + 16), rows(3 * UNITS * LANES),
            vmem((12, 256, LANES), BF16),
            vmem((12, 256, LANES), F32),
            vmem((3, 8 * LANES, LANES), F32),
            rows(7 * UNITS * BLOCK + 8), rows(8 * UNITS * BLOCK + 8),
            vmem((24, 1, LANES), F32),
            vmem((24, 1, LANES), F32),
            rows(3 * UNITS * LANES), rows(3 * UNITS * LANES), rows(UNITS * LANES),
            vmem((planes, cx, cx), BF16),
            vmem((planes, cx, cx), BF16),
            vmem((planes, cy, cy), BF16),
            vmem((planes, cy, cy), BF16),
            vmem((planes, 16, cx), BF16),
            vmem((planes, 16, cy), BF16),
            vmem((2 * planes, cx, LANES), F32),
            vmem((planes, 32, cy), BF16),
            vmem((48, 8, LANES), F32),
            vmem((2, 8, cx), F32),
            vmem((planes, cx, 2 * cy), BF16),
            vmem((8, cy), F32),
            vmem((8, 8, cy), F32),
            vmem((8, cx), F32),
            vmem((16, 8, cx), F32),
            dma((7,)), dma, dma((3,)), dma, dma((UNITS,)),
            dma, dma((UNITS,)), dma, dma((3,)), dma, dma((UNITS,)),
            dma, dma, dma, dma,
        ],
        compiler_params=pltpu.CompilerParams(collective_id=0, has_side_effects=True, vmem_limit_bytes=40 * 1024 * 1024),
        name="dual_step",
    )(
        *[
            pltpu.with_memory_space_constraint(a, pltpu.HBM)
            for a in (
                source_mass, target_density, potential,
                lanes(dest_device), lanes(dest_tile), lanes(mass_counts), reach,
            )
        ],
    )


def solution(mesh):
    in_specs = (
        P(None, "gx", "gy"),
        P(None, "gx", "gy"),
        P(None, "gx", "gy"),
        P("gx", "gy", None, None),
        P("gx", "gy", None, None),
        P("gx", "gy", None, None),
        P(),
    )
    out_specs = (P(None, "gx", "gy"), P(None, "gx", "gy"))
    return jax.shard_map(
        per_device, mesh=mesh, in_specs=in_specs, out_specs=out_specs, check_vma=False
    )
```

```python
import jax
import jax.numpy as jnp
from jax import lax
from jax.experimental import pallas as pl
from jax.experimental.pallas import tpu as pltpu
from jax.sharding import PartitionSpec as P

MESH = pl.DeviceIdType.MESH
TS = 16
SLOTS = 6
LANES = 128
UNITS = 8
AXES = ((0, 1, 2), (1, 2, 0), (2, 0, 1))
GROUP = SLOTS * 4
BLOCK = 4 * GROUP
EARLY = 5
PITCH = 9
F32 = jnp.float32
BF16 = jnp.bfloat16


def split2(a):
    hi = a.astype(BF16)
    return hi, (a - hi.astype(F32)).astype(BF16)


def dot(a, b, dims=((1,), (0,))):
    return lax.dot_general(a, b, (dims, ((), ())), preferred_element_type=F32)


def dot3(a, b, dims=((1,), (0,))):
    ah, al = a
    bh, bl = b
    return dot(ah, bh, dims) + (dot(ah, bl, dims) + dot(al, bh, dims))


def dot_f32(a, b, dims=((1,), (0,))):
    return lax.dot_general(
        a, b, (dims, ((), ())), precision=lax.Precision.HIGHEST, preferred_element_type=F32
    )


def iota(shape, axis):
    return lax.broadcasted_iota(jnp.int32, shape, axis)


def block_transpose(vectors):
    lane_block = iota((8, LANES), 1) // TS
    vectors = list(vectors)
    for bit in (4, 2, 1):
        low = (lane_block & bit) == 0
        result = [None] * 8
        for a in range(8):
            if a & bit:
                continue
            b = a | bit
            up, down = vectors[a], vectors[b]
            result[a] = jnp.where(low, up, pltpu.roll(down, bit * TS, 1))
            result[b] = jnp.where(low, pltpu.roll(up, LANES - bit * TS, 1), down)
        vectors = result
    return vectors


def powers(logs, exponent):
    return jnp.exp(exponent.astype(F32) * logs)


def whole(ref, first, count, sem):
    part = ref.at[pl.ds(first, count)]
    pltpu.make_async_copy(part, part, sem).wait()


def kernel(
    source_ref, target_ref, potential_ref, device_ref, tile_ref, count_ref, reach_hbm,
    pushed_ref, next_ref,
    natural, target, potential, smooth, reach_ref,
    meta, metas, tiles, regroup, spread_in, picks, weights, places,
    slots_out, slots_in, labels_out, labels_in,
    partial_out, partial_in, own_sum,
    xtab_hi, xtab_lo, ytab_hi, ytab_lo, xends_tab, yends_tab, xfill, yfill_tab,
    coef, edge_rows, halves, xmsg, xall, ymsg, yall,
    load_sem, meta_send, meta_recv, spread_send, spread_recv,
    slot_send, slot_recv, own_recv, label_send, label_recv,
    partial_send, partial_recv, x_send, x_recv, y_send, y_recv,
):
    p, q = lax.axis_index("gx"), lax.axis_index("gy")
    n_gx, n_gy = 8, 16
    planes, cx, cy = source_ref.shape
    tile_rows, tile_cols = cx // TS, cy // TS
    here = (q & 3, p >> 1, q >> 2)
    core = p & 1
    stride = (1, 2 * n_gy, 4)

    def device(moves, other):
        x, y, z = [(here[axis] + moves.get(axis, 0)) & 3 for axis in range(3)]
        return y * 2 + (core ^ other), z * 4 + x

    def remote(src, dst, send, recv, to):
        pltpu.make_async_remote_copy(
            src_ref=src, dst_ref=dst, send_sem=send, recv_sem=recv,
            device_id=to, device_id_type=MESH,
        ).start()

    split = [pl.ds(r * (cx // 2), cx // 2) for r in range(2)]
    loads = [
        pltpu.make_async_copy(a, b, load_sem.at[i])
        for i, (a, b) in enumerate([
            (source_ref.at[:, split[0]], natural.at[:, split[0]]),
            (source_ref.at[:, split[1]], natural.at[:, split[1]]),
            (device_ref, meta.at[0]), (tile_ref, meta.at[1]), (count_ref, meta.at[2]),
            (reach_hbm, reach_ref), (target_ref, target), (potential_ref, potential),
        ])
    ]
    for load in loads:
        load.start()

    barrier = pltpu.get_barrier_semaphore()
    peers = [({axis: s}, h) for axis in range(3) for s in range(1, 4) for h in range(2)]
    peers.append(({}, 1))
    for moves, other in peers:
        pl.semaphore_signal(
            barrier, inc=1, device_id=device(moves, other), device_id_type=MESH
        )

    for xo in range(tile_rows):
        if xo % (tile_rows // 2) == 0:
            loads[xo // (tile_rows // 2)].wait()
        parts = [
            natural[g // 2, pl.ds(xo * TS + (g % 2) * 8, 8), :] for g in range(2 * planes)
        ]
        for yo, value in enumerate(block_transpose(parts)):
            regroup[pl.ds((xo * tile_cols + yo) * PITCH, UNITS), :] = value
    for load in loads[2:5]:
        load.wait()
    pl.semaphore_wait(barrier, len(peers))
    for g, (a, _, _) in enumerate(AXES):
        for s in range(1, 4):
            remote(meta, metas.at[g * 3 + s - 1], meta_send, meta_recv.at[g], device({a: s}, 0))
    for c in range(UNITS):
        tiles[pl.ds(c * LANES, LANES), :] = regroup[pl.ds(c, LANES, stride=PITCH), :]
        for s in (2, 1, 3):
            remote(
                tiles.at[pl.ds(c * LANES, LANES)],
                spread_in.at[pl.ds((c * 3 + s - 1) * LANES, LANES)],
                spread_send, spread_recv.at[c], device({AXES[c % 3][0]: s}, 0),
            )

    loads[5].wait()
    decay = [jnp.full((1, 1), 1.0 - 1.0 / reach_ref[z], F32) for z in range(planes)]
    logs = [jnp.log(d) for d in decay]
    scale = [(1.0 - d) ** 2 for d in decay]
    row8 = iota((8, 1), 0)

    def both_rows(values):
        result = jnp.zeros((8, values[0].shape[1]), F32)
        for z, v in enumerate(values):
            result = jnp.where((row8 == z) | (row8 == planes + z), v, result)
        return result

    def stacked(a):
        hi = a.astype(BF16).astype(F32)
        return jnp.concatenate([hi, a - hi], axis=0).astype(BF16)

    logs8, scale8 = both_rows(logs), both_rows(scale)

    def rows_of(n):
        at = iota((8, n), 1)
        squares = powers(2.0 * logs8, at)
        hi = squares.astype(BF16).astype(F32)
        mid = (squares - hi).astype(BF16).astype(F32)
        parts = jnp.concatenate([hi, mid, squares - hi - mid, jnp.zeros_like(hi)], axis=0)
        inside = (iota((n, n), 0) + iota((n, n), 1) < n).astype(BF16)
        sums = dot(parts.astype(BF16), inside)
        sums = sums[0:8] + (sums[8:16] + sums[16:24])
        last = powers(logs8, n - 1 - at)
        fall = powers(logs8, n - at)
        first = scale8 * powers(logs8, at) * sums
        swept = scale8 * powers(logs8, at + 1) * sums
        return sums, last, first, swept, fall

    upper = row8 < planes
    sums_x, last_x, first_x, swept_x, fall_x = rows_of(cx)
    sums_y, last_rows, first_rows, swept_y, fall_y = rows_of(cy)
    edge_rows[0], edge_rows[1] = swept_x, fall_x
    spare = jnp.zeros((cy - 24, cx), F32)
    columns = jnp.transpose(
        jnp.concatenate(
            [sums_x, jnp.where(upper, swept_x, fall_x),
             jnp.concatenate([sums_y, sums_y], axis=1), spare],
            axis=0,
        )
    )
    across_row = iota((cy, cy), 0)
    gap = across_row - iota((cy, cy), 1)
    for z in range(planes):
        near = powers(logs[z], jnp.abs(gap)) * scale[z]
        below = powers(logs[z], gap + cy) * scale[z]
        above = powers(logs[z], cy - gap) * scale[z]

        def column(i, first, count):
            return jnp.broadcast_to(columns[first : first + count, i : i + 1], (count, cy))

        low = gap >= 0
        g0, g1, gy = column(z, 0, cy), column(z, cy, cy), column(16 + z, 0, cy)
        r0, r1, ry = sums_x[z : z + 1, :cy], sums_x[z : z + 1, cy:], sums_y[z : z + 1]
        for r, (left_part, right_part) in enumerate([
            (near * jnp.where(low, g0, r0), above * r1),
            (below * g1, near * jnp.where(low, g1, r1)),
        ]):
            at = pl.ds(r * cy, cy)
            for w, part in enumerate((left_part, right_part)):
                hi, lo = split2(part)
                xtab_hi[z, at, pl.ds(w * cy, cy)] = hi
                xtab_lo[z, at, pl.ds(w * cy, cy)] = lo
        ytab_hi[z], ytab_lo[z] = split2(near * jnp.where(low, gy, ry))
        xfill[z] = jnp.broadcast_to(columns[:, 8 + z : 9 + z], (cx, LANES))
        xfill[planes + z] = jnp.broadcast_to(
            columns[:, 8 + planes + z : 9 + planes + z], (cx, LANES)
        )
        one, two = row8 == z, row8 == planes + z
        xends_tab[z] = stacked(jnp.where(one, last_x, 0.0) + jnp.where(two, first_x, 0.0))
        yends_tab[z] = stacked(jnp.where(one, last_rows, 0.0) + jnp.where(two, first_rows, 0.0))
        fill = jnp.where(one, swept_y, 0.0) + jnp.where(two, fall_y, 0.0)
        hi = fill.astype(BF16).astype(F32)
        yfill_tab[z] = jnp.concatenate([hi, hi, fill - hi, fill - hi], axis=0).astype(BF16)

    def coefficients(base, count, at, n, first):
        across = jnp.exp(float(n) * logs8)
        powers_of = [jnp.ones((8, 1), F32)]
        for _ in range(count - 1):
            powers_of.append(powers_of[-1] * across)
        low = row8 < planes
        before, after = [], []
        for i in range(count):
            coming = jnp.zeros((8, 1), F32)
            going = jnp.zeros((8, 1), F32)
            for m in range(count - 1):
                coming = jnp.where(at - 1 - i == m, powers_of[m], coming)
                going = jnp.where(i - at - 1 == m, powers_of[m], going)
            before.append(coming)
            after.append(going)
        through = jnp.zeros((8, 1), F32)
        crossing = [None] * count
        for i in reversed(range(count)):
            crossing[i] = first * through
            through = after[i] + across * through
        for i in range(count):
            coef[base + i] = jnp.broadcast_to(jnp.where(low, before[i], after[i]), (8, LANES))
            coef[base + count + i] = jnp.broadcast_to(
                jnp.where(low, crossing[i], 0.0), (8, LANES)
            )

    coefficients(0, n_gx, p, cx, swept_x[:, 0:1])
    coefficients(2 * n_gx, n_gy, q, cy, swept_y[:, 0:1])

    earlier = (iota((LANES, LANES), 0) < iota((LANES, LANES), 1)).astype(BF16)
    row = iota((32, LANES), 0)
    row_target, row_j = row >> 2, row & 3
    order = iota((8, LANES), 0).astype(F32)

    def find_slots(g, s, info):
        a, b, e = AXES[g]
        names, spots, counts = info[0], info[1].astype(F32), info[2].astype(F32)
        shares = counts / jnp.sum(counts, axis=0, keepdims=True)
        number = (
            here[a] * stride[a] + ((here[b] + (row_target >> 1)) & 3) * stride[b]
            + (core ^ (row_target & 1)) * n_gy + ((here[e] + row_j) & 3) * stride[e]
        )
        share = jnp.zeros((32, LANES), F32)
        spot = jnp.zeros((32, LANES), F32)
        for f in range(4):
            match = number == names[f : f + 1, :]
            share = jnp.where(match, shares[f : f + 1, :], share)
            spot = jnp.where(match, spots[f : f + 1, :], spot)
        named = share > 0.0
        rank = dot(jnp.where(named, 1.0, 0.0).astype(BF16), earlier)
        rank = jnp.where(named, rank, -1.0)
        found = []
        for r in range(32):
            mine = rank[r : r + 1, :] == order
            found.append(jnp.where(mine, 1.0, 0.0))
            part = jnp.where(mine, share[r : r + 1, :], 0.0)
            weights[g * 4 + s, pl.ds(r * 8, 8), :] = jnp.broadcast_to(
                jnp.sum(part, axis=1, keepdims=True), (8, LANES)
            )
            places[g, pl.ds((r // 4) * LANES + (r % 4) * GROUP + s * SLOTS, SLOTS), :] = (
                jnp.where(mine, spot[r : r + 1, :], 0.0)[:SLOTS]
            )
        picks[g * 4 + s] = jnp.concatenate(found, axis=0).astype(BF16)

    def find_labels(g):
        b = AXES[g][1]
        for ih in range(8):
            places[g, pl.ds(ih * LANES + BLOCK, LANES - BLOCK), :] = jnp.zeros(
                (LANES - BLOCK, LANES), F32
            )
        found = dot(jnp.ones((8, LANES), BF16), places[g].astype(BF16), ((1,), (1,)))
        for ih in range(8):
            line = found[0:1, ih * LANES : (ih + 1) * LANES]
            if ih == 0:
                labels_in[g * 8] = line
            else:
                labels_out[g * 8 + ih - 1] = line
        for ih in range(1, 8):
            remote(
                labels_out.at[g * 8 + ih - 1], labels_in.at[g * 8 + ih],
                label_send, label_recv.at[g], device({b: ih // 2}, ih % 2),
            )

    for g in range(3):
        find_slots(g, 0, meta[...])
    for g in range(3):
        whole(metas, g * 3, 3, meta_recv.at[g])
        for s in range(1, 4):
            find_slots(g, s, metas[g * 3 + s - 1])
        find_labels(g)

    def pack(c):
        g = c % 3
        for s in range(4):
            if s == 1:
                whole(spread_in, c * 3 * LANES, 3 * LANES, spread_recv.at[c])
            if s == 0:
                value = tiles[pl.ds(c * LANES, LANES), :]
            else:
                value = spread_in[pl.ds((c * 3 + s - 1) * LANES, LANES), :]
            pick = picks[g * 4 + s]
            value = dot(
                jnp.concatenate([pick, pick], axis=1), jnp.concatenate(split2(value), axis=0)
            )
            value = value * weights[g * 4 + s]
            for r in range(32):
                ih, j = r // 4, r % 4
                piece = value[r * 8 : r * 8 + SLOTS]
                within = j * GROUP + s * SLOTS
                if ih == 0:
                    slots_in[pl.ds(c * 8 * BLOCK + within, SLOTS), :] = piece
                else:
                    slots_out[pl.ds((c * 7 + ih - 1) * BLOCK + within, SLOTS), :] = piece
        send_slots(c, GROUP, BLOCK - GROUP, slot_recv)

    def send_slots(c, first, count, recv):
        for ih in range(1, 8):
            remote(
                slots_out.at[pl.ds((c * 7 + ih - 1) * BLOCK + first, count)],
                slots_in.at[pl.ds((c * 8 + ih) * BLOCK + first, count)],
                slot_send, recv.at[c], device({AXES[c % 3][1]: ih // 2}, ih % 2),
            )

    for c in range(UNITS):
        pack(c)

    def inflow(base, count, all_ref, width):
        columns = []
        for w in range(width // LANES):
            direct, through = [], []
            for i in range(count):
                value = all_ref[i, :, pl.ds(w * LANES, LANES)]
                direct.append(coef[base + i] * value)
                through.append(coef[base + count + i] * value)
            while len(direct) > 1:
                direct = [a + b for a, b in zip(direct[::2], direct[1::2])]
                through = [a + b for a, b in zip(through[::2], through[1::2])]
            columns.append(direct[0] + pltpu.roll(through[0], planes, 0))
        return columns[0] if len(columns) == 1 else jnp.concatenate(columns, axis=1)

    wide = 8 * GROUP
    out_lane = iota((1, wide), 1)
    sender = jnp.zeros((1, wide), jnp.int32)
    for m in range(1, 8):
        sender += (out_lane >= m * GROUP).astype(jnp.int32)
    within = out_lane - sender * GROUP
    in_lane = iota((LANES, wide), 0)
    sender_row = iota((8, wide), 0) == sender
    tile_index = iota((LANES, wide), 0).astype(F32)
    selects = []
    for g in range(3):
        whole(labels_in, g * 8 + 1, 7, label_recv.at[g])
        lines = labels_in[pl.ds(g * 8, 8)].reshape(8, LANES).astype(BF16)
        row_of = []
        for j in range(4):
            choose = in_lane == within + j * GROUP
            named = dot(lines, choose.astype(BF16))
            named = jnp.sum(jnp.where(sender_row, named, 0.0), axis=0, keepdims=True)
            row_of.append((tile_index == named).astype(BF16))
        selects.append(row_of)

    def collect(c, j):
        rows = jnp.concatenate(
            [slots_in[pl.ds((c * 8 + ih) * BLOCK + j * GROUP, GROUP), :] for ih in range(8)],
            axis=0,
        )
        value = dot(selects[c % 3][j], jnp.concatenate(split2(rows), axis=1))
        return value[:, :LANES] + value[:, LANES:]

    for c in range(UNITS):
        whole(slots_in, (c * 8 + 1) * BLOCK, 7 * (BLOCK - GROUP), slot_recv.at[c])
        for j in (2, 1, 3):
            at = pl.ds((c * 3 + j - 1) * LANES, LANES)
            partial_out[at, :] = collect(c, j)
            remote(
                partial_out.at[at], partial_in.at[at],
                partial_send, partial_recv.at[c], device({AXES[c % 3][2]: j}, 0),
            )
        if c < EARLY:
            send_slots(c, 0, GROUP, own_recv)
    for c in range(EARLY, UNITS):
        send_slots(c, 0, GROUP, own_recv)
    for c in range(UNITS):
        whole(slots_in, (c * 8 + 1) * BLOCK, 7 * GROUP, own_recv.at[c])
        own_sum[pl.ds(c * LANES, LANES), :] = collect(c, 0)
    for c in range(UNITS):
        whole(partial_in, c * 3 * LANES, 3 * LANES, partial_recv.at[c])
        total = own_sum[pl.ds(c * LANES, LANES), :]
        for j in range(3):
            total += partial_in[pl.ds((c * 3 + j) * LANES, LANES), :]
        regroup[pl.ds(c, LANES, stride=PITCH), :] = total
    loads[6].wait()
    for xo in range(tile_rows):
        parts = [
            regroup[pl.ds((xo * tile_cols + yo) * PITCH, UNITS), :] for yo in range(tile_cols)
        ]
        for g, value in enumerate(block_transpose(parts)):
            pushed_ref[g // 2, pl.ds(xo * TS + (g % 2) * 8, 8), :] = value

    ends = jnp.zeros((8, cy), F32)
    for z in range(planes):
        both = jnp.concatenate(split2(target[z] - pushed_ref[z]), axis=1)
        halves[z] = both
        value = dot(xends_tab[z], both)
        ends += value[:8, :cy] + (value[:8, cy:] + value[8:, :cy])
    xmsg[...] = ends
    for s in range(4):
        for h in range(2):
            if s + h:
                remote(xmsg, xall.at[p], x_send, x_recv, device({1: s}, h))
    xall[p] = ends
    y_ends = jnp.zeros((8, cx), F32)
    for z in range(planes):
        both = halves[z]
        value = dot(xtab_hi[z], both)
        value = value[:, :cy] + (value[:, cy:] + dot(xtab_lo[z], both[:, :cy]))
        smooth[z] = value
        value = dot(yends_tab[z], jnp.concatenate(split2(value), axis=0), ((1,), (1,)))
        y_ends += value[:8, :cx] + (value[:8, cx:] + value[8:, :cx])
    whole(xall, 0, n_gx - 1, x_recv)
    flow = inflow(0, n_gx, xall, cy)
    at_last = jnp.sum(flow * last_rows, axis=1, keepdims=True)
    at_first = jnp.sum(flow * first_rows, axis=1, keepdims=True)
    entered = jnp.where(upper, at_last, pltpu.roll(jnp.broadcast_to(at_first, (8, LANES)), 4, 0)[:, 0:1])
    left = jnp.where(upper, pltpu.roll(jnp.broadcast_to(at_last, (8, LANES)), 4, 0)[:, 0:1], at_first)
    y_ends += edge_rows[0] * entered + edge_rows[1] * left
    ymsg[...] = y_ends
    for dz in range(4):
        for dx in range(4):
            if dz + dx:
                remote(ymsg, yall.at[q], y_send, y_recv, device({2: dz, 0: dx}, 0))
    yall[q] = y_ends

    loads[7].wait()
    for z in range(planes):
        value = smooth[z] + (
            xfill[z] * flow[z : z + 1] + xfill[planes + z] * flow[planes + z : planes + z + 1]
        )
        potential[z] = potential[z] + dot3(split2(value), (ytab_hi[z], ytab_lo[z]))
    whole(yall, 0, n_gy - 1, y_recv)
    flow = inflow(2 * n_gx, n_gy, yall, cx)
    hi = flow.astype(BF16).astype(F32)
    flow = jnp.concatenate([hi, flow - hi, hi, flow - hi], axis=0).astype(BF16)
    for z in range(planes):
        next_ref[z] = potential[z] + dot(flow, yfill_tab[z], ((0,), (0,)))

    whole(metas, 0, 9, meta_send)
    whole(spread_in, 0, 3 * UNITS * LANES, spread_send)
    whole(slots_out, 0, 7 * UNITS * BLOCK, slot_send)
    whole(labels_out, 0, 21, label_send)
    whole(partial_out, 0, 3 * UNITS * LANES, partial_send)
    whole(xall, 0, n_gx - 1, x_send)
    whole(yall, 0, n_gy - 1, y_send)


def store(pushed_ref, next_ref, pushed_out, next_out, sems):
    copies = [
        pltpu.make_async_copy(pushed_ref, pushed_out, sems.at[0]),
        pltpu.make_async_copy(next_ref, next_out, sems.at[1]),
    ]
    for copy in copies:
        copy.start()
    for copy in copies:
        copy.wait()


def per_device(source_mass, target_density, potential, dest_device, dest_tile, mass_counts, reach):
    planes, cx, cy = source_mass.shape

    def lanes(a):
        return jnp.swapaxes(a.reshape(a.shape[2:]), 0, 1)

    hbm = pl.BlockSpec(memory_space=pl.ANY)
    dma = pltpu.SemaphoreType.DMA
    vmem = pltpu.VMEM
    grid = jax.ShapeDtypeStruct((planes, cx, cy), F32)
    field = vmem((planes, cx, cy), F32)

    def rows(count):
        return vmem((count, LANES), F32)

    fields = pl.pallas_call(
        kernel,
        out_shape=(grid, grid),
        in_specs=[hbm] * 7,
        out_specs=(pl.BlockSpec(memory_space=vmem), pl.BlockSpec(memory_space=vmem)),
        scratch_shapes=[
            field, field, field, field,
            pltpu.SMEM((planes,), F32),
            vmem((3, 4, LANES), jnp.int32),
            vmem((9, 3, 4, LANES), jnp.int32),
            rows(UNITS * LANES), rows(LANES * PITCH + 16), rows(3 * UNITS * LANES),
            vmem((12, 256, LANES), BF16),
            vmem((12, 256, LANES), F32),
            vmem((3, 8 * LANES, LANES), F32),
            rows(7 * UNITS * BLOCK + 8), rows(8 * UNITS * BLOCK + 8),
            vmem((24, 1, LANES), F32),
            vmem((24, 1, LANES), F32),
            rows(3 * UNITS * LANES), rows(3 * UNITS * LANES), rows(UNITS * LANES),
            vmem((planes, cx, cx), BF16),
            vmem((planes, cx, cx), BF16),
            vmem((planes, cy, cy), BF16),
            vmem((planes, cy, cy), BF16),
            vmem((planes, 16, cx), BF16),
            vmem((planes, 16, cy), BF16),
            vmem((2 * planes, cx, LANES), F32),
            vmem((planes, 32, cy), BF16),
            vmem((48, 8, LANES), F32),
            vmem((2, 8, cx), F32),
            vmem((planes, cx, 2 * cy), BF16),
            vmem((8, cy), F32),
            vmem((8, 8, cy), F32),
            vmem((8, cx), F32),
            vmem((16, 8, cx), F32),
            dma((8,)), dma, dma((3,)), dma, dma((UNITS,)),
            dma, dma((UNITS,)), dma((UNITS,)), dma, dma((3,)), dma, dma((UNITS,)),
            dma, dma, dma, dma,
        ],
        compiler_params=pltpu.CompilerParams(collective_id=0, has_side_effects=True, vmem_limit_bytes=40 * 1024 * 1024),
        name="dual_step",
    )(
        *[
            pltpu.with_memory_space_constraint(a, pltpu.HBM)
            for a in (
                source_mass, target_density, potential,
                lanes(dest_device), lanes(dest_tile), lanes(mass_counts), reach,
            )
        ],
    )

    local = pl.BlockSpec(memory_space=vmem)
    return pl.pallas_call(
        store,
        out_shape=(grid, grid),
        in_specs=[local, local],
        out_specs=(hbm, hbm),
        scratch_shapes=[dma((2,))],
        compiler_params=pltpu.CompilerParams(vmem_limit_bytes=4 * 1024 * 1024),
        name="store",
    )(*fields)


def solution(mesh):
    in_specs = (
        P(None, "gx", "gy"),
        P(None, "gx", "gy"),
        P(None, "gx", "gy"),
        P("gx", "gy", None, None),
        P("gx", "gy", None, None),
        P("gx", "gy", None, None),
        P(),
    )
    out_specs = (P(None, "gx", "gy"), P(None, "gx", "gy"))
    return jax.shard_map(
        per_device, mesh=mesh, in_specs=in_specs, out_specs=out_specs, check_vma=False
    )
```

```python
import jax
import jax.numpy as jnp
from jax import lax
from jax.experimental import pallas as pl
from jax.experimental.pallas import tpu as pltpu
from jax.sharding import PartitionSpec as P

MESH = pl.DeviceIdType.MESH
TS = 16
SLOTS = 6
LANES = 128
UNITS = 8
AXES = ((0, 1, 2), (1, 2, 0), (2, 0, 1))
GROUP = SLOTS * 4
BLOCK = 4 * GROUP
PITCH = 9
F32 = jnp.float32
BF16 = jnp.bfloat16


def split2(a):
    hi = a.astype(BF16)
    return hi, (a - hi.astype(F32)).astype(BF16)


def dot(a, b, dims=((1,), (0,))):
    return lax.dot_general(a, b, (dims, ((), ())), preferred_element_type=F32)


def dot3(a, b, dims=((1,), (0,))):
    ah, al = a
    bh, bl = b
    return dot(ah, bh, dims) + (dot(ah, bl, dims) + dot(al, bh, dims))


def dot_f32(a, b, dims=((1,), (0,))):
    return lax.dot_general(
        a, b, (dims, ((), ())), precision=lax.Precision.HIGHEST, preferred_element_type=F32
    )


def iota(shape, axis):
    return lax.broadcasted_iota(jnp.int32, shape, axis)


def block_transpose(vectors):
    lane_block = iota((8, LANES), 1) // TS
    vectors = list(vectors)
    for bit in (4, 2, 1):
        low = (lane_block & bit) == 0
        result = [None] * 8
        for a in range(8):
            if a & bit:
                continue
            b = a | bit
            up, down = vectors[a], vectors[b]
            result[a] = jnp.where(low, up, pltpu.roll(down, bit * TS, 1))
            result[b] = jnp.where(low, pltpu.roll(up, LANES - bit * TS, 1), down)
        vectors = result
    return vectors


def powers(logs, exponent):
    return jnp.exp(exponent.astype(F32) * logs)


def whole(ref, first, count, sem):
    part = ref.at[pl.ds(first, count)]
    pltpu.make_async_copy(part, part, sem).wait()


def kernel(
    source_ref, target_ref, potential_ref, device_ref, tile_ref, count_ref, reach_hbm,
    pushed_ref, next_ref,
    natural, target, potential, smooth, reach_ref,
    meta, metas, tiles, regroup, spread_in, picks, weights, places,
    slots_out, slots_in, labels_out, labels_in,
    far_out, far_in, partial_out, partial_in, own_sum,
    xtab_hi, xtab_lo, ytab_hi, ytab_lo, xends_tab, yends_tab, xfill, yfill_tab,
    coef, edge_rows, halves, xmsg, xall, ymsg, yall,
    load_sem, meta_send, meta_recv, spread_send, spread_recv,
    slot_send, slot_recv, own_recv, label_send, label_recv, far_send, far_recv,
    partial_send, partial_recv, x_send, x_recv, y_send, y_recv,
):
    p, q = lax.axis_index("gx"), lax.axis_index("gy")
    n_gx, n_gy = 8, 16
    planes, cx, cy = source_ref.shape
    tile_rows, tile_cols = cx // TS, cy // TS
    half = LANES // 2
    here = (q & 3, p >> 1, q >> 2)
    core = p & 1
    stride = (1, 2 * n_gy, 4)

    def device(moves, other):
        x, y, z = [(here[axis] + moves.get(axis, 0)) & 3 for axis in range(3)]
        return y * 2 + (core ^ other), z * 4 + x

    def remote(src, dst, send, recv, to):
        pltpu.make_async_remote_copy(
            src_ref=src, dst_ref=dst, send_sem=send, recv_sem=recv,
            device_id=to, device_id_type=MESH,
        ).start()

    split = [pl.ds(r * (cx // 2), cx // 2) for r in range(2)]
    loads = [
        pltpu.make_async_copy(a, b, load_sem.at[i])
        for i, (a, b) in enumerate([
            (source_ref.at[:, split[0]], natural.at[:, split[0]]),
            (source_ref.at[:, split[1]], natural.at[:, split[1]]),
            (device_ref, meta.at[0]), (tile_ref, meta.at[1]), (count_ref, meta.at[2]),
            (reach_hbm, reach_ref), (target_ref, target), (potential_ref, potential),
        ])
    ]
    for load in loads:
        load.start()

    barrier = pltpu.get_barrier_semaphore()
    peers = [({axis: s}, h) for axis in range(3) for s in range(1, 4) for h in range(2)]
    peers.append(({}, 1))
    for moves, other in peers:
        pl.semaphore_signal(
            barrier, inc=1, device_id=device(moves, other), device_id_type=MESH
        )

    for xo in range(tile_rows):
        if xo % (tile_rows // 2) == 0:
            loads[xo // (tile_rows // 2)].wait()
        parts = [
            natural[g // 2, pl.ds(xo * TS + (g % 2) * 8, 8), :] for g in range(2 * planes)
        ]
        for yo, value in enumerate(block_transpose(parts)):
            regroup[pl.ds((xo * tile_cols + yo) * PITCH, UNITS), :] = value
    for load in loads[2:5]:
        load.wait()
    pl.semaphore_wait(barrier, len(peers))
    for g, (a, _, _) in enumerate(AXES):
        for s in range(1, 4):
            remote(meta, metas.at[g * 3 + s - 1], meta_send, meta_recv.at[g], device({a: s}, 0))
    for c in range(UNITS):
        tiles[pl.ds(c * LANES, LANES), :] = regroup[pl.ds(c, LANES, stride=PITCH), :]
        for s in (2, 1, 3):
            remote(
                tiles.at[pl.ds(c * LANES, LANES)],
                spread_in.at[pl.ds((c * 3 + s - 1) * LANES, LANES)],
                spread_send, spread_recv.at[c], device({AXES[c % 3][0]: s}, 0),
            )

    loads[5].wait()
    decay = [jnp.full((1, 1), 1.0 - 1.0 / reach_ref[z], F32) for z in range(planes)]
    logs = [jnp.log(d) for d in decay]
    scale = [(1.0 - d) ** 2 for d in decay]
    row8 = iota((8, 1), 0)

    def both_rows(values):
        result = jnp.zeros((8, values[0].shape[1]), F32)
        for z, v in enumerate(values):
            result = jnp.where((row8 == z) | (row8 == planes + z), v, result)
        return result

    def stacked(a):
        hi = a.astype(BF16).astype(F32)
        return jnp.concatenate([hi, a - hi], axis=0).astype(BF16)

    logs8, scale8 = both_rows(logs), both_rows(scale)

    def rows_of(n):
        at = iota((8, n), 1)
        squares = powers(2.0 * logs8, at)
        hi = squares.astype(BF16).astype(F32)
        mid = (squares - hi).astype(BF16).astype(F32)
        parts = jnp.concatenate([hi, mid, squares - hi - mid, jnp.zeros_like(hi)], axis=0)
        inside = (iota((n, n), 0) + iota((n, n), 1) < n).astype(BF16)
        sums = dot(parts.astype(BF16), inside)
        sums = sums[0:8] + (sums[8:16] + sums[16:24])
        last = powers(logs8, n - 1 - at)
        fall = powers(logs8, n - at)
        first = scale8 * powers(logs8, at) * sums
        swept = scale8 * powers(logs8, at + 1) * sums
        return sums, last, first, swept, fall

    upper = row8 < planes
    sums_x, last_x, first_x, swept_x, fall_x = rows_of(cx)
    sums_y, last_rows, first_rows, swept_y, fall_y = rows_of(cy)
    edge_rows[0], edge_rows[1] = swept_x, fall_x
    spare = jnp.zeros((cy - 24, cx), F32)
    columns = jnp.transpose(
        jnp.concatenate(
            [sums_x, jnp.where(upper, swept_x, fall_x),
             jnp.concatenate([sums_y, sums_y], axis=1), spare],
            axis=0,
        )
    )
    across_row = iota((cy, cy), 0)
    gap = across_row - iota((cy, cy), 1)
    for z in range(planes):
        near = powers(logs[z], jnp.abs(gap)) * scale[z]
        below = powers(logs[z], gap + cy) * scale[z]
        above = powers(logs[z], cy - gap) * scale[z]

        def column(i, first, count):
            return jnp.broadcast_to(columns[first : first + count, i : i + 1], (count, cy))

        low = gap >= 0
        g0, g1, gy = column(z, 0, cy), column(z, cy, cy), column(16 + z, 0, cy)
        r0, r1, ry = sums_x[z : z + 1, :cy], sums_x[z : z + 1, cy:], sums_y[z : z + 1]
        for r, (left_part, right_part) in enumerate([
            (near * jnp.where(low, g0, r0), above * r1),
            (below * g1, near * jnp.where(low, g1, r1)),
        ]):
            at = pl.ds(r * cy, cy)
            for w, part in enumerate((left_part, right_part)):
                hi, lo = split2(part)
                xtab_hi[z, at, pl.ds(w * cy, cy)] = hi
                xtab_lo[z, at, pl.ds(w * cy, cy)] = lo
        ytab_hi[z], ytab_lo[z] = split2(near * jnp.where(low, gy, ry))
        xfill[z] = jnp.broadcast_to(columns[:, 8 + z : 9 + z], (cx, LANES))
        xfill[planes + z] = jnp.broadcast_to(
            columns[:, 8 + planes + z : 9 + planes + z], (cx, LANES)
        )
        one, two = row8 == z, row8 == planes + z
        xends_tab[z] = stacked(jnp.where(one, last_x, 0.0) + jnp.where(two, first_x, 0.0))
        yends_tab[z] = stacked(jnp.where(one, last_rows, 0.0) + jnp.where(two, first_rows, 0.0))
        fill = jnp.where(one, swept_y, 0.0) + jnp.where(two, fall_y, 0.0)
        hi = fill.astype(BF16).astype(F32)
        yfill_tab[z] = jnp.concatenate([hi, hi, fill - hi, fill - hi], axis=0).astype(BF16)

    def coefficients(base, count, at, n, first):
        across = jnp.exp(float(n) * logs8)
        powers_of = [jnp.ones((8, 1), F32)]
        for _ in range(count - 1):
            powers_of.append(powers_of[-1] * across)
        low = row8 < planes
        before, after = [], []
        for i in range(count):
            coming = jnp.zeros((8, 1), F32)
            going = jnp.zeros((8, 1), F32)
            for m in range(count - 1):
                coming = jnp.where(at - 1 - i == m, powers_of[m], coming)
                going = jnp.where(i - at - 1 == m, powers_of[m], going)
            before.append(coming)
            after.append(going)
        through = jnp.zeros((8, 1), F32)
        crossing = [None] * count
        for i in reversed(range(count)):
            crossing[i] = first * through
            through = after[i] + across * through
        for i in range(count):
            coef[base + i] = jnp.broadcast_to(jnp.where(low, before[i], after[i]), (8, LANES))
            coef[base + count + i] = jnp.broadcast_to(
                jnp.where(low, crossing[i], 0.0), (8, LANES)
            )

    coefficients(0, n_gx, p, cx, swept_x[:, 0:1])
    coefficients(2 * n_gx, n_gy, q, cy, swept_y[:, 0:1])

    earlier = (iota((LANES, LANES), 0) < iota((LANES, LANES), 1)).astype(BF16)
    row = iota((32, LANES), 0)
    row_target, row_j = row >> 2, row & 3
    order = iota((8, LANES), 0).astype(F32)

    def find_slots(g, s, info):
        a, b, e = AXES[g]
        names, spots, counts = info[0], info[1].astype(F32), info[2].astype(F32)
        shares = counts / jnp.sum(counts, axis=0, keepdims=True)
        number = (
            here[a] * stride[a] + ((here[b] + (row_target >> 1)) & 3) * stride[b]
            + (core ^ (row_target & 1)) * n_gy + ((here[e] + row_j) & 3) * stride[e]
        )
        share = jnp.zeros((32, LANES), F32)
        spot = jnp.zeros((32, LANES), F32)
        for f in range(4):
            match = number == names[f : f + 1, :]
            share = jnp.where(match, shares[f : f + 1, :], share)
            spot = jnp.where(match, spots[f : f + 1, :], spot)
        named = share > 0.0
        rank = dot(jnp.where(named, 1.0, 0.0).astype(BF16), earlier)
        rank = jnp.where(named, rank, -1.0)
        found = []
        for r in range(32):
            mine = rank[r : r + 1, :] == order
            found.append(jnp.where(mine, 1.0, 0.0))
            part = jnp.where(mine, share[r : r + 1, :], 0.0)
            weights[g * 4 + s, pl.ds(r * 8, 8), :] = jnp.broadcast_to(
                jnp.sum(part, axis=1, keepdims=True), (8, LANES)
            )
            places[g, pl.ds((r // 4) * LANES + (r % 4) * GROUP + s * SLOTS, SLOTS), :] = (
                jnp.where(mine, spot[r : r + 1, :], 0.0)[:SLOTS]
            )
        picks[g * 4 + s] = jnp.concatenate(found, axis=0).astype(BF16)

    def find_labels(g):
        b = AXES[g][1]
        for ih in range(8):
            places[g, pl.ds(ih * LANES + BLOCK, LANES - BLOCK), :] = jnp.zeros(
                (LANES - BLOCK, LANES), F32
            )
        found = dot(jnp.ones((8, LANES), BF16), places[g].astype(BF16), ((1,), (1,)))
        for ih in range(8):
            line = found[0:1, ih * LANES : (ih + 1) * LANES]
            if ih == 0:
                labels_in[g * 8] = line
            else:
                labels_out[g * 8 + ih - 1] = line
        for ih in range(1, 8):
            remote(
                labels_out.at[g * 8 + ih - 1], labels_in.at[g * 8 + ih],
                label_send, label_recv.at[g], device({b: ih // 2}, ih % 2),
            )

    for g in range(3):
        find_slots(g, 0, meta[...])
    for g in range(3):
        whole(metas, g * 3, 3, meta_recv.at[g])
        for s in range(1, 4):
            find_slots(g, s, metas[g * 3 + s - 1])
        find_labels(g)

    def pack(c):
        g = c % 3
        for s in range(4):
            if s == 1:
                whole(spread_in, c * 3 * LANES, 3 * LANES, spread_recv.at[c])
            if s == 0:
                value = tiles[pl.ds(c * LANES, LANES), :]
            else:
                value = spread_in[pl.ds((c * 3 + s - 1) * LANES, LANES), :]
            pick = picks[g * 4 + s]
            value = dot(
                jnp.concatenate([pick, pick], axis=1), jnp.concatenate(split2(value), axis=0)
            )
            value = value * weights[g * 4 + s]
            for r in range(32):
                ih, j = r // 4, r % 4
                piece = value[r * 8 : r * 8 + SLOTS]
                within = j * GROUP + s * SLOTS
                if ih == 0:
                    slots_in[pl.ds(c * 8 * BLOCK + within, SLOTS), :] = piece
                else:
                    slots_out[pl.ds((c * 7 + ih - 1) * BLOCK + within, SLOTS), :] = piece
        send_slots(c, GROUP, BLOCK - GROUP, slot_recv)

    def send_slots(c, first, count, recv):
        for ih in range(1, 8):
            remote(
                slots_out.at[pl.ds((c * 7 + ih - 1) * BLOCK + first, count)],
                slots_in.at[pl.ds((c * 8 + ih) * BLOCK + first, count)],
                slot_send, recv.at[c], device({AXES[c % 3][1]: ih // 2}, ih % 2),
            )

    for c in range(UNITS):
        pack(c)

    def inflow(base, count, all_ref, width):
        columns = []
        for w in range(width // LANES):
            direct, through = [], []
            for i in range(count):
                value = all_ref[i, :, pl.ds(w * LANES, LANES)]
                direct.append(coef[base + i] * value)
                through.append(coef[base + count + i] * value)
            while len(direct) > 1:
                direct = [a + b for a, b in zip(direct[::2], direct[1::2])]
                through = [a + b for a, b in zip(through[::2], through[1::2])]
            columns.append(direct[0] + pltpu.roll(through[0], planes, 0))
        return columns[0] if len(columns) == 1 else jnp.concatenate(columns, axis=1)

    wide = 8 * GROUP
    out_lane = iota((1, wide), 1)
    sender = jnp.zeros((1, wide), jnp.int32)
    for m in range(1, 8):
        sender += (out_lane >= m * GROUP).astype(jnp.int32)
    within = out_lane - sender * GROUP
    in_lane = iota((LANES, wide), 0)
    sender_row = iota((8, wide), 0) == sender
    tile_index = iota((LANES, wide), 0).astype(F32)
    selects = []
    for g in range(3):
        whole(labels_in, g * 8 + 1, 7, label_recv.at[g])
        lines = labels_in[pl.ds(g * 8, 8)].reshape(8, LANES).astype(BF16)
        row_of = []
        for j in range(4):
            choose = in_lane == within + j * GROUP
            named = dot(lines, choose.astype(BF16))
            named = jnp.sum(jnp.where(sender_row, named, 0.0), axis=0, keepdims=True)
            row_of.append((tile_index == named).astype(BF16))
        selects.append(row_of)

    def collect(c, j):
        rows = jnp.concatenate(
            [slots_in[pl.ds((c * 8 + ih) * BLOCK + j * GROUP, GROUP), :] for ih in range(8)],
            axis=0,
        )
        value = dot(selects[c % 3][j], jnp.concatenate(split2(rows), axis=1))
        return value[:, :LANES] + value[:, LANES:]

    def partial_row(c, s):
        return (c * 2 + s) * LANES

    sides = ((0, 1), (1, 3))

    def send_partial(c, s, move, r):
        at = pl.ds(partial_row(c, s) + r * half, half)
        remote(
            partial_out.at[at], partial_in.at[at],
            partial_send, partial_recv.at[c], device({AXES[c % 3][2]: move}, 0),
        )

    for c in range(UNITS):
        whole(slots_in, (c * 8 + 1) * BLOCK, 7 * (BLOCK - GROUP), slot_recv.at[c])
        far_out[pl.ds(c * LANES, LANES), :] = collect(c, 2)
        for s, move in sides:
            at = pl.ds(c * LANES + s * half, half)
            remote(
                far_out.at[at], far_in.at[at],
                far_send, far_recv.at[c], device({AXES[c % 3][2]: move}, 0),
            )
        for s, move in sides:
            partial_out[pl.ds(partial_row(c, s), LANES), :] = collect(c, move)
            send_partial(c, s, move, 1 - s)
        send_slots(c, 0, GROUP, own_recv)
    for c in range(UNITS):
        whole(far_in, c * LANES, LANES, far_recv.at[c])
        for s, move in sides:
            at = pl.ds(partial_row(c, s) + s * half, half)
            partial_out[at, :] = (
                partial_out[at, :] + far_in[pl.ds(c * LANES + s * half, half), :]
            )
            send_partial(c, s, move, s)
    for c in range(UNITS):
        whole(slots_in, (c * 8 + 1) * BLOCK, 7 * GROUP, own_recv.at[c])
        own_sum[pl.ds(c * LANES, LANES), :] = collect(c, 0)
    for c in range(UNITS):
        whole(partial_in, partial_row(c, 0), 2 * LANES, partial_recv.at[c])
        regroup[pl.ds(c, LANES, stride=PITCH), :] = (
            own_sum[pl.ds(c * LANES, LANES), :]
            + partial_in[pl.ds(partial_row(c, 0), LANES), :]
            + partial_in[pl.ds(partial_row(c, 1), LANES), :]
        )
    loads[6].wait()
    for xo in range(tile_rows):
        parts = [
            regroup[pl.ds((xo * tile_cols + yo) * PITCH, UNITS), :] for yo in range(tile_cols)
        ]
        for g, value in enumerate(block_transpose(parts)):
            pushed_ref[g // 2, pl.ds(xo * TS + (g % 2) * 8, 8), :] = value

    ends = jnp.zeros((8, cy), F32)
    for z in range(planes):
        both = jnp.concatenate(split2(target[z] - pushed_ref[z]), axis=1)
        halves[z] = both
        value = dot(xends_tab[z], both)
        ends += value[:8, :cy] + (value[:8, cy:] + value[8:, :cy])
    xmsg[...] = ends
    for s in range(4):
        for h in range(2):
            if s + h:
                remote(xmsg, xall.at[p], x_send, x_recv, device({1: s}, h))
    xall[p] = ends
    y_ends = jnp.zeros((8, cx), F32)
    for z in range(planes):
        both = halves[z]
        value = dot(xtab_hi[z], both)
        value = value[:, :cy] + (value[:, cy:] + dot(xtab_lo[z], both[:, :cy]))
        smooth[z] = value
        value = dot(yends_tab[z], jnp.concatenate(split2(value), axis=0), ((1,), (1,)))
        y_ends += value[:8, :cx] + (value[:8, cx:] + value[8:, :cx])
    whole(xall, 0, n_gx - 1, x_recv)
    flow = inflow(0, n_gx, xall, cy)
    at_last = jnp.sum(flow * last_rows, axis=1, keepdims=True)
    at_first = jnp.sum(flow * first_rows, axis=1, keepdims=True)
    entered = jnp.where(upper, at_last, pltpu.roll(jnp.broadcast_to(at_first, (8, LANES)), 4, 0)[:, 0:1])
    left = jnp.where(upper, pltpu.roll(jnp.broadcast_to(at_last, (8, LANES)), 4, 0)[:, 0:1], at_first)
    y_ends += edge_rows[0] * entered + edge_rows[1] * left
    ymsg[...] = y_ends
    for dz in range(4):
        for dx in range(4):
            if dz + dx:
                remote(ymsg, yall.at[q], y_send, y_recv, device({2: dz, 0: dx}, 0))
    yall[q] = y_ends

    loads[7].wait()
    for z in range(planes):
        value = smooth[z] + (
            xfill[z] * flow[z : z + 1] + xfill[planes + z] * flow[planes + z : planes + z + 1]
        )
        potential[z] = potential[z] + dot3(split2(value), (ytab_hi[z], ytab_lo[z]))
    whole(yall, 0, n_gy - 1, y_recv)
    flow = inflow(2 * n_gx, n_gy, yall, cx)
    hi = flow.astype(BF16).astype(F32)
    flow = jnp.concatenate([hi, flow - hi, hi, flow - hi], axis=0).astype(BF16)
    for z in range(planes):
        next_ref[z] = potential[z] + dot(flow, yfill_tab[z], ((0,), (0,)))

    whole(metas, 0, 9, meta_send)
    whole(spread_in, 0, 3 * UNITS * LANES, spread_send)
    whole(slots_out, 0, 7 * UNITS * BLOCK, slot_send)
    whole(labels_out, 0, 21, label_send)
    whole(far_out, 0, UNITS * LANES, far_send)
    whole(partial_out, 0, 2 * UNITS * LANES, partial_send)
    whole(xall, 0, n_gx - 1, x_send)
    whole(yall, 0, n_gy - 1, y_send)


def store(pushed_ref, next_ref, pushed_out, next_out, sems):
    copies = [
        pltpu.make_async_copy(pushed_ref, pushed_out, sems.at[0]),
        pltpu.make_async_copy(next_ref, next_out, sems.at[1]),
    ]
    for copy in copies:
        copy.start()
    for copy in copies:
        copy.wait()


def per_device(source_mass, target_density, potential, dest_device, dest_tile, mass_counts, reach):
    planes, cx, cy = source_mass.shape

    def lanes(a):
        return jnp.swapaxes(a.reshape(a.shape[2:]), 0, 1)

    hbm = pl.BlockSpec(memory_space=pl.ANY)
    dma = pltpu.SemaphoreType.DMA
    vmem = pltpu.VMEM
    grid = jax.ShapeDtypeStruct((planes, cx, cy), F32)
    field = vmem((planes, cx, cy), F32)

    def rows(count):
        return vmem((count, LANES), F32)

    fields = pl.pallas_call(
        kernel,
        out_shape=(grid, grid),
        in_specs=[hbm] * 7,
        out_specs=(pl.BlockSpec(memory_space=vmem), pl.BlockSpec(memory_space=vmem)),
        scratch_shapes=[
            field, field, field, field,
            pltpu.SMEM((planes,), F32),
            vmem((3, 4, LANES), jnp.int32),
            vmem((9, 3, 4, LANES), jnp.int32),
            rows(UNITS * LANES), rows(LANES * PITCH + 16), rows(3 * UNITS * LANES),
            vmem((12, 256, LANES), BF16),
            vmem((12, 256, LANES), F32),
            vmem((3, 8 * LANES, LANES), F32),
            rows(7 * UNITS * BLOCK + 8), rows(8 * UNITS * BLOCK + 8),
            vmem((24, 1, LANES), F32),
            vmem((24, 1, LANES), F32),
            rows(UNITS * LANES), rows(UNITS * LANES),
            rows(2 * UNITS * LANES), rows(2 * UNITS * LANES), rows(UNITS * LANES),
            vmem((planes, cx, cx), BF16),
            vmem((planes, cx, cx), BF16),
            vmem((planes, cy, cy), BF16),
            vmem((planes, cy, cy), BF16),
            vmem((planes, 16, cx), BF16),
            vmem((planes, 16, cy), BF16),
            vmem((2 * planes, cx, LANES), F32),
            vmem((planes, 32, cy), BF16),
            vmem((48, 8, LANES), F32),
            vmem((2, 8, cx), F32),
            vmem((planes, cx, 2 * cy), BF16),
            vmem((8, cy), F32),
            vmem((8, 8, cy), F32),
            vmem((8, cx), F32),
            vmem((16, 8, cx), F32),
            dma((8,)), dma, dma((3,)), dma, dma((UNITS,)),
            dma, dma((UNITS,)), dma((UNITS,)), dma, dma((3,)), dma, dma((UNITS,)),
            dma, dma((UNITS,)),
            dma, dma, dma, dma,
        ],
        compiler_params=pltpu.CompilerParams(collective_id=0, has_side_effects=True, vmem_limit_bytes=40 * 1024 * 1024),
        name="dual_step",
    )(
        *[
            pltpu.with_memory_space_constraint(a, pltpu.HBM)
            for a in (
                source_mass, target_density, potential,
                lanes(dest_device), lanes(dest_tile), lanes(mass_counts), reach,
            )
        ],
    )

    local = pl.BlockSpec(memory_space=vmem)
    return pl.pallas_call(
        store,
        out_shape=(grid, grid),
        in_specs=[local, local],
        out_specs=(hbm, hbm),
        scratch_shapes=[dma((2,))],
        compiler_params=pltpu.CompilerParams(vmem_limit_bytes=4 * 1024 * 1024),
        name="store",
    )(*fields)


def solution(mesh):
    in_specs = (
        P(None, "gx", "gy"),
        P(None, "gx", "gy"),
        P(None, "gx", "gy"),
        P("gx", "gy", None, None),
        P("gx", "gy", None, None),
        P("gx", "gy", None, None),
        P(),
    )
    out_specs = (P(None, "gx", "gy"), P(None, "gx", "gy"))
    return jax.shard_map(
        per_device, mesh=mesh, in_specs=in_specs, out_specs=out_specs, check_vma=False
    )
```

```python
import jax
import jax.numpy as jnp
from jax import lax
from jax.experimental import pallas as pl
from jax.experimental.pallas import tpu as pltpu
from jax.sharding import PartitionSpec as P

MESH = pl.DeviceIdType.MESH
TS = 16
SLOTS = 6
LANES = 128
UNITS = 8
AXES = ((0, 1, 2), (1, 2, 0), (2, 0, 1))
GROUP = SLOTS * 4
BLOCK = 4 * GROUP
EARLY = 5
PITCH = 9
F32 = jnp.float32
BF16 = jnp.bfloat16


def split2(a):
    hi = a.astype(BF16)
    return hi, (a - hi.astype(F32)).astype(BF16)


def split3(a):
    hi = a.astype(BF16)
    rest = a - hi.astype(F32)
    mid = rest.astype(BF16)
    return hi, mid, (rest - mid.astype(F32)).astype(BF16)


def dot(a, b, dims=((1,), (0,))):
    return lax.dot_general(a, b, (dims, ((), ())), preferred_element_type=F32)


def dot3(a, b, dims=((1,), (0,))):
    ah, al = a
    bh, bl = b
    return dot(ah, bh, dims) + (dot(ah, bl, dims) + dot(al, bh, dims))


def dot_f32(a, b, dims=((1,), (0,))):
    return lax.dot_general(
        a, b, (dims, ((), ())), precision=lax.Precision.HIGHEST, preferred_element_type=F32
    )


def iota(shape, axis):
    return lax.broadcasted_iota(jnp.int32, shape, axis)


def block_transpose(vectors):
    lane_block = iota((8, LANES), 1) // TS
    vectors = list(vectors)
    for bit in (4, 2, 1):
        low = (lane_block & bit) == 0
        result = [None] * 8
        for a in range(8):
            if a & bit:
                continue
            b = a | bit
            up, down = vectors[a], vectors[b]
            result[a] = jnp.where(low, up, pltpu.roll(down, bit * TS, 1))
            result[b] = jnp.where(low, pltpu.roll(up, LANES - bit * TS, 1), down)
        vectors = result
    return vectors


def powers(logs, exponent):
    return jnp.exp(exponent.astype(F32) * logs)


def whole(ref, first, count, sem):
    part = ref.at[pl.ds(first, count)]
    pltpu.make_async_copy(part, part, sem).wait()


def kernel(
    source_ref, target_ref, potential_ref, device_ref, tile_ref, count_ref, reach_hbm,
    pushed_ref, next_ref,
    natural, target, potential, smooth, reach_ref,
    meta, metas, tiles, regroup, spread_in, picks, weights, places,
    slots_out, slots_in, labels_out, labels_in,
    far_out, far_in, partial_out, partial_in, own_sum,
    xtab_hi, xtab_lo, ytab_hi, ytab_lo, xends_tab, yends_tab, xfill, yfill_tab,
    coef, edge_rows, column_tab, halves, xmsg, xall, ymsg, yall,
    load_sem, meta_send, meta_recv, spread_send, spread_recv,
    slot_send, slot_recv, own_recv, label_send, label_recv, far_send, far_recv,
    partial_send, partial_recv, x_send, x_recv, y_send, y_recv,
):
    p, q = lax.axis_index("gx"), lax.axis_index("gy")
    n_gx, n_gy = 8, 16
    planes, cx, cy = source_ref.shape
    tile_rows, tile_cols = cx // TS, cy // TS
    half = LANES // 2
    here = (q & 3, p >> 1, q >> 2)
    core = p & 1
    stride = (1, 2 * n_gy, 4)

    def device(moves, other):
        x, y, z = [(here[axis] + moves.get(axis, 0)) & 3 for axis in range(3)]
        return y * 2 + (core ^ other), z * 4 + x

    def remote(src, dst, send, recv, to):
        pltpu.make_async_remote_copy(
            src_ref=src, dst_ref=dst, send_sem=send, recv_sem=recv,
            device_id=to, device_id_type=MESH,
        ).start()

    split = [pl.ds(r * (cx // 2), cx // 2) for r in range(2)]
    loads = [
        pltpu.make_async_copy(a, b, load_sem.at[i])
        for i, (a, b) in enumerate([
            (source_ref.at[:, split[0]], natural.at[:, split[0]]),
            (source_ref.at[:, split[1]], natural.at[:, split[1]]),
            (device_ref, meta.at[0]), (tile_ref, meta.at[1]), (count_ref, meta.at[2]),
            (reach_hbm, reach_ref), (target_ref, target), (potential_ref, potential),
        ])
    ]
    for load in loads:
        load.start()

    barrier = pltpu.get_barrier_semaphore()
    peers = [({axis: s}, h) for axis in range(3) for s in range(1, 4) for h in range(2)]
    peers.append(({}, 1))
    for moves, other in peers:
        pl.semaphore_signal(
            barrier, inc=1, device_id=device(moves, other), device_id_type=MESH
        )

    for xo in range(tile_rows):
        if xo % (tile_rows // 2) == 0:
            loads[xo // (tile_rows // 2)].wait()
        parts = [
            natural[g // 2, pl.ds(xo * TS + (g % 2) * 8, 8), :] for g in range(2 * planes)
        ]
        for yo, value in enumerate(block_transpose(parts)):
            regroup[pl.ds((xo * tile_cols + yo) * PITCH, UNITS), :] = value
    for load in loads[2:5]:
        load.wait()
    pl.semaphore_wait(barrier, len(peers))
    for g, (a, _, _) in enumerate(AXES):
        for s in range(1, 4):
            remote(meta, metas.at[g * 3 + s - 1], meta_send, meta_recv.at[g], device({a: s}, 0))
    for c in range(UNITS):
        tiles[pl.ds(c * LANES, LANES), :] = regroup[pl.ds(c, LANES, stride=PITCH), :]
        for s in (2, 1, 3):
            remote(
                tiles.at[pl.ds(c * LANES, LANES)],
                spread_in.at[pl.ds((c * 3 + s - 1) * LANES, LANES)],
                spread_send, spread_recv.at[c], device({AXES[c % 3][0]: s}, 0),
            )

    loads[5].wait()
    decay = [jnp.full((1, 1), 1.0 - 1.0 / reach_ref[z], F32) for z in range(planes)]
    logs = [jnp.log(d) for d in decay]
    scale = [(1.0 - d) ** 2 for d in decay]
    row8 = iota((8, 1), 0)

    def both_rows(values):
        result = jnp.zeros((8, values[0].shape[1]), F32)
        for z, v in enumerate(values):
            result = jnp.where((row8 == z) | (row8 == planes + z), v, result)
        return result

    def stacked(a):
        hi = a.astype(BF16).astype(F32)
        return jnp.concatenate([hi, a - hi], axis=0).astype(BF16)

    logs8, scale8 = both_rows(logs), both_rows(scale)

    def rows_of(n):
        at = iota((8, n), 1)
        squares = powers(2.0 * logs8, at)
        hi = squares.astype(BF16).astype(F32)
        mid = (squares - hi).astype(BF16).astype(F32)
        parts = jnp.concatenate([hi, mid, squares - hi - mid, jnp.zeros_like(hi)], axis=0)
        inside = (iota((n, n), 0) + iota((n, n), 1) < n).astype(BF16)
        sums = dot(parts.astype(BF16), inside)
        sums = sums[0:8] + (sums[8:16] + sums[16:24])
        last = powers(logs8, n - 1 - at)
        fall = powers(logs8, n - at)
        first = scale8 * powers(logs8, at) * sums
        swept = scale8 * powers(logs8, at + 1) * sums
        return sums, last, first, swept, fall

    upper = row8 < planes
    sums_x, last_x, first_x, swept_x, fall_x = rows_of(cx)
    sums_y, last_rows, first_rows, swept_y, fall_y = rows_of(cy)
    edge_rows[0], edge_rows[1] = swept_x, fall_x
    spare = jnp.zeros((cy - 32, cx), F32)
    column_tab[...] = jnp.transpose(
        jnp.concatenate(
            [sums_x, jnp.where(upper, swept_x, fall_x),
             jnp.concatenate([sums_y, sums_y], axis=1),
             jnp.where(upper, last_x, first_x), spare],
            axis=0,
        )
    )
    columns = column_tab[...]
    across_row = iota((cy, cy), 0)
    gap = across_row - iota((cy, cy), 1)
    for z in range(planes):
        near = powers(logs[z], jnp.abs(gap)) * scale[z]
        below = powers(logs[z], gap + cy) * scale[z]
        above = powers(logs[z], cy - gap) * scale[z]

        def column(i, first, count):
            return jnp.broadcast_to(columns[first : first + count, i : i + 1], (count, cy))

        low = gap >= 0
        g0, g1, gy = column(z, 0, cy), column(z, cy, cy), column(16 + z, 0, cy)
        r0, r1, ry = sums_x[z : z + 1, :cy], sums_x[z : z + 1, cy:], sums_y[z : z + 1]
        for r, (left_part, right_part) in enumerate([
            (near * jnp.where(low, g0, r0), above * r1),
            (below * g1, near * jnp.where(low, g1, r1)),
        ]):
            at = pl.ds(r * cy, cy)
            for w, part in enumerate((left_part, right_part)):
                hi, lo = split2(part)
                xtab_hi[z, at, pl.ds(w * cy, cy)] = hi
                xtab_lo[z, at, pl.ds(w * cy, cy)] = lo
        ytab_hi[z], ytab_lo[z] = split2(near * jnp.where(low, gy, ry))
        xfill[z] = jnp.broadcast_to(columns[:, 8 + z : 9 + z], (cx, LANES))
        xfill[planes + z] = jnp.broadcast_to(
            columns[:, 8 + planes + z : 9 + planes + z], (cx, LANES)
        )
        one, two = row8 == z, row8 == planes + z
        xends_tab[z] = stacked(jnp.where(one, last_x, 0.0) + jnp.where(two, first_x, 0.0))
        yends_tab[z] = stacked(jnp.where(one, last_rows, 0.0) + jnp.where(two, first_rows, 0.0))
        fill = jnp.where(one, swept_y, 0.0) + jnp.where(two, fall_y, 0.0)
        hi = fill.astype(BF16).astype(F32)
        yfill_tab[z] = jnp.concatenate([hi, hi, fill - hi, fill - hi], axis=0).astype(BF16)

    def coefficients(base, count, at, n, first):
        across = jnp.exp(float(n) * logs8)
        powers_of = [jnp.ones((8, 1), F32)]
        for _ in range(count - 1):
            powers_of.append(powers_of[-1] * across)
        low = row8 < planes
        before, after = [], []
        for i in range(count):
            coming = jnp.zeros((8, 1), F32)
            going = jnp.zeros((8, 1), F32)
            for m in range(count - 1):
                coming = jnp.where(at - 1 - i == m, powers_of[m], coming)
                going = jnp.where(i - at - 1 == m, powers_of[m], going)
            before.append(coming)
            after.append(going)
        through = jnp.zeros((8, 1), F32)
        crossing = [None] * count
        for i in reversed(range(count)):
            crossing[i] = first * through
            through = after[i] + across * through
        for i in range(count):
            coef[base + i] = jnp.broadcast_to(jnp.where(low, before[i], after[i]), (8, LANES))
            coef[base + count + i] = jnp.broadcast_to(
                jnp.where(low, crossing[i], 0.0), (8, LANES)
            )

    coefficients(0, n_gx, p, cx, swept_x[:, 0:1])
    coefficients(2 * n_gx, n_gy, q, cy, swept_y[:, 0:1])

    earlier = (iota((LANES, LANES), 0) < iota((LANES, LANES), 1)).astype(BF16)
    row = iota((32, LANES), 0)
    row_target, row_j = row >> 2, row & 3
    order = iota((8, LANES), 0).astype(F32)

    def find_slots(g, s, info):
        a, b, e = AXES[g]
        names, spots, counts = info[0], info[1].astype(F32), info[2].astype(F32)
        shares = counts / jnp.sum(counts, axis=0, keepdims=True)
        number = (
            here[a] * stride[a] + ((here[b] + (row_target >> 1)) & 3) * stride[b]
            + (core ^ (row_target & 1)) * n_gy + ((here[e] + row_j) & 3) * stride[e]
        )
        share = jnp.zeros((32, LANES), F32)
        spot = jnp.zeros((32, LANES), F32)
        for f in range(4):
            match = number == names[f : f + 1, :]
            share = jnp.where(match, shares[f : f + 1, :], share)
            spot = jnp.where(match, spots[f : f + 1, :], spot)
        named = share > 0.0
        rank = dot(jnp.where(named, 1.0, 0.0).astype(BF16), earlier)
        rank = jnp.where(named, rank, -1.0)
        found = []
        for r in range(32):
            mine = rank[r : r + 1, :] == order
            found.append(jnp.where(mine, 1.0, 0.0))
            part = jnp.where(mine, share[r : r + 1, :], 0.0)
            weights[g * 4 + s, pl.ds(r * 8, 8), :] = jnp.broadcast_to(
                jnp.sum(part, axis=1, keepdims=True), (8, LANES)
            )
            places[g, pl.ds((r // 4) * LANES + (r % 4) * GROUP + s * SLOTS, SLOTS), :] = (
                jnp.where(mine, spot[r : r + 1, :], 0.0)[:SLOTS]
            )
        picks[g * 4 + s] = jnp.concatenate(found, axis=0).astype(BF16)

    def find_labels(g):
        b = AXES[g][1]
        for ih in range(8):
            places[g, pl.ds(ih * LANES + BLOCK, LANES - BLOCK), :] = jnp.zeros(
                (LANES - BLOCK, LANES), F32
            )
        found = dot(jnp.ones((8, LANES), BF16), places[g].astype(BF16), ((1,), (1,)))
        for ih in range(8):
            line = found[0:1, ih * LANES : (ih + 1) * LANES]
            if ih == 0:
                labels_in[g * 8] = line
            else:
                labels_out[g * 8 + ih - 1] = line
        for ih in range(1, 8):
            remote(
                labels_out.at[g * 8 + ih - 1], labels_in.at[g * 8 + ih],
                label_send, label_recv.at[g], device({b: ih // 2}, ih % 2),
            )

    for g in range(3):
        find_slots(g, 0, meta[...])
    for g in range(3):
        whole(metas, g * 3, 3, meta_recv.at[g])
        for s in range(1, 4):
            find_slots(g, s, metas[g * 3 + s - 1])
        find_labels(g)

    def pack(c):
        g = c % 3
        for s in range(4):
            if s == 1:
                whole(spread_in, c * 3 * LANES, 3 * LANES, spread_recv.at[c])
            if s == 0:
                value = tiles[pl.ds(c * LANES, LANES), :]
            else:
                value = spread_in[pl.ds((c * 3 + s - 1) * LANES, LANES), :]
            pick = picks[g * 4 + s]
            value = dot(
                jnp.concatenate([pick, pick], axis=1), jnp.concatenate(split2(value), axis=0)
            )
            value = value * weights[g * 4 + s]
            for r in range(32):
                ih, j = r // 4, r % 4
                piece = value[r * 8 : r * 8 + SLOTS]
                within = j * GROUP + s * SLOTS
                if ih == 0:
                    slots_in[pl.ds(c * 8 * BLOCK + within, SLOTS), :] = piece
                else:
                    slots_out[pl.ds((c * 7 + ih - 1) * BLOCK + within, SLOTS), :] = piece
        send_slots(c, GROUP, BLOCK - GROUP, slot_recv)

    def send_slots(c, first, count, recv):
        for ih in range(1, 8):
            remote(
                slots_out.at[pl.ds((c * 7 + ih - 1) * BLOCK + first, count)],
                slots_in.at[pl.ds((c * 8 + ih) * BLOCK + first, count)],
                slot_send, recv.at[c], device({AXES[c % 3][1]: ih // 2}, ih % 2),
            )

    for c in range(UNITS):
        pack(c)

    def inflow(base, count, all_ref, width):
        columns = []
        for w in range(width // LANES):
            direct, through = [], []
            for i in range(count):
                value = all_ref[i, :, pl.ds(w * LANES, LANES)]
                direct.append(coef[base + i] * value)
                through.append(coef[base + count + i] * value)
            while len(direct) > 1:
                direct = [a + b for a, b in zip(direct[::2], direct[1::2])]
                through = [a + b for a, b in zip(through[::2], through[1::2])]
            columns.append(direct[0] + pltpu.roll(through[0], planes, 0))
        return columns[0] if len(columns) == 1 else jnp.concatenate(columns, axis=1)

    wide = 8 * GROUP
    out_lane = iota((1, wide), 1)
    sender = jnp.zeros((1, wide), jnp.int32)
    for m in range(1, 8):
        sender += (out_lane >= m * GROUP).astype(jnp.int32)
    within = out_lane - sender * GROUP
    in_lane = iota((LANES, wide), 0)
    sender_row = iota((8, wide), 0) == sender
    tile_index = iota((LANES, wide), 0).astype(F32)
    selects = []
    for g in range(3):
        whole(labels_in, g * 8 + 1, 7, label_recv.at[g])
        lines = labels_in[pl.ds(g * 8, 8)].reshape(8, LANES).astype(BF16)
        row_of = []
        for j in range(4):
            choose = in_lane == within + j * GROUP
            named = dot(lines, choose.astype(BF16))
            named = jnp.sum(jnp.where(sender_row, named, 0.0), axis=0, keepdims=True)
            row_of.append((tile_index == named).astype(BF16))
        selects.append(row_of)

    part_lane = iota((LANES, LANES), 1)
    source_lane = iota((LANES, LANES), 0)
    unit_row = iota((LANES, cx), 0)
    cell = iota((LANES, cx), 1)
    unit_weights = []
    for first in (24, 24 + planes):
        expand = (source_lane == first + (part_lane >> 5)).astype(BF16)
        values = sum(dot(part, expand) for part in split3(column_tab[...]))
        values = split3(values)
        rows = []
        for h in range(2):
            pick = (cell == (unit_row & 15) * TS + h * 8 + (unit_row >> 4)).astype(BF16)
            rows.append(sum(dot(pick, part) for part in values))
        unit_weights.append(jnp.where((part_lane & TS) == 0, rows[0], rows[1]))
    loads[6].wait()
    ends = jnp.zeros((8, cy), F32)
    for z in range(planes):
        value = dot(xends_tab[z], jnp.concatenate(split2(target[z]), axis=1))
        ends += value[:8, :cy] + (value[:8, cy:] + value[8:, :cy])
    unit_ends = [jnp.zeros((8, LANES), F32), jnp.zeros((8, LANES), F32)]

    def collect(c, j):
        rows = jnp.concatenate(
            [slots_in[pl.ds((c * 8 + ih) * BLOCK + j * GROUP, GROUP), :] for ih in range(8)],
            axis=0,
        )
        value = dot(selects[c % 3][j], jnp.concatenate(split2(rows), axis=1))
        return value[:, :LANES] + value[:, LANES:]

    def partial_row(c, s):
        return (c * 2 + s) * LANES

    sides = ((0, 1), (1, 3))

    def send_partial(c, s, move, r):
        at = pl.ds(partial_row(c, s) + r * half, half)
        remote(
            partial_out.at[at], partial_in.at[at],
            partial_send, partial_recv.at[c], device({AXES[c % 3][2]: move}, 0),
        )

    for c in range(UNITS):
        whole(slots_in, (c * 8 + 1) * BLOCK, 7 * (BLOCK - GROUP), slot_recv.at[c])
        far_out[pl.ds(c * LANES, LANES), :] = collect(c, 2)
        for s, move in sides:
            at = pl.ds(c * LANES + s * half, half)
            remote(
                far_out.at[at], far_in.at[at],
                far_send, far_recv.at[c], device({AXES[c % 3][2]: move}, 0),
            )
        for s, move in sides:
            partial_out[pl.ds(partial_row(c, s), LANES), :] = collect(c, move)
            send_partial(c, s, move, 1 - s)
        if c < EARLY:
            send_slots(c, 0, GROUP, own_recv)
    for c in range(UNITS):
        if c == EARLY:
            for last in range(EARLY, UNITS):
                send_slots(last, 0, GROUP, own_recv)
        whole(far_in, c * LANES, LANES, far_recv.at[c])
        for s, move in sides:
            at = pl.ds(partial_row(c, s) + s * half, half)
            partial_out[at, :] = (
                partial_out[at, :] + far_in[pl.ds(c * LANES + s * half, half), :]
            )
            send_partial(c, s, move, s)
    for c in range(UNITS):
        whole(slots_in, (c * 8 + 1) * BLOCK, 7 * GROUP, own_recv.at[c])
        own_sum[pl.ds(c * LANES, LANES), :] = collect(c, 0)
    for c in range(UNITS):
        whole(partial_in, partial_row(c, 0), 2 * LANES, partial_recv.at[c])
        total = (
            own_sum[pl.ds(c * LANES, LANES), :]
            + partial_in[pl.ds(partial_row(c, 0), LANES), :]
            + partial_in[pl.ds(partial_row(c, 1), LANES), :]
        )
        for i in range(2):
            terms = [
                total[xo * 8 : (xo + 1) * 8] * unit_weights[i][c * 16 + xo : c * 16 + xo + 1]
                for xo in range(tile_rows)
            ]
            while len(terms) > 1:
                terms = [a + b for a, b in zip(terms[::2], terms[1::2])]
            unit_ends[i] = unit_ends[i] + terms[0]
        regroup[pl.ds(c, LANES, stride=PITCH), :] = total

    lane = iota((8, LANES), 1)
    last, first = [a + pltpu.roll(a, LANES - TS, 1) for a in unit_ends]
    block = lane >> 4 == iota((8, LANES), 0)
    for i, value in enumerate((last, first)):
        for z in range(planes):
            moved = pltpu.roll(value, (LANES - 2 * TS * z) % LANES, 1) if z else value
            moved = pltpu.roll(moved, 0, 1, stride=TS, stride_axis=0)
            moved = jnp.sum(jnp.where(block, moved, 0.0), axis=0, keepdims=True)
            ends -= jnp.where(row8 == i * planes + z, moved, 0.0)
    xmsg[...] = ends
    for s in range(4):
        for h in range(2):
            if s + h:
                remote(xmsg, xall.at[p], x_send, x_recv, device({1: s}, h))
    xall[p] = ends
    for xo in range(tile_rows):
        parts = [
            regroup[pl.ds((xo * tile_cols + yo) * PITCH, UNITS), :] for yo in range(tile_cols)
        ]
        for g, value in enumerate(block_transpose(parts)):
            pushed_ref[g // 2, pl.ds(xo * TS + (g % 2) * 8, 8), :] = value
    for z in range(planes):
        halves[z] = jnp.concatenate(split2(target[z] - pushed_ref[z]), axis=1)
    y_ends = jnp.zeros((8, cx), F32)
    for z in range(planes):
        both = halves[z]
        value = dot(xtab_hi[z], both)
        value = value[:, :cy] + (value[:, cy:] + dot(xtab_lo[z], both[:, :cy]))
        smooth[z] = value
        value = dot(yends_tab[z], jnp.concatenate(split2(value), axis=0), ((1,), (1,)))
        y_ends += value[:8, :cx] + (value[:8, cx:] + value[8:, :cx])
    whole(xall, 0, n_gx - 1, x_recv)
    flow = inflow(0, n_gx, xall, cy)
    at_last = jnp.sum(flow * last_rows, axis=1, keepdims=True)
    at_first = jnp.sum(flow * first_rows, axis=1, keepdims=True)
    entered = jnp.where(upper, at_last, pltpu.roll(jnp.broadcast_to(at_first, (8, LANES)), 4, 0)[:, 0:1])
    left = jnp.where(upper, pltpu.roll(jnp.broadcast_to(at_last, (8, LANES)), 4, 0)[:, 0:1], at_first)
    y_ends += edge_rows[0] * entered + edge_rows[1] * left
    ymsg[...] = y_ends
    for dz in range(4):
        for dx in range(4):
            if dz + dx:
                remote(ymsg, yall.at[q], y_send, y_recv, device({2: dz, 0: dx}, 0))
    yall[q] = y_ends

    loads[7].wait()
    for z in range(planes):
        value = smooth[z] + (
            xfill[z] * flow[z : z + 1] + xfill[planes + z] * flow[planes + z : planes + z + 1]
        )
        potential[z] = potential[z] + dot3(split2(value), (ytab_hi[z], ytab_lo[z]))
    whole(yall, 0, n_gy - 1, y_recv)
    flow = inflow(2 * n_gx, n_gy, yall, cx)
    hi = flow.astype(BF16).astype(F32)
    flow = jnp.concatenate([hi, flow - hi, hi, flow - hi], axis=0).astype(BF16)
    for z in range(planes):
        next_ref[z] = potential[z] + dot(flow, yfill_tab[z], ((0,), (0,)))

    whole(metas, 0, 9, meta_send)
    whole(spread_in, 0, 3 * UNITS * LANES, spread_send)
    whole(slots_out, 0, 7 * UNITS * BLOCK, slot_send)
    whole(labels_out, 0, 21, label_send)
    whole(far_out, 0, UNITS * LANES, far_send)
    whole(partial_out, 0, 2 * UNITS * LANES, partial_send)
    whole(xall, 0, n_gx - 1, x_send)
    whole(yall, 0, n_gy - 1, y_send)


def store(pushed_ref, next_ref, pushed_out, next_out, sems):
    copies = [
        pltpu.make_async_copy(pushed_ref, pushed_out, sems.at[0]),
        pltpu.make_async_copy(next_ref, next_out, sems.at[1]),
    ]
    for copy in copies:
        copy.start()
    for copy in copies:
        copy.wait()


def per_device(source_mass, target_density, potential, dest_device, dest_tile, mass_counts, reach):
    planes, cx, cy = source_mass.shape

    def lanes(a):
        return jnp.swapaxes(a.reshape(a.shape[2:]), 0, 1)

    hbm = pl.BlockSpec(memory_space=pl.ANY)
    dma = pltpu.SemaphoreType.DMA
    vmem = pltpu.VMEM
    grid = jax.ShapeDtypeStruct((planes, cx, cy), F32)
    field = vmem((planes, cx, cy), F32)

    def rows(count):
        return vmem((count, LANES), F32)

    fields = pl.pallas_call(
        kernel,
        out_shape=(grid, grid),
        in_specs=[hbm] * 7,
        out_specs=(pl.BlockSpec(memory_space=vmem), pl.BlockSpec(memory_space=vmem)),
        scratch_shapes=[
            field, field, field, field,
            pltpu.SMEM((planes,), F32),
            vmem((3, 4, LANES), jnp.int32),
            vmem((9, 3, 4, LANES), jnp.int32),
            rows(UNITS * LANES), rows(LANES * PITCH + 16), rows(3 * UNITS * LANES),
            vmem((12, 256, LANES), BF16),
            vmem((12, 256, LANES), F32),
            vmem((3, 8 * LANES, LANES), F32),
            rows(7 * UNITS * BLOCK + 8), rows(8 * UNITS * BLOCK + 8),
            vmem((24, 1, LANES), F32),
            vmem((24, 1, LANES), F32),
            rows(UNITS * LANES), rows(UNITS * LANES),
            rows(2 * UNITS * LANES), rows(2 * UNITS * LANES), rows(UNITS * LANES),
            vmem((planes, cx, cx), BF16),
            vmem((planes, cx, cx), BF16),
            vmem((planes, cy, cy), BF16),
            vmem((planes, cy, cy), BF16),
            vmem((planes, 16, cx), BF16),
            vmem((planes, 16, cy), BF16),
            vmem((2 * planes, cx, LANES), F32),
            vmem((planes, 32, cy), BF16),
            vmem((48, 8, LANES), F32),
            vmem((2, 8, cx), F32),
            vmem((cx, LANES), F32),
            vmem((planes, cx, 2 * cy), BF16),
            vmem((8, cy), F32),
            vmem((8, 8, cy), F32),
            vmem((8, cx), F32),
            vmem((16, 8, cx), F32),
            dma((8,)), dma, dma((3,)), dma, dma((UNITS,)),
            dma, dma((UNITS,)), dma((UNITS,)), dma, dma((3,)), dma, dma((UNITS,)),
            dma, dma((UNITS,)),
            dma, dma, dma, dma,
        ],
        compiler_params=pltpu.CompilerParams(collective_id=0, has_side_effects=True, vmem_limit_bytes=40 * 1024 * 1024),
        name="dual_step",
    )(
        *[
            pltpu.with_memory_space_constraint(a, pltpu.HBM)
            for a in (
                source_mass, target_density, potential,
                lanes(dest_device), lanes(dest_tile), lanes(mass_counts), reach,
            )
        ],
    )

    local = pl.BlockSpec(memory_space=vmem)
    return pl.pallas_call(
        store,
        out_shape=(grid, grid),
        in_specs=[local, local],
        out_specs=(hbm, hbm),
        scratch_shapes=[dma((2,))],
        compiler_params=pltpu.CompilerParams(vmem_limit_bytes=4 * 1024 * 1024),
        name="store",
    )(*fields)


def solution(mesh):
    in_specs = (
        P(None, "gx", "gy"),
        P(None, "gx", "gy"),
        P(None, "gx", "gy"),
        P("gx", "gy", None, None),
        P("gx", "gy", None, None),
        P("gx", "gy", None, None),
        P(),
    )
    out_specs = (P(None, "gx", "gy"), P(None, "gx", "gy"))
    return jax.shard_map(
        per_device, mesh=mesh, in_specs=in_specs, out_specs=out_specs, check_vma=False
    )
```

```python
import jax
import jax.numpy as jnp
from jax import lax
from jax.experimental import pallas as pl
from jax.experimental.pallas import tpu as pltpu
from jax.sharding import PartitionSpec as P

MESH = pl.DeviceIdType.MESH
TS = 16
SLOTS = 6
LANES = 128
UNITS = 8
AXES = ((0, 1, 2), (1, 2, 0), (2, 0, 1))
GROUP = SLOTS * 4
BLOCK = 4 * GROUP
PITCH = 9
F32 = jnp.float32
BF16 = jnp.bfloat16


def split2(a):
    hi = a.astype(BF16)
    return hi, (a - hi.astype(F32)).astype(BF16)


def split3(a):
    hi = a.astype(BF16)
    rest = a - hi.astype(F32)
    mid = rest.astype(BF16)
    return hi, mid, (rest - mid.astype(F32)).astype(BF16)


def dot(a, b, dims=((1,), (0,))):
    return lax.dot_general(a, b, (dims, ((), ())), preferred_element_type=F32)


def dot3(a, b, dims=((1,), (0,))):
    ah, al = a
    bh, bl = b
    return dot(ah, bh, dims) + (dot(ah, bl, dims) + dot(al, bh, dims))


def dot_f32(a, b, dims=((1,), (0,))):
    return lax.dot_general(
        a, b, (dims, ((), ())), precision=lax.Precision.HIGHEST, preferred_element_type=F32
    )


def iota(shape, axis):
    return lax.broadcasted_iota(jnp.int32, shape, axis)


def block_transpose(vectors):
    lane_block = iota((8, LANES), 1) // TS
    vectors = list(vectors)
    for bit in (4, 2, 1):
        low = (lane_block & bit) == 0
        result = [None] * 8
        for a in range(8):
            if a & bit:
                continue
            b = a | bit
            up, down = vectors[a], vectors[b]
            result[a] = jnp.where(low, up, pltpu.roll(down, bit * TS, 1))
            result[b] = jnp.where(low, pltpu.roll(up, LANES - bit * TS, 1), down)
        vectors = result
    return vectors


def powers(logs, exponent):
    return jnp.exp(exponent.astype(F32) * logs)


def whole(ref, first, count, sem):
    part = ref.at[pl.ds(first, count)]
    pltpu.make_async_copy(part, part, sem).wait()


def kernel(
    source_ref, target_ref, potential_ref, device_ref, tile_ref, count_ref, reach_hbm,
    pushed_ref, next_ref,
    natural, target, potential, smooth, reach_ref,
    meta, metas, tiles, regroup, spread_in, picks, weights, places,
    slots_out, slots_in, labels_out, labels_in,
    far_out, far_in, partial_out, partial_in, own_sum,
    xtab_hi, xtab_lo, ytab_hi, ytab_lo, xends_tab, yends_tab, xfill, yfill_tab,
    coef, edge_rows, column_tab, halves, corner_coef, corner_out, corners, xmsg, xall, ymsg, yall,
    load_sem, meta_send, meta_recv, spread_send, spread_recv,
    slot_send, slot_recv, own_recv, label_send, label_recv, far_send, far_recv,
    partial_send, partial_recv, x_send, x_recv, y_send, y_recv, corner_send, corner_recv,
):
    p, q = lax.axis_index("gx"), lax.axis_index("gy")
    n_gx, n_gy = 8, 16
    planes, cx, cy = source_ref.shape
    tile_rows, tile_cols = cx // TS, cy // TS
    half = LANES // 2
    here = (q & 3, p >> 1, q >> 2)
    core = p & 1
    stride = (1, 2 * n_gy, 4)

    def device(moves, other):
        x, y, z = [(here[axis] + moves.get(axis, 0)) & 3 for axis in range(3)]
        return y * 2 + (core ^ other), z * 4 + x

    def remote(src, dst, send, recv, to):
        pltpu.make_async_remote_copy(
            src_ref=src, dst_ref=dst, send_sem=send, recv_sem=recv,
            device_id=to, device_id_type=MESH,
        ).start()

    split = [pl.ds(r * (cx // 2), cx // 2) for r in range(2)]
    loads = [
        pltpu.make_async_copy(a, b, load_sem.at[i])
        for i, (a, b) in enumerate([
            (source_ref.at[:, split[0]], natural.at[:, split[0]]),
            (source_ref.at[:, split[1]], natural.at[:, split[1]]),
            (device_ref, meta.at[0]), (tile_ref, meta.at[1]), (count_ref, meta.at[2]),
            (reach_hbm, reach_ref), (target_ref, target), (potential_ref, potential),
        ])
    ]
    for load in loads:
        load.start()

    barrier = pltpu.get_barrier_semaphore()
    peers = [({axis: s}, h) for axis in range(3) for s in range(1, 4) for h in range(2)]
    peers.append(({}, 1))
    for moves, other in peers:
        pl.semaphore_signal(
            barrier, inc=1, device_id=device(moves, other), device_id_type=MESH
        )

    for xo in range(tile_rows):
        if xo % (tile_rows // 2) == 0:
            loads[xo // (tile_rows // 2)].wait()
        parts = [
            natural[g // 2, pl.ds(xo * TS + (g % 2) * 8, 8), :] for g in range(2 * planes)
        ]
        for yo, value in enumerate(block_transpose(parts)):
            regroup[pl.ds((xo * tile_cols + yo) * PITCH, UNITS), :] = value
    for load in loads[2:5]:
        load.wait()
    pl.semaphore_wait(barrier, len(peers))
    for g, (a, _, _) in enumerate(AXES):
        for s in range(1, 4):
            remote(meta, metas.at[g * 3 + s - 1], meta_send, meta_recv.at[g], device({a: s}, 0))
    for c in range(UNITS):
        tiles[pl.ds(c * LANES, LANES), :] = regroup[pl.ds(c, LANES, stride=PITCH), :]
        for s in (2, 1, 3):
            remote(
                tiles.at[pl.ds(c * LANES, LANES)],
                spread_in.at[pl.ds((c * 3 + s - 1) * LANES, LANES)],
                spread_send, spread_recv.at[c], device({AXES[c % 3][0]: s}, 0),
            )

    loads[5].wait()
    decay = [jnp.full((1, 1), 1.0 - 1.0 / reach_ref[z], F32) for z in range(planes)]
    logs = [jnp.log(d) for d in decay]
    scale = [(1.0 - d) ** 2 for d in decay]
    row8 = iota((8, 1), 0)

    def both_rows(values):
        result = jnp.zeros((8, values[0].shape[1]), F32)
        for z, v in enumerate(values):
            result = jnp.where((row8 == z) | (row8 == planes + z), v, result)
        return result

    def stacked(a):
        hi = a.astype(BF16).astype(F32)
        return jnp.concatenate([hi, a - hi], axis=0).astype(BF16)

    logs8, scale8 = both_rows(logs), both_rows(scale)

    def rows_of(n):
        at = iota((8, n), 1)
        squares = powers(2.0 * logs8, at)
        hi = squares.astype(BF16).astype(F32)
        mid = (squares - hi).astype(BF16).astype(F32)
        parts = jnp.concatenate([hi, mid, squares - hi - mid, jnp.zeros_like(hi)], axis=0)
        inside = (iota((n, n), 0) + iota((n, n), 1) < n).astype(BF16)
        sums = dot(parts.astype(BF16), inside)
        sums = sums[0:8] + (sums[8:16] + sums[16:24])
        last = powers(logs8, n - 1 - at)
        fall = powers(logs8, n - at)
        first = scale8 * powers(logs8, at) * sums
        swept = scale8 * powers(logs8, at + 1) * sums
        return sums, last, first, swept, fall

    upper = row8 < planes
    sums_x, last_x, first_x, swept_x, fall_x = rows_of(cx)
    sums_y, last_rows, first_rows, swept_y, fall_y = rows_of(cy)
    edge_rows[0], edge_rows[1] = swept_x, fall_x
    spare = jnp.zeros((cy - 32, cx), F32)
    column_tab[...] = jnp.transpose(
        jnp.concatenate(
            [sums_x, jnp.where(upper, swept_x, fall_x),
             jnp.concatenate([sums_y, sums_y], axis=1),
             jnp.where(upper, last_x, first_x), spare],
            axis=0,
        )
    )
    columns = column_tab[...]
    across_row = iota((cy, cy), 0)
    gap = across_row - iota((cy, cy), 1)
    for z in range(planes):
        near = powers(logs[z], jnp.abs(gap)) * scale[z]
        below = powers(logs[z], gap + cy) * scale[z]
        above = powers(logs[z], cy - gap) * scale[z]

        def column(i, first, count):
            return jnp.broadcast_to(columns[first : first + count, i : i + 1], (count, cy))

        low = gap >= 0
        g0, g1, gy = column(z, 0, cy), column(z, cy, cy), column(16 + z, 0, cy)
        r0, r1, ry = sums_x[z : z + 1, :cy], sums_x[z : z + 1, cy:], sums_y[z : z + 1]
        for r, (left_part, right_part) in enumerate([
            (near * jnp.where(low, g0, r0), above * r1),
            (below * g1, near * jnp.where(low, g1, r1)),
        ]):
            at = pl.ds(r * cy, cy)
            for w, part in enumerate((left_part, right_part)):
                hi, lo = split2(part)
                xtab_hi[z, at, pl.ds(w * cy, cy)] = hi
                xtab_lo[z, at, pl.ds(w * cy, cy)] = lo
        ytab_hi[z], ytab_lo[z] = split2(near * jnp.where(low, gy, ry))
        xfill[z] = jnp.broadcast_to(columns[:, 8 + z : 9 + z], (cx, LANES))
        xfill[planes + z] = jnp.broadcast_to(
            columns[:, 8 + planes + z : 9 + planes + z], (cx, LANES)
        )
        one, two = row8 == z, row8 == planes + z
        xends_tab[z] = stacked(jnp.where(one, last_x, 0.0) + jnp.where(two, first_x, 0.0))
        yends_tab[z] = stacked(jnp.where(one, last_rows, 0.0) + jnp.where(two, first_rows, 0.0))
        fill = jnp.where(one, swept_y, 0.0) + jnp.where(two, fall_y, 0.0)
        hi = fill.astype(BF16).astype(F32)
        yfill_tab[z] = jnp.concatenate([hi, hi, fill - hi, fill - hi], axis=0).astype(BF16)

    def coefficients(base, count, at, n, first):
        across = jnp.exp(float(n) * logs8)
        powers_of = [jnp.ones((8, 1), F32)]
        for _ in range(count - 1):
            powers_of.append(powers_of[-1] * across)
        low = row8 < planes
        before, after = [], []
        for i in range(count):
            coming = jnp.zeros((8, 1), F32)
            going = jnp.zeros((8, 1), F32)
            for m in range(count - 1):
                coming = jnp.where(at - 1 - i == m, powers_of[m], coming)
                going = jnp.where(i - at - 1 == m, powers_of[m], going)
            before.append(coming)
            after.append(going)
        through = jnp.zeros((8, 1), F32)
        crossing = [None] * count
        for i in reversed(range(count)):
            crossing[i] = first * through
            through = after[i] + across * through
        for i in range(count):
            coef[base + i] = jnp.broadcast_to(jnp.where(low, before[i], after[i]), (8, LANES))
            coef[base + count + i] = jnp.broadcast_to(
                jnp.where(low, crossing[i], 0.0), (8, LANES)
            )

    coefficients(0, n_gx, p, cx, swept_x[:, 0:1])
    coefficients(2 * n_gx, n_gy, q, cy, swept_y[:, 0:1])

    earlier = (iota((LANES, LANES), 0) < iota((LANES, LANES), 1)).astype(BF16)
    row = iota((32, LANES), 0)
    row_target, row_j = row >> 2, row & 3
    order = iota((8, LANES), 0).astype(F32)

    def find_slots(g, s, info):
        a, b, e = AXES[g]
        names, spots, counts = info[0], info[1].astype(F32), info[2].astype(F32)
        shares = counts / jnp.sum(counts, axis=0, keepdims=True)
        number = (
            here[a] * stride[a] + ((here[b] + (row_target >> 1)) & 3) * stride[b]
            + (core ^ (row_target & 1)) * n_gy + ((here[e] + row_j) & 3) * stride[e]
        )
        share = jnp.zeros((32, LANES), F32)
        spot = jnp.zeros((32, LANES), F32)
        for f in range(4):
            match = number == names[f : f + 1, :]
            share = jnp.where(match, shares[f : f + 1, :], share)
            spot = jnp.where(match, spots[f : f + 1, :], spot)
        named = share > 0.0
        rank = dot(jnp.where(named, 1.0, 0.0).astype(BF16), earlier)
        rank = jnp.where(named, rank, -1.0)
        found = []
        for r in range(32):
            mine = rank[r : r + 1, :] == order
            found.append(jnp.where(mine, 1.0, 0.0))
            part = jnp.where(mine, share[r : r + 1, :], 0.0)
            weights[g * 4 + s, pl.ds(r * 8, 8), :] = jnp.broadcast_to(
                jnp.sum(part, axis=1, keepdims=True), (8, LANES)
            )
            places[g, pl.ds((r // 4) * LANES + (r % 4) * GROUP + s * SLOTS, SLOTS), :] = (
                jnp.where(mine, spot[r : r + 1, :], 0.0)[:SLOTS]
            )
        picks[g * 4 + s] = jnp.concatenate(found, axis=0).astype(BF16)

    def find_labels(g):
        b = AXES[g][1]
        for ih in range(8):
            places[g, pl.ds(ih * LANES + BLOCK, LANES - BLOCK), :] = jnp.zeros(
                (LANES - BLOCK, LANES), F32
            )
        found = dot(jnp.ones((8, LANES), BF16), places[g].astype(BF16), ((1,), (1,)))
        for ih in range(8):
            line = found[0:1, ih * LANES : (ih + 1) * LANES]
            if ih == 0:
                labels_in[g * 8] = line
            else:
                labels_out[g * 8 + ih - 1] = line
        for ih in range(1, 8):
            remote(
                labels_out.at[g * 8 + ih - 1], labels_in.at[g * 8 + ih],
                label_send, label_recv.at[g], device({b: ih // 2}, ih % 2),
            )

    for g in range(3):
        find_slots(g, 0, meta[...])
    for g in range(3):
        whole(metas, g * 3, 3, meta_recv.at[g])
        for s in range(1, 4):
            find_slots(g, s, metas[g * 3 + s - 1])
        find_labels(g)

    def pack(c):
        g = c % 3
        for s in range(4):
            if s == 1:
                whole(spread_in, c * 3 * LANES, 3 * LANES, spread_recv.at[c])
            if s == 0:
                value = tiles[pl.ds(c * LANES, LANES), :]
            else:
                value = spread_in[pl.ds((c * 3 + s - 1) * LANES, LANES), :]
            pick = picks[g * 4 + s]
            value = dot(
                jnp.concatenate([pick, pick], axis=1), jnp.concatenate(split2(value), axis=0)
            )
            value = value * weights[g * 4 + s]
            for r in range(32):
                ih, j = r // 4, r % 4
                piece = value[r * 8 : r * 8 + SLOTS]
                within = j * GROUP + s * SLOTS
                if ih == 0:
                    slots_in[pl.ds(c * 8 * BLOCK + within, SLOTS), :] = piece
                else:
                    slots_out[pl.ds((c * 7 + ih - 1) * BLOCK + within, SLOTS), :] = piece
        send_slots(c, GROUP, BLOCK - GROUP, slot_recv)

    def send_slots(c, first, count, recv):
        for ih in range(1, 8):
            remote(
                slots_out.at[pl.ds((c * 7 + ih - 1) * BLOCK + first, count)],
                slots_in.at[pl.ds((c * 8 + ih) * BLOCK + first, count)],
                slot_send, recv.at[c], device({AXES[c % 3][1]: ih // 2}, ih % 2),
            )

    for c in range(UNITS):
        pack(c)

    corner_lane = iota((8, LANES), 1)
    corner_row = (corner_lane >> 3) * planes + (corner_lane & 3) == iota((8, LANES), 0)
    for i in range(2 * n_gx):
        corner_coef[pl.ds(i, 1), :] = jnp.sum(
            jnp.where(corner_row, coef[i], 0.0), axis=0, keepdims=True
        )

    def inflow(base, count, all_ref, width):
        columns = []
        for w in range(width // LANES):
            direct, through = [], []
            for i in range(count):
                value = all_ref[i, :, pl.ds(w * LANES, LANES)]
                direct.append(coef[base + i] * value)
                through.append(coef[base + count + i] * value)
            while len(direct) > 1:
                direct = [a + b for a, b in zip(direct[::2], direct[1::2])]
                through = [a + b for a, b in zip(through[::2], through[1::2])]
            columns.append(direct[0] + pltpu.roll(through[0], planes, 0))
        return columns[0] if len(columns) == 1 else jnp.concatenate(columns, axis=1)

    wide = 8 * GROUP
    out_lane = iota((1, wide), 1)
    sender = jnp.zeros((1, wide), jnp.int32)
    for m in range(1, 8):
        sender += (out_lane >= m * GROUP).astype(jnp.int32)
    within = out_lane - sender * GROUP
    in_lane = iota((LANES, wide), 0)
    sender_row = iota((8, wide), 0) == sender
    tile_index = iota((LANES, wide), 0).astype(F32)
    selects = []
    for g in range(3):
        whole(labels_in, g * 8 + 1, 7, label_recv.at[g])
        lines = labels_in[pl.ds(g * 8, 8)].reshape(8, LANES).astype(BF16)
        row_of = []
        for j in range(4):
            choose = in_lane == within + j * GROUP
            named = dot(lines, choose.astype(BF16))
            named = jnp.sum(jnp.where(sender_row, named, 0.0), axis=0, keepdims=True)
            row_of.append((tile_index == named).astype(BF16))
        selects.append(row_of)

    part_lane = iota((LANES, LANES), 1)
    source_lane = iota((LANES, LANES), 0)
    unit_row = iota((LANES, cx), 0)
    cell = iota((LANES, cx), 1)
    unit_weights = []
    for first in (24, 24 + planes):
        expand = (source_lane == first + (part_lane >> 5)).astype(BF16)
        values = sum(dot(part, expand) for part in split3(column_tab[...]))
        values = split3(values)
        rows = []
        for h in range(2):
            pick = (cell == (unit_row & 15) * TS + h * 8 + (unit_row >> 4)).astype(BF16)
            rows.append(sum(dot(pick, part) for part in values))
        unit_weights.append(jnp.where((part_lane & TS) == 0, rows[0], rows[1]))
    loads[6].wait()
    ends = jnp.zeros((8, cy), F32)
    for z in range(planes):
        value = dot(xends_tab[z], jnp.concatenate(split2(target[z]), axis=1))
        ends += value[:8, :cy] + (value[:8, cy:] + value[8:, :cy])
    unit_ends = [jnp.zeros((8, LANES), F32), jnp.zeros((8, LANES), F32)]

    def collect(c, j):
        rows = jnp.concatenate(
            [slots_in[pl.ds((c * 8 + ih) * BLOCK + j * GROUP, GROUP), :] for ih in range(8)],
            axis=0,
        )
        value = dot(selects[c % 3][j], jnp.concatenate(split2(rows), axis=1))
        return value[:, :LANES] + value[:, LANES:]

    def partial_row(c, s):
        return (c * 2 + s) * LANES

    sides = ((0, 1), (1, 3))

    def send_partial(c, s, move, r):
        at = pl.ds(partial_row(c, s) + r * half, half)
        remote(
            partial_out.at[at], partial_in.at[at],
            partial_send, partial_recv.at[c], device({AXES[c % 3][2]: move}, 0),
        )

    for c in range(UNITS):
        whole(slots_in, (c * 8 + 1) * BLOCK, 7 * (BLOCK - GROUP), slot_recv.at[c])
        far_out[pl.ds(c * LANES, LANES), :] = collect(c, 2)
        for s, move in sides:
            at = pl.ds(c * LANES + s * half, half)
            remote(
                far_out.at[at], far_in.at[at],
                far_send, far_recv.at[c], device({AXES[c % 3][2]: move}, 0),
            )
        for s, move in sides:
            partial_out[pl.ds(partial_row(c, s), LANES), :] = collect(c, move)
            send_partial(c, s, move, 1 - s)
        send_slots(c, 0, GROUP, own_recv)
    for c in range(UNITS):
        whole(far_in, c * LANES, LANES, far_recv.at[c])
        for s, move in sides:
            at = pl.ds(partial_row(c, s) + s * half, half)
            partial_out[at, :] = (
                partial_out[at, :] + far_in[pl.ds(c * LANES + s * half, half), :]
            )
            send_partial(c, s, move, s)
    for c in range(UNITS):
        whole(slots_in, (c * 8 + 1) * BLOCK, 7 * GROUP, own_recv.at[c])
        own_sum[pl.ds(c * LANES, LANES), :] = collect(c, 0)
    for c in range(UNITS):
        whole(partial_in, partial_row(c, 0), 2 * LANES, partial_recv.at[c])
        total = (
            own_sum[pl.ds(c * LANES, LANES), :]
            + partial_in[pl.ds(partial_row(c, 0), LANES), :]
            + partial_in[pl.ds(partial_row(c, 1), LANES), :]
        )
        for i in range(2):
            terms = [
                total[xo * 8 : (xo + 1) * 8] * unit_weights[i][c * 16 + xo : c * 16 + xo + 1]
                for xo in range(tile_rows)
            ]
            while len(terms) > 1:
                terms = [a + b for a, b in zip(terms[::2], terms[1::2])]
            unit_ends[i] = unit_ends[i] + terms[0]
        regroup[pl.ds(c, LANES, stride=PITCH), :] = total

    lane = iota((8, LANES), 1)
    last, first = [a + pltpu.roll(a, LANES - TS, 1) for a in unit_ends]
    block = lane >> 4 == iota((8, LANES), 0)
    for i, value in enumerate((last, first)):
        for z in range(planes):
            moved = pltpu.roll(value, (LANES - 2 * TS * z) % LANES, 1) if z else value
            moved = pltpu.roll(moved, 0, 1, stride=TS, stride_axis=0)
            moved = jnp.sum(jnp.where(block, moved, 0.0), axis=0, keepdims=True)
            ends -= jnp.where(row8 == i * planes + z, moved, 0.0)
    xmsg[...] = ends
    for s in range(4):
        for h in range(2):
            if s + h:
                remote(xmsg, xall.at[p], x_send, x_recv, device({1: s}, h))
    xall[p] = ends
    at_last = jnp.sum(ends * last_rows, axis=1, keepdims=True)
    at_first = jnp.sum(ends * first_rows, axis=1, keepdims=True)
    corner = jnp.sum(
        jnp.where(corner_row, jnp.where((corner_lane & 4) == 0, at_last, at_first), 0.0),
        axis=0, keepdims=True,
    )
    here_block = p * n_gy + q
    corner_out[0] = corner
    corners[here_block] = corner
    for far in (2, 1, 3, 0):
        for dz in (2, 1, 3, 0):
            for dx in (2, 1, 3, 0):
                for h in range(2):
                    if far + h + dz + dx:
                        remote(
                            corner_out.at[0], corners.at[here_block], corner_send, corner_recv,
                            device({1: far, 2: dz, 0: dx}, h),
                        )
    for xo in range(tile_rows):
        parts = [
            regroup[pl.ds((xo * tile_cols + yo) * PITCH, UNITS), :] for yo in range(tile_cols)
        ]
        for g, value in enumerate(block_transpose(parts)):
            pushed_ref[g // 2, pl.ds(xo * TS + (g % 2) * 8, 8), :] = value
    for z in range(planes):
        halves[z] = jnp.concatenate(split2(target[z] - pushed_ref[z]), axis=1)
    y_ends = jnp.zeros((8, cx), F32)
    for z in range(planes):
        both = halves[z]
        value = dot(xtab_hi[z], both)
        value = value[:, :cy] + (value[:, cy:] + dot(xtab_lo[z], both[:, :cy]))
        smooth[z] = value
        value = dot(yends_tab[z], jnp.concatenate(split2(value), axis=0), ((1,), (1,)))
        y_ends += value[:8, :cx] + (value[:8, cx:] + value[8:, :cx])
    ymsg[...] = y_ends
    for dz in range(4):
        for dx in range(4):
            if dz + dx:
                remote(ymsg, yall.at[q], y_send, y_recv, device({2: dz, 0: dx}, 0))
    yall[q] = y_ends
    whole(xall, 0, n_gx - 1, x_recv)
    flow = inflow(0, n_gx, xall, cy)

    loads[7].wait()
    for z in range(planes):
        value = smooth[z] + (
            xfill[z] * flow[z : z + 1] + xfill[planes + z] * flow[planes + z : planes + z + 1]
        )
        potential[z] = potential[z] + dot3(split2(value), (ytab_hi[z], ytab_lo[z]))
    whole(corners, 0, n_gx * n_gy - 1, corner_recv)
    direct, through = [], []
    for i in range(n_gx):
        value = corners[pl.ds(i * n_gy, n_gy)].reshape(n_gy, LANES)
        direct.append(value * corner_coef[pl.ds(i, 1), :])
        through.append(value * corner_coef[pl.ds(n_gx + i, 1), :])
    while len(direct) > 1:
        direct = [a + b for a, b in zip(direct[::2], direct[1::2])]
        through = [a + b for a, b in zip(through[::2], through[1::2])]
    crossed = direct[0] + pltpu.roll(through[0], 8, 1)
    crossed = jnp.transpose(
        jnp.concatenate([crossed, jnp.zeros((LANES - n_gy, LANES), F32)], axis=0)
    )
    whole(yall, 0, n_gy - 1, y_recv)
    for i in range(n_gy):
        yall[i] = (
            yall[i]
            + edge_rows[0] * crossed[0:8, i : i + 1]
            + edge_rows[1] * crossed[8:16, i : i + 1]
        )
    flow = inflow(2 * n_gx, n_gy, yall, cx)
    hi = flow.astype(BF16).astype(F32)
    flow = jnp.concatenate([hi, flow - hi, hi, flow - hi], axis=0).astype(BF16)
    for z in range(planes):
        next_ref[z] = potential[z] + dot(flow, yfill_tab[z], ((0,), (0,)))

    whole(metas, 0, 9, meta_send)
    whole(spread_in, 0, 3 * UNITS * LANES, spread_send)
    whole(slots_out, 0, 7 * UNITS * BLOCK, slot_send)
    whole(labels_out, 0, 21, label_send)
    whole(far_out, 0, UNITS * LANES, far_send)
    whole(partial_out, 0, 2 * UNITS * LANES, partial_send)
    whole(xall, 0, n_gx - 1, x_send)
    whole(yall, 0, n_gy - 1, y_send)
    whole(corners, 0, n_gx * n_gy - 1, corner_send)


def store(pushed_ref, next_ref, pushed_out, next_out, sems):
    copies = [
        pltpu.make_async_copy(pushed_ref, pushed_out, sems.at[0]),
        pltpu.make_async_copy(next_ref, next_out, sems.at[1]),
    ]
    for copy in copies:
        copy.start()
    for copy in copies:
        copy.wait()


def per_device(source_mass, target_density, potential, dest_device, dest_tile, mass_counts, reach):
    planes, cx, cy = source_mass.shape

    def lanes(a):
        return jnp.swapaxes(a.reshape(a.shape[2:]), 0, 1)

    hbm = pl.BlockSpec(memory_space=pl.ANY)
    dma = pltpu.SemaphoreType.DMA
    vmem = pltpu.VMEM
    grid = jax.ShapeDtypeStruct((planes, cx, cy), F32)
    field = vmem((planes, cx, cy), F32)

    def rows(count):
        return vmem((count, LANES), F32)

    fields = pl.pallas_call(
        kernel,
        out_shape=(grid, grid),
        in_specs=[hbm] * 7,
        out_specs=(pl.BlockSpec(memory_space=vmem), pl.BlockSpec(memory_space=vmem)),
        scratch_shapes=[
            field, field, field, field,
            pltpu.SMEM((planes,), F32),
            vmem((3, 4, LANES), jnp.int32),
            vmem((9, 3, 4, LANES), jnp.int32),
            rows(UNITS * LANES), rows(LANES * PITCH + 16), rows(3 * UNITS * LANES),
            vmem((12, 256, LANES), BF16),
            vmem((12, 256, LANES), F32),
            vmem((3, 8 * LANES, LANES), F32),
            rows(7 * UNITS * BLOCK + 8), rows(8 * UNITS * BLOCK + 8),
            vmem((24, 1, LANES), F32),
            vmem((24, 1, LANES), F32),
            rows(UNITS * LANES), rows(UNITS * LANES),
            rows(2 * UNITS * LANES), rows(2 * UNITS * LANES), rows(UNITS * LANES),
            vmem((planes, cx, cx), BF16),
            vmem((planes, cx, cx), BF16),
            vmem((planes, cy, cy), BF16),
            vmem((planes, cy, cy), BF16),
            vmem((planes, 16, cx), BF16),
            vmem((planes, 16, cy), BF16),
            vmem((2 * planes, cx, LANES), F32),
            vmem((planes, 32, cy), BF16),
            vmem((48, 8, LANES), F32),
            vmem((2, 8, cx), F32),
            vmem((cx, LANES), F32),
            vmem((planes, cx, 2 * cy), BF16),
            vmem((16, LANES), F32),
            vmem((1, 1, LANES), F32),
            vmem((LANES, 1, LANES), F32),
            vmem((8, cy), F32),
            vmem((8, 8, cy), F32),
            vmem((8, cx), F32),
            vmem((16, 8, cx), F32),
            dma((8,)), dma, dma((3,)), dma, dma((UNITS,)),
            dma, dma((UNITS,)), dma((UNITS,)), dma, dma((3,)), dma, dma((UNITS,)),
            dma, dma((UNITS,)),
            dma, dma, dma, dma, dma, dma,
        ],
        compiler_params=pltpu.CompilerParams(collective_id=0, has_side_effects=True, vmem_limit_bytes=40 * 1024 * 1024),
        name="dual_step",
    )(
        *[
            pltpu.with_memory_space_constraint(a, pltpu.HBM)
            for a in (
                source_mass, target_density, potential,
                lanes(dest_device), lanes(dest_tile), lanes(mass_counts), reach,
            )
        ],
    )

    local = pl.BlockSpec(memory_space=vmem)
    return pl.pallas_call(
        store,
        out_shape=(grid, grid),
        in_specs=[local, local],
        out_specs=(hbm, hbm),
        scratch_shapes=[dma((2,))],
        compiler_params=pltpu.CompilerParams(vmem_limit_bytes=4 * 1024 * 1024),
        name="store",
    )(*fields)


def solution(mesh):
    in_specs = (
        P(None, "gx", "gy"),
        P(None, "gx", "gy"),
        P(None, "gx", "gy"),
        P("gx", "gy", None, None),
        P("gx", "gy", None, None),
        P("gx", "gy", None, None),
        P(),
    )
    out_specs = (P(None, "gx", "gy"), P(None, "gx", "gy"))
    return jax.shard_map(
        per_device, mesh=mesh, in_specs=in_specs, out_specs=out_specs, check_vma=False
    )
```

```python
import jax
import jax.numpy as jnp
from jax import lax
from jax.experimental import pallas as pl
from jax.experimental.pallas import tpu as pltpu
from jax.sharding import PartitionSpec as P

MESH = pl.DeviceIdType.MESH
TS = 16
SLOTS = 6
LANES = 128
UNITS = 8
AXES = ((0, 1, 2), (1, 2, 0), (2, 0, 1))
GROUP = SLOTS * 4
BLOCK = 4 * GROUP
PITCH = 9
F32 = jnp.float32
BF16 = jnp.bfloat16


def split2(a):
    hi = a.astype(BF16)
    return hi, (a - hi.astype(F32)).astype(BF16)


def split3(a):
    hi = a.astype(BF16)
    rest = a - hi.astype(F32)
    mid = rest.astype(BF16)
    return hi, mid, (rest - mid.astype(F32)).astype(BF16)


def dot(a, b, dims=((1,), (0,))):
    return lax.dot_general(a, b, (dims, ((), ())), preferred_element_type=F32)


def dot3(a, b, dims=((1,), (0,))):
    ah, al = a
    bh, bl = b
    return dot(ah, bh, dims) + (dot(ah, bl, dims) + dot(al, bh, dims))


def dot_f32(a, b, dims=((1,), (0,))):
    return lax.dot_general(
        a, b, (dims, ((), ())), precision=lax.Precision.HIGHEST, preferred_element_type=F32
    )


def iota(shape, axis):
    return lax.broadcasted_iota(jnp.int32, shape, axis)


def block_transpose(vectors):
    lane_block = iota((8, LANES), 1) // TS
    vectors = list(vectors)
    for bit in (4, 2, 1):
        low = (lane_block & bit) == 0
        result = [None] * 8
        for a in range(8):
            if a & bit:
                continue
            b = a | bit
            up, down = vectors[a], vectors[b]
            result[a] = jnp.where(low, up, pltpu.roll(down, bit * TS, 1))
            result[b] = jnp.where(low, pltpu.roll(up, LANES - bit * TS, 1), down)
        vectors = result
    return vectors


def powers(logs, exponent):
    return jnp.exp(exponent.astype(F32) * logs)


def whole(ref, first, count, sem):
    part = ref.at[pl.ds(first, count)]
    pltpu.make_async_copy(part, part, sem).wait()


def kernel(
    source_ref, target_ref, potential_ref, device_ref, tile_ref, count_ref, reach_hbm,
    pushed_ref, next_ref,
    natural, target, potential, smooth, reach_ref,
    meta, metas, tiles, regroup, spread_in, picks, weights, places,
    slots_out, slots_in, labels_out, labels_in,
    far_out, far_in, partial_out, partial_in, own_sum,
    xtab_hi, xtab_lo, ytab_hi, ytab_lo, xends_tab, yends_tab, xfill, yfill_tab,
    coef, edge_rows, column_tab, halves, line_coef, corner_coef, corner_out, corners, xmsg, xall, ymsg, yall,
    load_sem, meta_send, meta_recv, spread_send, spread_recv,
    slot_send, slot_recv, own_recv, label_send, label_recv, far_send, far_recv,
    partial_send, partial_recv, x_send, x_recv, y_send, y_recv, corner_send, corner_recv,
):
    p, q = lax.axis_index("gx"), lax.axis_index("gy")
    n_gx, n_gy = 8, 16
    planes, cx, cy = source_ref.shape
    tile_rows, tile_cols = cx // TS, cy // TS
    half = LANES // 2
    here = (q & 3, p >> 1, q >> 2)
    core = p & 1
    stride = (1, 2 * n_gy, 4)

    def device(moves, other):
        x, y, z = [(here[axis] + moves.get(axis, 0)) & 3 for axis in range(3)]
        return y * 2 + (core ^ other), z * 4 + x

    def remote(src, dst, send, recv, to):
        pltpu.make_async_remote_copy(
            src_ref=src, dst_ref=dst, send_sem=send, recv_sem=recv,
            device_id=to, device_id_type=MESH,
        ).start()

    split = [pl.ds(r * (cx // 2), cx // 2) for r in range(2)]
    loads = [
        pltpu.make_async_copy(a, b, load_sem.at[i])
        for i, (a, b) in enumerate([
            (source_ref.at[:, split[0]], natural.at[:, split[0]]),
            (source_ref.at[:, split[1]], natural.at[:, split[1]]),
            (device_ref, meta.at[0]), (tile_ref, meta.at[1]), (count_ref, meta.at[2]),
            (reach_hbm, reach_ref), (target_ref, target), (potential_ref, potential),
        ])
    ]
    for load in loads:
        load.start()

    barrier = pltpu.get_barrier_semaphore()
    peers = [({axis: s}, h) for axis in range(3) for s in range(1, 4) for h in range(2)]
    peers.append(({}, 1))
    for moves, other in peers:
        pl.semaphore_signal(
            barrier, inc=1, device_id=device(moves, other), device_id_type=MESH
        )

    for xo in range(tile_rows):
        if xo % (tile_rows // 2) == 0:
            loads[xo // (tile_rows // 2)].wait()
        parts = [
            natural[g // 2, pl.ds(xo * TS + (g % 2) * 8, 8), :] for g in range(2 * planes)
        ]
        for yo, value in enumerate(block_transpose(parts)):
            regroup[pl.ds((xo * tile_cols + yo) * PITCH, UNITS), :] = value
    for load in loads[2:5]:
        load.wait()
    pl.semaphore_wait(barrier, len(peers))
    for g, (a, _, _) in enumerate(AXES):
        for s in range(1, 4):
            remote(meta, metas.at[g * 3 + s - 1], meta_send, meta_recv.at[g], device({a: s}, 0))
    for c in range(UNITS):
        tiles[pl.ds(c * LANES, LANES), :] = regroup[pl.ds(c, LANES, stride=PITCH), :]
        for s in (2, 1, 3):
            remote(
                tiles.at[pl.ds(c * LANES, LANES)],
                spread_in.at[pl.ds((c * 3 + s - 1) * LANES, LANES)],
                spread_send, spread_recv.at[c], device({AXES[c % 3][0]: s}, 0),
            )

    loads[5].wait()
    decay = [jnp.full((1, 1), 1.0 - 1.0 / reach_ref[z], F32) for z in range(planes)]
    logs = [jnp.log(d) for d in decay]
    scale = [(1.0 - d) ** 2 for d in decay]
    row8 = iota((8, 1), 0)

    def both_rows(values):
        result = jnp.zeros((8, values[0].shape[1]), F32)
        for z, v in enumerate(values):
            result = jnp.where((row8 == z) | (row8 == planes + z), v, result)
        return result

    def stacked(a):
        hi = a.astype(BF16).astype(F32)
        return jnp.concatenate([hi, a - hi], axis=0).astype(BF16)

    logs8, scale8 = both_rows(logs), both_rows(scale)

    def rows_of(n):
        at = iota((8, n), 1)
        squares = powers(2.0 * logs8, at)
        hi = squares.astype(BF16).astype(F32)
        mid = (squares - hi).astype(BF16).astype(F32)
        parts = jnp.concatenate([hi, mid, squares - hi - mid, jnp.zeros_like(hi)], axis=0)
        inside = (iota((n, n), 0) + iota((n, n), 1) < n).astype(BF16)
        sums = dot(parts.astype(BF16), inside)
        sums = sums[0:8] + (sums[8:16] + sums[16:24])
        last = powers(logs8, n - 1 - at)
        fall = powers(logs8, n - at)
        first = scale8 * powers(logs8, at) * sums
        swept = scale8 * powers(logs8, at + 1) * sums
        return sums, last, first, swept, fall

    upper = row8 < planes
    sums_x, last_x, first_x, swept_x, fall_x = rows_of(cx)
    sums_y, last_rows, first_rows, swept_y, fall_y = rows_of(cy)
    edge_rows[0], edge_rows[1] = swept_x, fall_x
    spare = jnp.zeros((cy - 32, cx), F32)
    column_tab[...] = jnp.transpose(
        jnp.concatenate(
            [sums_x, jnp.where(upper, swept_x, fall_x),
             jnp.concatenate([sums_y, sums_y], axis=1),
             jnp.where(upper, last_x, first_x), spare],
            axis=0,
        )
    )
    columns = column_tab[...]
    across_row = iota((cy, cy), 0)
    gap = across_row - iota((cy, cy), 1)
    for z in range(planes):
        near = powers(logs[z], jnp.abs(gap)) * scale[z]
        below = powers(logs[z], gap + cy) * scale[z]
        above = powers(logs[z], cy - gap) * scale[z]

        def column(i, first, count):
            return jnp.broadcast_to(columns[first : first + count, i : i + 1], (count, cy))

        low = gap >= 0
        g0, g1, gy = column(z, 0, cy), column(z, cy, cy), column(16 + z, 0, cy)
        r0, r1, ry = sums_x[z : z + 1, :cy], sums_x[z : z + 1, cy:], sums_y[z : z + 1]
        for r, (left_part, right_part) in enumerate([
            (near * jnp.where(low, g0, r0), above * r1),
            (below * g1, near * jnp.where(low, g1, r1)),
        ]):
            at = pl.ds(r * cy, cy)
            for w, part in enumerate((left_part, right_part)):
                hi, lo = split2(part)
                xtab_hi[z, at, pl.ds(w * cy, cy)] = hi
                xtab_lo[z, at, pl.ds(w * cy, cy)] = lo
        ytab_hi[z], ytab_lo[z] = split2(near * jnp.where(low, gy, ry))
        xfill[z] = jnp.broadcast_to(columns[:, 8 + z : 9 + z], (cx, LANES))
        xfill[planes + z] = jnp.broadcast_to(
            columns[:, 8 + planes + z : 9 + planes + z], (cx, LANES)
        )
        one, two = row8 == z, row8 == planes + z
        xends_tab[z] = stacked(jnp.where(one, last_x, 0.0) + jnp.where(two, first_x, 0.0))
        yends_tab[z] = stacked(jnp.where(one, last_rows, 0.0) + jnp.where(two, first_rows, 0.0))
        fill = jnp.where(one, swept_y, 0.0) + jnp.where(two, fall_y, 0.0)
        hi = fill.astype(BF16).astype(F32)
        yfill_tab[z] = jnp.concatenate([hi, hi, fill - hi, fill - hi], axis=0).astype(BF16)

    def coefficients(base, count, at, n, first):
        across = jnp.exp(float(n) * logs8)
        powers_of = [jnp.ones((8, 1), F32)]
        for _ in range(count - 1):
            powers_of.append(powers_of[-1] * across)
        low = row8 < planes
        before, after = [], []
        for i in range(count):
            coming = jnp.zeros((8, 1), F32)
            going = jnp.zeros((8, 1), F32)
            for m in range(count - 1):
                coming = jnp.where(at - 1 - i == m, powers_of[m], coming)
                going = jnp.where(i - at - 1 == m, powers_of[m], going)
            before.append(coming)
            after.append(going)
        through = jnp.zeros((8, 1), F32)
        crossing = [None] * count
        for i in reversed(range(count)):
            crossing[i] = first * through
            through = after[i] + across * through
        for i in range(count):
            coef[base + i] = jnp.broadcast_to(jnp.where(low, before[i], after[i]), (8, LANES))
            coef[base + count + i] = jnp.broadcast_to(
                jnp.where(low, crossing[i], 0.0), (8, LANES)
            )

    coefficients(0, n_gx, p, cx, swept_x[:, 0:1])
    coefficients(2 * n_gx, n_gy, q, cy, swept_y[:, 0:1])

    earlier = (iota((LANES, LANES), 0) < iota((LANES, LANES), 1)).astype(BF16)
    row = iota((32, LANES), 0)
    row_target, row_j = row >> 2, row & 3
    order = iota((8, LANES), 0).astype(F32)

    def find_slots(g, s, info):
        a, b, e = AXES[g]
        names, spots, counts = info[0], info[1].astype(F32), info[2].astype(F32)
        shares = counts / jnp.sum(counts, axis=0, keepdims=True)
        number = (
            here[a] * stride[a] + ((here[b] + (row_target >> 1)) & 3) * stride[b]
            + (core ^ (row_target & 1)) * n_gy + ((here[e] + row_j) & 3) * stride[e]
        )
        share = jnp.zeros((32, LANES), F32)
        spot = jnp.zeros((32, LANES), F32)
        for f in range(4):
            match = number == names[f : f + 1, :]
            share = jnp.where(match, shares[f : f + 1, :], share)
            spot = jnp.where(match, spots[f : f + 1, :], spot)
        named = share > 0.0
        rank = dot(jnp.where(named, 1.0, 0.0).astype(BF16), earlier)
        rank = jnp.where(named, rank, -1.0)
        found = []
        for r in range(32):
            mine = rank[r : r + 1, :] == order
            found.append(jnp.where(mine, 1.0, 0.0))
            part = jnp.where(mine, share[r : r + 1, :], 0.0)
            weights[g * 4 + s, pl.ds(r * 8, 8), :] = jnp.broadcast_to(
                jnp.sum(part, axis=1, keepdims=True), (8, LANES)
            )
            places[g, pl.ds((r // 4) * LANES + (r % 4) * GROUP + s * SLOTS, SLOTS), :] = (
                jnp.where(mine, spot[r : r + 1, :], 0.0)[:SLOTS]
            )
        picks[g * 4 + s] = jnp.concatenate(found, axis=0).astype(BF16)

    def find_labels(g):
        b = AXES[g][1]
        for ih in range(8):
            places[g, pl.ds(ih * LANES + BLOCK, LANES - BLOCK), :] = jnp.zeros(
                (LANES - BLOCK, LANES), F32
            )
        found = dot(jnp.ones((8, LANES), BF16), places[g].astype(BF16), ((1,), (1,)))
        for ih in range(8):
            line = found[0:1, ih * LANES : (ih + 1) * LANES]
            if ih == 0:
                labels_in[g * 8] = line
            else:
                labels_out[g * 8 + ih - 1] = line
        for ih in range(1, 8):
            remote(
                labels_out.at[g * 8 + ih - 1], labels_in.at[g * 8 + ih],
                label_send, label_recv.at[g], device({b: ih // 2}, ih % 2),
            )

    for g in range(3):
        find_slots(g, 0, meta[...])
    for g in range(3):
        whole(metas, g * 3, 3, meta_recv.at[g])
        for s in range(1, 4):
            find_slots(g, s, metas[g * 3 + s - 1])
        find_labels(g)

    def pack(c):
        g = c % 3
        for s in range(4):
            if s == 1:
                whole(spread_in, c * 3 * LANES, 3 * LANES, spread_recv.at[c])
            if s == 0:
                value = tiles[pl.ds(c * LANES, LANES), :]
            else:
                value = spread_in[pl.ds((c * 3 + s - 1) * LANES, LANES), :]
            pick = picks[g * 4 + s]
            value = dot(
                jnp.concatenate([pick, pick], axis=1), jnp.concatenate(split2(value), axis=0)
            )
            value = value * weights[g * 4 + s]
            for r in range(32):
                ih, j = r // 4, r % 4
                piece = value[r * 8 : r * 8 + SLOTS]
                within = j * GROUP + s * SLOTS
                if ih == 0:
                    slots_in[pl.ds(c * 8 * BLOCK + within, SLOTS), :] = piece
                else:
                    slots_out[pl.ds((c * 7 + ih - 1) * BLOCK + within, SLOTS), :] = piece
        send_slots(c, GROUP, BLOCK - GROUP, slot_recv)

    def send_slots(c, first, count, recv):
        for ih in range(1, 8):
            remote(
                slots_out.at[pl.ds((c * 7 + ih - 1) * BLOCK + first, count)],
                slots_in.at[pl.ds((c * 8 + ih) * BLOCK + first, count)],
                slot_send, recv.at[c], device({AXES[c % 3][1]: ih // 2}, ih % 2),
            )

    for c in range(UNITS):
        pack(c)

    corner_lane = iota((8, LANES), 1)
    corner_row = (corner_lane >> 3) * planes + (corner_lane & 3) == iota((8, LANES), 0)
    for i in range(2 * n_gx):
        corner_coef[pl.ds(i, 1), :] = jnp.sum(
            jnp.where(corner_row, coef[i], 0.0), axis=0, keepdims=True
        )

    for k in range(2):
        value = jnp.zeros((8, LANES), F32)
        for i in range(n_gy):
            value = jnp.where(corner_lane == i, coef[2 * n_gx + k * n_gy + i], value)
        line_coef[k] = value

    def inflow(base, count, all_ref, width):
        columns = []
        for w in range(width // LANES):
            direct, through = [], []
            for i in range(count):
                value = all_ref[i, :, pl.ds(w * LANES, LANES)]
                direct.append(coef[base + i] * value)
                through.append(coef[base + count + i] * value)
            while len(direct) > 1:
                direct = [a + b for a, b in zip(direct[::2], direct[1::2])]
                through = [a + b for a, b in zip(through[::2], through[1::2])]
            columns.append(direct[0] + pltpu.roll(through[0], planes, 0))
        return columns[0] if len(columns) == 1 else jnp.concatenate(columns, axis=1)

    wide = 8 * GROUP
    out_lane = iota((1, wide), 1)
    sender = jnp.zeros((1, wide), jnp.int32)
    for m in range(1, 8):
        sender += (out_lane >= m * GROUP).astype(jnp.int32)
    within = out_lane - sender * GROUP
    in_lane = iota((LANES, wide), 0)
    sender_row = iota((8, wide), 0) == sender
    tile_index = iota((LANES, wide), 0).astype(F32)
    selects = []
    for g in range(3):
        whole(labels_in, g * 8 + 1, 7, label_recv.at[g])
        lines = labels_in[pl.ds(g * 8, 8)].reshape(8, LANES).astype(BF16)
        row_of = []
        for j in range(4):
            choose = in_lane == within + j * GROUP
            named = dot(lines, choose.astype(BF16))
            named = jnp.sum(jnp.where(sender_row, named, 0.0), axis=0, keepdims=True)
            row_of.append((tile_index == named).astype(BF16))
        selects.append(row_of)

    part_lane = iota((LANES, LANES), 1)
    source_lane = iota((LANES, LANES), 0)
    unit_row = iota((LANES, cx), 0)
    cell = iota((LANES, cx), 1)
    unit_weights = []
    for first in (24, 24 + planes):
        expand = (source_lane == first + (part_lane >> 5)).astype(BF16)
        values = sum(dot(part, expand) for part in split3(column_tab[...]))
        values = split3(values)
        rows = []
        for h in range(2):
            pick = (cell == (unit_row & 15) * TS + h * 8 + (unit_row >> 4)).astype(BF16)
            rows.append(sum(dot(pick, part) for part in values))
        unit_weights.append(jnp.where((part_lane & TS) == 0, rows[0], rows[1]))
    loads[6].wait()
    ends = jnp.zeros((8, cy), F32)
    for z in range(planes):
        value = dot(xends_tab[z], jnp.concatenate(split2(target[z]), axis=1))
        ends += value[:8, :cy] + (value[:8, cy:] + value[8:, :cy])
    unit_ends = [jnp.zeros((8, LANES), F32), jnp.zeros((8, LANES), F32)]

    def collect(c, j):
        rows = jnp.concatenate(
            [slots_in[pl.ds((c * 8 + ih) * BLOCK + j * GROUP, GROUP), :] for ih in range(8)],
            axis=0,
        )
        value = dot(selects[c % 3][j], jnp.concatenate(split2(rows), axis=1))
        return value[:, :LANES] + value[:, LANES:]

    def partial_row(c, s):
        return (c * 2 + s) * LANES

    sides = ((0, 1), (1, 3))

    def send_partial(c, s, move, r):
        at = pl.ds(partial_row(c, s) + r * half, half)
        remote(
            partial_out.at[at], partial_in.at[at],
            partial_send, partial_recv.at[c], device({AXES[c % 3][2]: move}, 0),
        )

    for c in range(UNITS):
        whole(slots_in, (c * 8 + 1) * BLOCK, 7 * (BLOCK - GROUP), slot_recv.at[c])
        far_out[pl.ds(c * LANES, LANES), :] = collect(c, 2)
        for s, move in sides:
            at = pl.ds(c * LANES + s * half, half)
            remote(
                far_out.at[at], far_in.at[at],
                far_send, far_recv.at[c], device({AXES[c % 3][2]: move}, 0),
            )
        for s, move in sides:
            partial_out[pl.ds(partial_row(c, s), LANES), :] = collect(c, move)
            send_partial(c, s, move, 1 - s)
        send_slots(c, 0, GROUP, own_recv)
    for c in range(UNITS):
        whole(far_in, c * LANES, LANES, far_recv.at[c])
        for s, move in sides:
            at = pl.ds(partial_row(c, s) + s * half, half)
            partial_out[at, :] = (
                partial_out[at, :] + far_in[pl.ds(c * LANES + s * half, half), :]
            )
            send_partial(c, s, move, s)
    for c in range(UNITS):
        whole(slots_in, (c * 8 + 1) * BLOCK, 7 * GROUP, own_recv.at[c])
        own_sum[pl.ds(c * LANES, LANES), :] = collect(c, 0)
    for c in range(UNITS):
        whole(partial_in, partial_row(c, 0), 2 * LANES, partial_recv.at[c])
        total = (
            own_sum[pl.ds(c * LANES, LANES), :]
            + partial_in[pl.ds(partial_row(c, 0), LANES), :]
            + partial_in[pl.ds(partial_row(c, 1), LANES), :]
        )
        for i in range(2):
            terms = [
                total[xo * 8 : (xo + 1) * 8] * unit_weights[i][c * 16 + xo : c * 16 + xo + 1]
                for xo in range(tile_rows)
            ]
            while len(terms) > 1:
                terms = [a + b for a, b in zip(terms[::2], terms[1::2])]
            unit_ends[i] = unit_ends[i] + terms[0]
        regroup[pl.ds(c, LANES, stride=PITCH), :] = total

    lane = iota((8, LANES), 1)
    last, first = [a + pltpu.roll(a, LANES - TS, 1) for a in unit_ends]
    block = lane >> 4 == iota((8, LANES), 0)
    for i, value in enumerate((last, first)):
        for z in range(planes):
            moved = pltpu.roll(value, (LANES - 2 * TS * z) % LANES, 1) if z else value
            moved = pltpu.roll(moved, 0, 1, stride=TS, stride_axis=0)
            moved = jnp.sum(jnp.where(block, moved, 0.0), axis=0, keepdims=True)
            ends -= jnp.where(row8 == i * planes + z, moved, 0.0)
    xmsg[...] = ends
    for s in range(4):
        for h in range(2):
            if s + h:
                remote(xmsg, xall.at[p], x_send, x_recv, device({1: s}, h))
    xall[p] = ends
    at_last = jnp.sum(ends * last_rows, axis=1, keepdims=True)
    at_first = jnp.sum(ends * first_rows, axis=1, keepdims=True)
    corner = jnp.sum(
        jnp.where(corner_row, jnp.where((corner_lane & 4) == 0, at_last, at_first), 0.0),
        axis=0, keepdims=True,
    )
    here_block = p * n_gy + q
    corner_out[0] = corner
    corners[here_block] = corner
    moves = [
        (sum(min(v, 4 - v) for v in (dx, dy, dz)), dx, dy, dz, h)
        for dx in range(4) for dy in range(4) for dz in range(4) for h in range(2)
    ]
    moves = sorted(moves, reverse=True)[:-1]

    def send_corner(hops, dx, dy, dz, h):
        remote(
            corner_out.at[0], corners.at[here_block], corner_send, corner_recv,
            device({0: dx, 1: dy, 2: dz}, h),
        )

    for move in moves:
        if move[0] >= 4:
            send_corner(*move)
    for xo in range(tile_rows):
        parts = [
            regroup[pl.ds((xo * tile_cols + yo) * PITCH, UNITS), :] for yo in range(tile_cols)
        ]
        for g, value in enumerate(block_transpose(parts)):
            pushed_ref[g // 2, pl.ds(xo * TS + (g % 2) * 8, 8), :] = value
    for z in range(planes):
        halves[z] = jnp.concatenate(split2(target[z] - pushed_ref[z]), axis=1)
    y_ends = jnp.zeros((8, cx), F32)
    for z in range(planes):
        both = halves[z]
        value = dot(xtab_hi[z], both)
        value = value[:, :cy] + (value[:, cy:] + dot(xtab_lo[z], both[:, :cy]))
        smooth[z] = value
        value = dot(yends_tab[z], jnp.concatenate(split2(value), axis=0), ((1,), (1,)))
        y_ends += value[:8, :cx] + (value[:8, cx:] + value[8:, :cx])
    ymsg[...] = y_ends
    for dz in range(4):
        for dx in range(4):
            if dz + dx:
                remote(ymsg, yall.at[q], y_send, y_recv, device({2: dz, 0: dx}, 0))
    yall[q] = y_ends
    for move in moves:
        if move[0] < 4:
            send_corner(*move)
    whole(xall, 0, n_gx - 1, x_recv)
    flow = inflow(0, n_gx, xall, cy)

    loads[7].wait()
    for z in range(planes):
        value = smooth[z] + (
            xfill[z] * flow[z : z + 1] + xfill[planes + z] * flow[planes + z : planes + z + 1]
        )
        potential[z] = potential[z] + dot3(split2(value), (ytab_hi[z], ytab_lo[z]))
    whole(corners, 0, n_gx * n_gy - 1, corner_recv)
    direct, through = [], []
    for i in range(n_gx):
        value = corners[pl.ds(i * n_gy, n_gy)].reshape(n_gy, LANES)
        direct.append(value * corner_coef[pl.ds(i, 1), :])
        through.append(value * corner_coef[pl.ds(n_gx + i, 1), :])
    while len(direct) > 1:
        direct = [a + b for a, b in zip(direct[::2], direct[1::2])]
        through = [a + b for a, b in zip(through[::2], through[1::2])]
    crossed = direct[0] + pltpu.roll(through[0], 8, 1)
    crossed = jnp.transpose(
        jnp.concatenate([crossed, jnp.zeros((LANES - n_gy, LANES), F32)], axis=0)
    )

    def crossed_by(k):
        entered = jnp.sum(crossed[0:8] * line_coef[k], axis=1, keepdims=True)
        left = jnp.sum(crossed[8:16] * line_coef[k], axis=1, keepdims=True)
        return edge_rows[0] * entered + edge_rows[1] * left

    crossing, far_crossing = crossed_by(0), crossed_by(1)
    whole(yall, 0, n_gy - 1, y_recv)
    flow = inflow(2 * n_gx, n_gy, yall, cx)
    flow += crossing + pltpu.roll(far_crossing, planes, 0)
    hi = flow.astype(BF16).astype(F32)
    flow = jnp.concatenate([hi, flow - hi, hi, flow - hi], axis=0).astype(BF16)
    for z in range(planes):
        next_ref[z] = potential[z] + dot(flow, yfill_tab[z], ((0,), (0,)))

    whole(metas, 0, 9, meta_send)
    whole(spread_in, 0, 3 * UNITS * LANES, spread_send)
    whole(slots_out, 0, 7 * UNITS * BLOCK, slot_send)
    whole(labels_out, 0, 21, label_send)
    whole(far_out, 0, UNITS * LANES, far_send)
    whole(partial_out, 0, 2 * UNITS * LANES, partial_send)
    whole(xall, 0, n_gx - 1, x_send)
    whole(yall, 0, n_gy - 1, y_send)
    whole(corners, 0, n_gx * n_gy - 1, corner_send)


def store(pushed_ref, next_ref, pushed_out, next_out, sems):
    copies = [
        pltpu.make_async_copy(pushed_ref, pushed_out, sems.at[0]),
        pltpu.make_async_copy(next_ref, next_out, sems.at[1]),
    ]
    for copy in copies:
        copy.start()
    for copy in copies:
        copy.wait()


def per_device(source_mass, target_density, potential, dest_device, dest_tile, mass_counts, reach):
    planes, cx, cy = source_mass.shape

    def lanes(a):
        return jnp.swapaxes(a.reshape(a.shape[2:]), 0, 1)

    hbm = pl.BlockSpec(memory_space=pl.ANY)
    dma = pltpu.SemaphoreType.DMA
    vmem = pltpu.VMEM
    grid = jax.ShapeDtypeStruct((planes, cx, cy), F32)
    field = vmem((planes, cx, cy), F32)

    def rows(count):
        return vmem((count, LANES), F32)

    fields = pl.pallas_call(
        kernel,
        out_shape=(grid, grid),
        in_specs=[hbm] * 7,
        out_specs=(pl.BlockSpec(memory_space=vmem), pl.BlockSpec(memory_space=vmem)),
        scratch_shapes=[
            field, field, field, field,
            pltpu.SMEM((planes,), F32),
            vmem((3, 4, LANES), jnp.int32),
            vmem((9, 3, 4, LANES), jnp.int32),
            rows(UNITS * LANES), rows(LANES * PITCH + 16), rows(3 * UNITS * LANES),
            vmem((12, 256, LANES), BF16),
            vmem((12, 256, LANES), F32),
            vmem((3, 8 * LANES, LANES), F32),
            rows(7 * UNITS * BLOCK + 8), rows(8 * UNITS * BLOCK + 8),
            vmem((24, 1, LANES), F32),
            vmem((24, 1, LANES), F32),
            rows(UNITS * LANES), rows(UNITS * LANES),
            rows(2 * UNITS * LANES), rows(2 * UNITS * LANES), rows(UNITS * LANES),
            vmem((planes, cx, cx), BF16),
            vmem((planes, cx, cx), BF16),
            vmem((planes, cy, cy), BF16),
            vmem((planes, cy, cy), BF16),
            vmem((planes, 16, cx), BF16),
            vmem((planes, 16, cy), BF16),
            vmem((2 * planes, cx, LANES), F32),
            vmem((planes, 32, cy), BF16),
            vmem((48, 8, LANES), F32),
            vmem((2, 8, cx), F32),
            vmem((cx, LANES), F32),
            vmem((planes, cx, 2 * cy), BF16),
            vmem((2, 8, LANES), F32),
            vmem((16, LANES), F32),
            vmem((1, 1, LANES), F32),
            vmem((LANES, 1, LANES), F32),
            vmem((8, cy), F32),
            vmem((8, 8, cy), F32),
            vmem((8, cx), F32),
            vmem((16, 8, cx), F32),
            dma((8,)), dma, dma((3,)), dma, dma((UNITS,)),
            dma, dma((UNITS,)), dma((UNITS,)), dma, dma((3,)), dma, dma((UNITS,)),
            dma, dma((UNITS,)),
            dma, dma, dma, dma, dma, dma,
        ],
        compiler_params=pltpu.CompilerParams(collective_id=0, has_side_effects=True, vmem_limit_bytes=40 * 1024 * 1024),
        name="dual_step",
    )(
        *[
            pltpu.with_memory_space_constraint(a, pltpu.HBM)
            for a in (
                source_mass, target_density, potential,
                lanes(dest_device), lanes(dest_tile), lanes(mass_counts), reach,
            )
        ],
    )

    local = pl.BlockSpec(memory_space=vmem)
    return pl.pallas_call(
        store,
        out_shape=(grid, grid),
        in_specs=[local, local],
        out_specs=(hbm, hbm),
        scratch_shapes=[dma((2,))],
        compiler_params=pltpu.CompilerParams(vmem_limit_bytes=4 * 1024 * 1024),
        name="store",
    )(*fields)


def solution(mesh):
    in_specs = (
        P(None, "gx", "gy"),
        P(None, "gx", "gy"),
        P(None, "gx", "gy"),
        P("gx", "gy", None, None),
        P("gx", "gy", None, None),
        P("gx", "gy", None, None),
        P(),
    )
    out_specs = (P(None, "gx", "gy"), P(None, "gx", "gy"))
    return jax.shard_map(
        per_device, mesh=mesh, in_specs=in_specs, out_specs=out_specs, check_vma=False
    )
```

```python
import jax
import jax.numpy as jnp
from jax import lax
from jax.experimental import pallas as pl
from jax.experimental.pallas import tpu as pltpu
from jax.sharding import PartitionSpec as P

MESH = pl.DeviceIdType.MESH
TS = 16
SLOTS = 6
LANES = 128
UNITS = 8
AXES = ((0, 1, 2), (1, 2, 0), (2, 0, 1))
GROUP = SLOTS * 4
BLOCK = 4 * GROUP
PITCH = 9
F32 = jnp.float32
BF16 = jnp.bfloat16


def split2(a):
    hi = a.astype(BF16)
    return hi, (a - hi.astype(F32)).astype(BF16)


def split3(a):
    hi = a.astype(BF16)
    rest = a - hi.astype(F32)
    mid = rest.astype(BF16)
    return hi, mid, (rest - mid.astype(F32)).astype(BF16)


def dot(a, b, dims=((1,), (0,))):
    return lax.dot_general(a, b, (dims, ((), ())), preferred_element_type=F32)


def dot3(a, b, dims=((1,), (0,))):
    ah, al = a
    bh, bl = b
    return dot(ah, bh, dims) + (dot(ah, bl, dims) + dot(al, bh, dims))


def dot_f32(a, b, dims=((1,), (0,))):
    return lax.dot_general(
        a, b, (dims, ((), ())), precision=lax.Precision.HIGHEST, preferred_element_type=F32
    )


def iota(shape, axis):
    return lax.broadcasted_iota(jnp.int32, shape, axis)


def block_transpose(vectors):
    lane_block = iota((8, LANES), 1) // TS
    vectors = list(vectors)
    for bit in (4, 2, 1):
        low = (lane_block & bit) == 0
        result = [None] * 8
        for a in range(8):
            if a & bit:
                continue
            b = a | bit
            up, down = vectors[a], vectors[b]
            result[a] = jnp.where(low, up, pltpu.roll(down, bit * TS, 1))
            result[b] = jnp.where(low, pltpu.roll(up, LANES - bit * TS, 1), down)
        vectors = result
    return vectors


def powers(logs, exponent):
    return jnp.exp(exponent.astype(F32) * logs)


def whole(ref, first, count, sem):
    part = ref.at[pl.ds(first, count)]
    pltpu.make_async_copy(part, part, sem).wait()


def kernel(
    source_ref, target_ref, potential_ref, device_ref, tile_ref, count_ref, reach_hbm,
    pushed_ref, next_ref,
    natural, target, potential, smooth, reach_ref,
    meta, metas, tiles, regroup, spread_in, picks, weights, places,
    slots_out, slots_in, labels_out, labels_in,
    far_out, far_in, partial_out, partial_in, own_sum,
    xtab_hi, xtab_lo, ytab_hi, ytab_lo, xends_tab, yends_tab, xfill, yfill_tab,
    coef, edge_rows, column_tab, halves, line_coef, corner_coef, corner_out, corners, xmsg, xall, ymsg, yall,
    load_sem, meta_send, meta_recv, spread_send, spread_recv,
    slot_send, slot_recv, own_recv, label_send, label_recv, far_send, far_recv,
    partial_send, partial_recv, x_send, x_recv, y_send, y_recv, corner_send, corner_recv,
):
    p, q = lax.axis_index("gx"), lax.axis_index("gy")
    n_gx, n_gy = 8, 16
    planes, cx, cy = source_ref.shape
    tile_rows, tile_cols = cx // TS, cy // TS
    half = LANES // 2
    here = (q & 3, p >> 1, q >> 2)
    core = p & 1
    stride = (1, 2 * n_gy, 4)

    def device(moves, other):
        x, y, z = [(here[axis] + moves.get(axis, 0)) & 3 for axis in range(3)]
        return y * 2 + (core ^ other), z * 4 + x

    def remote(src, dst, send, recv, to):
        pltpu.make_async_remote_copy(
            src_ref=src, dst_ref=dst, send_sem=send, recv_sem=recv,
            device_id=to, device_id_type=MESH,
        ).start()

    split = [pl.ds(r * (cx // 2), cx // 2) for r in range(2)]
    loads = [
        pltpu.make_async_copy(a, b, load_sem.at[i])
        for i, (a, b) in enumerate([
            (source_ref.at[:, split[0]], natural.at[:, split[0]]),
            (source_ref.at[:, split[1]], natural.at[:, split[1]]),
            (device_ref, meta.at[0]), (tile_ref, meta.at[1]), (count_ref, meta.at[2]),
            (reach_hbm, reach_ref), (target_ref, target), (potential_ref, potential),
        ])
    ]
    for load in loads:
        load.start()

    barrier = pltpu.get_barrier_semaphore()
    peers = [({axis: s}, h) for axis in range(3) for s in range(1, 4) for h in range(2)]
    peers.append(({}, 1))
    for moves, other in peers:
        pl.semaphore_signal(
            barrier, inc=1, device_id=device(moves, other), device_id_type=MESH
        )

    for xo in range(tile_rows):
        if xo % (tile_rows // 2) == 0:
            loads[xo // (tile_rows // 2)].wait()
        parts = [
            natural[g // 2, pl.ds(xo * TS + (g % 2) * 8, 8), :] for g in range(2 * planes)
        ]
        for yo, value in enumerate(block_transpose(parts)):
            regroup[pl.ds((xo * tile_cols + yo) * PITCH, UNITS), :] = value
    for load in loads[2:5]:
        load.wait()
    pl.semaphore_wait(barrier, len(peers))
    for g, (a, _, _) in enumerate(AXES):
        for s in range(1, 4):
            remote(meta, metas.at[g * 3 + s - 1], meta_send, meta_recv.at[g], device({a: s}, 0))
    for c in range(UNITS):
        tiles[pl.ds(c * LANES, LANES), :] = regroup[pl.ds(c, LANES, stride=PITCH), :]
        for s in (2, 1, 3):
            remote(
                tiles.at[pl.ds(c * LANES, LANES)],
                spread_in.at[pl.ds((c * 3 + s - 1) * LANES, LANES)],
                spread_send, spread_recv.at[c], device({AXES[c % 3][0]: s}, 0),
            )

    loads[5].wait()
    decay = [jnp.full((1, 1), 1.0 - 1.0 / reach_ref[z], F32) for z in range(planes)]
    logs = [jnp.log(d) for d in decay]
    scale = [(1.0 - d) ** 2 for d in decay]
    row8 = iota((8, 1), 0)

    def both_rows(values):
        result = jnp.zeros((8, values[0].shape[1]), F32)
        for z, v in enumerate(values):
            result = jnp.where((row8 == z) | (row8 == planes + z), v, result)
        return result

    def stacked(a):
        hi = a.astype(BF16).astype(F32)
        return jnp.concatenate([hi, a - hi], axis=0).astype(BF16)

    logs8, scale8 = both_rows(logs), both_rows(scale)

    def rows_of(n):
        at = iota((8, n), 1)
        squares = powers(2.0 * logs8, at)
        hi = squares.astype(BF16).astype(F32)
        mid = (squares - hi).astype(BF16).astype(F32)
        parts = jnp.concatenate([hi, mid, squares - hi - mid, jnp.zeros_like(hi)], axis=0)
        inside = (iota((n, n), 0) + iota((n, n), 1) < n).astype(BF16)
        sums = dot(parts.astype(BF16), inside)
        sums = sums[0:8] + (sums[8:16] + sums[16:24])
        last = powers(logs8, n - 1 - at)
        fall = powers(logs8, n - at)
        first = scale8 * powers(logs8, at) * sums
        swept = scale8 * powers(logs8, at + 1) * sums
        return sums, last, first, swept, fall

    upper = row8 < planes
    sums_x, last_x, first_x, swept_x, fall_x = rows_of(cx)
    sums_y, last_rows, first_rows, swept_y, fall_y = rows_of(cy)
    edge_rows[0], edge_rows[1] = swept_x, fall_x
    spare = jnp.zeros((cy - 32, cx), F32)
    column_tab[...] = jnp.transpose(
        jnp.concatenate(
            [sums_x, jnp.where(upper, swept_x, fall_x),
             jnp.concatenate([sums_y, sums_y], axis=1),
             jnp.where(upper, last_x, first_x), spare],
            axis=0,
        )
    )
    columns = column_tab[...]
    across_row = iota((cy, cy), 0)
    gap = across_row - iota((cy, cy), 1)
    for z in range(planes):
        near = powers(logs[z], jnp.abs(gap)) * scale[z]
        below = powers(logs[z], gap + cy) * scale[z]
        above = powers(logs[z], cy - gap) * scale[z]

        def column(i, first, count):
            return jnp.broadcast_to(columns[first : first + count, i : i + 1], (count, cy))

        low = gap >= 0
        g0, g1, gy = column(z, 0, cy), column(z, cy, cy), column(16 + z, 0, cy)
        r0, r1, ry = sums_x[z : z + 1, :cy], sums_x[z : z + 1, cy:], sums_y[z : z + 1]
        for r, (left_part, right_part) in enumerate([
            (near * jnp.where(low, g0, r0), above * r1),
            (below * g1, near * jnp.where(low, g1, r1)),
        ]):
            at = pl.ds(r * cy, cy)
            for w, part in enumerate((left_part, right_part)):
                hi, lo = split2(part)
                xtab_hi[z, at, pl.ds(w * cy, cy)] = hi
                xtab_lo[z, at, pl.ds(w * cy, cy)] = lo
        ytab_hi[z], ytab_lo[z] = split2(near * jnp.where(low, gy, ry))
        xfill[z] = jnp.broadcast_to(columns[:, 8 + z : 9 + z], (cx, LANES))
        xfill[planes + z] = jnp.broadcast_to(
            columns[:, 8 + planes + z : 9 + planes + z], (cx, LANES)
        )
        one, two = row8 == z, row8 == planes + z
        xends_tab[z] = stacked(jnp.where(one, last_x, 0.0) + jnp.where(two, first_x, 0.0))
        yends_tab[z] = stacked(jnp.where(one, last_rows, 0.0) + jnp.where(two, first_rows, 0.0))
        fill = jnp.where(one, swept_y, 0.0) + jnp.where(two, fall_y, 0.0)
        hi = fill.astype(BF16).astype(F32)
        yfill_tab[z] = jnp.concatenate([hi, hi, fill - hi, fill - hi], axis=0).astype(BF16)

    def coefficients(base, count, at, n, first):
        across = jnp.exp(float(n) * logs8)
        powers_of = [jnp.ones((8, 1), F32)]
        for _ in range(count - 1):
            powers_of.append(powers_of[-1] * across)
        low = row8 < planes
        before, after = [], []
        for i in range(count):
            coming = jnp.zeros((8, 1), F32)
            going = jnp.zeros((8, 1), F32)
            for m in range(count - 1):
                coming = jnp.where(at - 1 - i == m, powers_of[m], coming)
                going = jnp.where(i - at - 1 == m, powers_of[m], going)
            before.append(coming)
            after.append(going)
        through = jnp.zeros((8, 1), F32)
        crossing = [None] * count
        for i in reversed(range(count)):
            crossing[i] = first * through
            through = after[i] + across * through
        for i in range(count):
            coef[base + i] = jnp.broadcast_to(jnp.where(low, before[i], after[i]), (8, LANES))
            coef[base + count + i] = jnp.broadcast_to(
                jnp.where(low, crossing[i], 0.0), (8, LANES)
            )

    coefficients(0, n_gx, p, cx, swept_x[:, 0:1])
    coefficients(2 * n_gx, n_gy, q, cy, swept_y[:, 0:1])

    earlier = (iota((LANES, LANES), 0) < iota((LANES, LANES), 1)).astype(BF16)
    row = iota((32, LANES), 0)
    row_target, row_j = row >> 2, row & 3
    order = iota((8, LANES), 0).astype(F32)

    def find_slots(g, s, info):
        a, b, e = AXES[g]
        names, spots, counts = info[0], info[1].astype(F32), info[2].astype(F32)
        shares = counts / jnp.sum(counts, axis=0, keepdims=True)
        number = (
            here[a] * stride[a] + ((here[b] + (row_target >> 1)) & 3) * stride[b]
            + (core ^ (row_target & 1)) * n_gy + ((here[e] + row_j) & 3) * stride[e]
        )
        share = jnp.zeros((32, LANES), F32)
        spot = jnp.zeros((32, LANES), F32)
        for f in range(4):
            match = number == names[f : f + 1, :]
            share = jnp.where(match, shares[f : f + 1, :], share)
            spot = jnp.where(match, spots[f : f + 1, :], spot)
        named = share > 0.0
        rank = dot(jnp.where(named, 1.0, 0.0).astype(BF16), earlier)
        rank = jnp.where(named, rank, -1.0)
        found = []
        for r in range(32):
            mine = rank[r : r + 1, :] == order
            found.append(jnp.where(mine, 1.0, 0.0))
            part = jnp.where(mine, share[r : r + 1, :], 0.0)
            weights[g * 4 + s, pl.ds(r * 8, 8), :] = jnp.broadcast_to(
                jnp.sum(part, axis=1, keepdims=True), (8, LANES)
            )
            places[g, pl.ds((r // 4) * LANES + (r % 4) * GROUP + s * SLOTS, SLOTS), :] = (
                jnp.where(mine, spot[r : r + 1, :], 0.0)[:SLOTS]
            )
        picks[g * 4 + s] = jnp.concatenate(found, axis=0).astype(BF16)

    def find_labels(g):
        b = AXES[g][1]
        for ih in range(8):
            places[g, pl.ds(ih * LANES + BLOCK, LANES - BLOCK), :] = jnp.zeros(
                (LANES - BLOCK, LANES), F32
            )
        found = dot(jnp.ones((8, LANES), BF16), places[g].astype(BF16), ((1,), (1,)))
        for ih in range(8):
            line = found[0:1, ih * LANES : (ih + 1) * LANES]
            if ih == 0:
                labels_in[g * 8] = line
            else:
                labels_out[g * 8 + ih - 1] = line
        for ih in range(1, 8):
            remote(
                labels_out.at[g * 8 + ih - 1], labels_in.at[g * 8 + ih],
                label_send, label_recv.at[g], device({b: ih // 2}, ih % 2),
            )

    for g in range(3):
        find_slots(g, 0, meta[...])
    for g in range(3):
        whole(metas, g * 3, 3, meta_recv.at[g])
        for s in range(1, 4):
            find_slots(g, s, metas[g * 3 + s - 1])
        find_labels(g)

    def pack(c):
        g = c % 3
        for s in range(4):
            if s == 1:
                whole(spread_in, c * 3 * LANES, 3 * LANES, spread_recv.at[c])
            if s == 0:
                value = tiles[pl.ds(c * LANES, LANES), :]
            else:
                value = spread_in[pl.ds((c * 3 + s - 1) * LANES, LANES), :]
            pick = picks[g * 4 + s]
            value = dot(
                jnp.concatenate([pick, pick], axis=1), jnp.concatenate(split2(value), axis=0)
            )
            value = value * weights[g * 4 + s]
            for r in range(32):
                ih, j = r // 4, r % 4
                piece = value[r * 8 : r * 8 + SLOTS]
                within = j * GROUP + s * SLOTS
                if ih == 0:
                    slots_in[pl.ds(c * 8 * BLOCK + within, SLOTS), :] = piece
                else:
                    slots_out[pl.ds((c * 7 + ih - 1) * BLOCK + within, SLOTS), :] = piece
        send_slots(c, GROUP, BLOCK - GROUP, slot_recv)

    def send_slots(c, first, count, recv):
        for ih in range(1, 8):
            remote(
                slots_out.at[pl.ds((c * 7 + ih - 1) * BLOCK + first, count)],
                slots_in.at[pl.ds((c * 8 + ih) * BLOCK + first, count)],
                slot_send, recv.at[c], device({AXES[c % 3][1]: ih // 2}, ih % 2),
            )

    for c in range(UNITS):
        pack(c)

    corner_lane = iota((8, LANES), 1)
    corner_row = (corner_lane >> 3) * planes + (corner_lane & 3) == iota((8, LANES), 0)
    for i in range(2 * n_gx):
        corner_coef[pl.ds(i, 1), :] = jnp.sum(
            jnp.where(corner_row, coef[i], 0.0), axis=0, keepdims=True
        )

    for k in range(2):
        value = jnp.zeros((8, LANES), F32)
        for i in range(n_gy):
            value = jnp.where(corner_lane == i, coef[2 * n_gx + k * n_gy + i], value)
        line_coef[k] = value

    def inflow(base, count, all_ref, width):
        columns = []
        for w in range(width // LANES):
            direct, through = [], []
            for i in range(count):
                value = all_ref[i, :, pl.ds(w * LANES, LANES)]
                direct.append(coef[base + i] * value)
                through.append(coef[base + count + i] * value)
            while len(direct) > 1:
                direct = [a + b for a, b in zip(direct[::2], direct[1::2])]
                through = [a + b for a, b in zip(through[::2], through[1::2])]
            columns.append(direct[0] + pltpu.roll(through[0], planes, 0))
        return columns[0] if len(columns) == 1 else jnp.concatenate(columns, axis=1)

    wide = 8 * GROUP
    out_lane = iota((1, wide), 1)
    sender = jnp.zeros((1, wide), jnp.int32)
    for m in range(1, 8):
        sender += (out_lane >= m * GROUP).astype(jnp.int32)
    within = out_lane - sender * GROUP
    in_lane = iota((LANES, wide), 0)
    sender_row = iota((8, wide), 0) == sender
    tile_index = iota((LANES, wide), 0).astype(F32)
    selects = []
    for g in range(3):
        whole(labels_in, g * 8 + 1, 7, label_recv.at[g])
        lines = labels_in[pl.ds(g * 8, 8)].reshape(8, LANES).astype(BF16)
        row_of = []
        for j in range(4):
            choose = in_lane == within + j * GROUP
            named = dot(lines, choose.astype(BF16))
            named = jnp.sum(jnp.where(sender_row, named, 0.0), axis=0, keepdims=True)
            row_of.append((tile_index == named).astype(BF16))
        selects.append(row_of)

    part_lane = iota((LANES, LANES), 1)
    source_lane = iota((LANES, LANES), 0)
    unit_row = iota((LANES, cx), 0)
    cell = iota((LANES, cx), 1)
    unit_weights = []
    for first in (24, 24 + planes):
        expand = (source_lane == first + (part_lane >> 5)).astype(BF16)
        values = sum(dot(part, expand) for part in split3(column_tab[...]))
        values = split3(values)
        rows = []
        for h in range(2):
            pick = (cell == (unit_row & 15) * TS + h * 8 + (unit_row >> 4)).astype(BF16)
            rows.append(sum(dot(pick, part) for part in values))
        unit_weights.append(jnp.where((part_lane & TS) == 0, rows[0], rows[1]))
    loads[6].wait()
    ends = jnp.zeros((8, cy), F32)
    for z in range(planes):
        value = dot(xends_tab[z], jnp.concatenate(split2(target[z]), axis=1))
        ends += value[:8, :cy] + (value[:8, cy:] + value[8:, :cy])
    unit_ends = [jnp.zeros((8, LANES), F32), jnp.zeros((8, LANES), F32)]

    def collect(c, j):
        rows = jnp.concatenate(
            [slots_in[pl.ds((c * 8 + ih) * BLOCK + j * GROUP, GROUP), :] for ih in range(8)],
            axis=0,
        )
        value = dot(selects[c % 3][j], jnp.concatenate(split2(rows), axis=1))
        return value[:, :LANES] + value[:, LANES:]

    def partial_row(c, s):
        return (c * 2 + s) * LANES

    sides = ((0, 1), (1, 3))

    def send_partial(c, s, move, r):
        at = pl.ds(partial_row(c, s) + r * half, half)
        remote(
            partial_out.at[at], partial_in.at[at],
            partial_send, partial_recv.at[c], device({AXES[c % 3][2]: move}, 0),
        )

    for c in range(UNITS):
        whole(slots_in, (c * 8 + 1) * BLOCK, 7 * (BLOCK - GROUP), slot_recv.at[c])
        far_out[pl.ds(c * LANES, LANES), :] = collect(c, 2)
        for s, move in sides:
            at = pl.ds(c * LANES + s * half, half)
            remote(
                far_out.at[at], far_in.at[at],
                far_send, far_recv.at[c], device({AXES[c % 3][2]: move}, 0),
            )
        for s, move in sides:
            partial_out[pl.ds(partial_row(c, s), LANES), :] = collect(c, move)
            send_partial(c, s, move, 1 - s)
        send_slots(c, 0, GROUP, own_recv)
    for c in range(UNITS):
        whole(far_in, c * LANES, LANES, far_recv.at[c])
        for s, move in sides:
            at = pl.ds(partial_row(c, s) + s * half, half)
            partial_out[at, :] = (
                partial_out[at, :] + far_in[pl.ds(c * LANES + s * half, half), :]
            )
            send_partial(c, s, move, s)
    for c in range(UNITS):
        whole(slots_in, (c * 8 + 1) * BLOCK, 7 * GROUP, own_recv.at[c])
        own_sum[pl.ds(c * LANES, LANES), :] = collect(c, 0)
    for c in range(UNITS):
        whole(partial_in, partial_row(c, 0), 2 * LANES, partial_recv.at[c])
        total = (
            own_sum[pl.ds(c * LANES, LANES), :]
            + partial_in[pl.ds(partial_row(c, 0), LANES), :]
            + partial_in[pl.ds(partial_row(c, 1), LANES), :]
        )
        for i in range(2):
            terms = [
                total[xo * 8 : (xo + 1) * 8] * unit_weights[i][c * 16 + xo : c * 16 + xo + 1]
                for xo in range(tile_rows)
            ]
            while len(terms) > 1:
                terms = [a + b for a, b in zip(terms[::2], terms[1::2])]
            unit_ends[i] = unit_ends[i] + terms[0]
        regroup[pl.ds(c, LANES, stride=PITCH), :] = total

    lane = iota((8, LANES), 1)
    last, first = [a + pltpu.roll(a, LANES - TS, 1) for a in unit_ends]
    block = lane >> 4 == iota((8, LANES), 0)
    for i, value in enumerate((last, first)):
        for z in range(planes):
            moved = pltpu.roll(value, (LANES - 2 * TS * z) % LANES, 1) if z else value
            moved = pltpu.roll(moved, 0, 1, stride=TS, stride_axis=0)
            moved = jnp.sum(jnp.where(block, moved, 0.0), axis=0, keepdims=True)
            ends -= jnp.where(row8 == i * planes + z, moved, 0.0)
    xmsg[...] = ends
    for s in range(4):
        for h in range(2):
            if s + h:
                remote(xmsg, xall.at[p], x_send, x_recv, device({1: s}, h))
    xall[p] = ends
    at_last = jnp.sum(ends * last_rows, axis=1, keepdims=True)
    at_first = jnp.sum(ends * first_rows, axis=1, keepdims=True)
    corner = jnp.sum(
        jnp.where(corner_row, jnp.where((corner_lane & 4) == 0, at_last, at_first), 0.0),
        axis=0, keepdims=True,
    )
    here_block = p * n_gy + q
    corner_out[0] = corner
    corners[here_block] = corner
    for far in (2, 1, 3, 0):
        for dz in (2, 1, 3, 0):
            for dx in (2, 1, 3, 0):
                for h in range(2):
                    if far + h + dz + dx:
                        remote(
                            corner_out.at[0], corners.at[here_block], corner_send, corner_recv,
                            device({1: far, 2: dz, 0: dx}, h),
                        )
    for xo in range(tile_rows):
        parts = [
            regroup[pl.ds((xo * tile_cols + yo) * PITCH, UNITS), :] for yo in range(tile_cols)
        ]
        for g, value in enumerate(block_transpose(parts)):
            pushed_ref[g // 2, pl.ds(xo * TS + (g % 2) * 8, 8), :] = value
    for z in range(planes):
        halves[z] = jnp.concatenate(split2(target[z] - pushed_ref[z]), axis=1)
    y_ends = jnp.zeros((8, cx), F32)
    for z in range(planes):
        both = halves[z]
        value = dot(xtab_hi[z], both)
        value = value[:, :cy] + (value[:, cy:] + dot(xtab_lo[z], both[:, :cy]))
        smooth[z] = value
        value = dot(yends_tab[z], jnp.concatenate(split2(value), axis=0), ((1,), (1,)))
        y_ends += value[:8, :cx] + (value[:8, cx:] + value[8:, :cx])
    ymsg[...] = y_ends
    for dz in range(4):
        for dx in range(4):
            if dz + dx:
                remote(ymsg, yall.at[q], y_send, y_recv, device({2: dz, 0: dx}, 0))
    yall[q] = y_ends
    whole(xall, 0, n_gx - 1, x_recv)
    flow = inflow(0, n_gx, xall, cy)

    loads[7].wait()
    for z in range(planes):
        value = smooth[z] + (
            xfill[z] * flow[z : z + 1] + xfill[planes + z] * flow[planes + z : planes + z + 1]
        )
        potential[z] = potential[z] + dot3(split2(value), (ytab_hi[z], ytab_lo[z]))
    whole(corners, 0, n_gx * n_gy - 1, corner_recv)
    direct, through = [], []
    for i in range(n_gx):
        value = corners[pl.ds(i * n_gy, n_gy)].reshape(n_gy, LANES)
        direct.append(value * corner_coef[pl.ds(i, 1), :])
        through.append(value * corner_coef[pl.ds(n_gx + i, 1), :])
    while len(direct) > 1:
        direct = [a + b for a, b in zip(direct[::2], direct[1::2])]
        through = [a + b for a, b in zip(through[::2], through[1::2])]
    crossed = direct[0] + pltpu.roll(through[0], 8, 1)
    crossed = jnp.transpose(
        jnp.concatenate([crossed, jnp.zeros((LANES - n_gy, LANES), F32)], axis=0)
    )

    def crossed_by(k):
        entered = jnp.sum(crossed[0:8] * line_coef[k], axis=1, keepdims=True)
        left = jnp.sum(crossed[8:16] * line_coef[k], axis=1, keepdims=True)
        return edge_rows[0] * entered + edge_rows[1] * left

    crossing, far_crossing = crossed_by(0), crossed_by(1)
    whole(yall, 0, n_gy - 1, y_recv)
    flow = inflow(2 * n_gx, n_gy, yall, cx)
    flow += crossing + pltpu.roll(far_crossing, planes, 0)
    hi = flow.astype(BF16).astype(F32)
    flow = jnp.concatenate([hi, flow - hi, hi, flow - hi], axis=0).astype(BF16)
    for z in range(planes):
        next_ref[z] = potential[z] + dot(flow, yfill_tab[z], ((0,), (0,)))

    whole(metas, 0, 9, meta_send)
    whole(spread_in, 0, 3 * UNITS * LANES, spread_send)
    whole(slots_out, 0, 7 * UNITS * BLOCK, slot_send)
    whole(labels_out, 0, 21, label_send)
    whole(far_out, 0, UNITS * LANES, far_send)
    whole(partial_out, 0, 2 * UNITS * LANES, partial_send)
    whole(xall, 0, n_gx - 1, x_send)
    whole(yall, 0, n_gy - 1, y_send)
    whole(corners, 0, n_gx * n_gy - 1, corner_send)


def store(pushed_ref, next_ref, pushed_out, next_out, sems):
    copies = [
        pltpu.make_async_copy(pushed_ref, pushed_out, sems.at[0]),
        pltpu.make_async_copy(next_ref, next_out, sems.at[1]),
    ]
    for copy in copies:
        copy.start()
    for copy in copies:
        copy.wait()


def per_device(source_mass, target_density, potential, dest_device, dest_tile, mass_counts, reach):
    planes, cx, cy = source_mass.shape

    def lanes(a):
        return jnp.swapaxes(a.reshape(a.shape[2:]), 0, 1)

    hbm = pl.BlockSpec(memory_space=pl.ANY)
    dma = pltpu.SemaphoreType.DMA
    vmem = pltpu.VMEM
    grid = jax.ShapeDtypeStruct((planes, cx, cy), F32)
    field = vmem((planes, cx, cy), F32)

    def rows(count):
        return vmem((count, LANES), F32)

    fields = pl.pallas_call(
        kernel,
        out_shape=(grid, grid),
        in_specs=[hbm] * 7,
        out_specs=(pl.BlockSpec(memory_space=vmem), pl.BlockSpec(memory_space=vmem)),
        scratch_shapes=[
            field, field, field, field,
            pltpu.SMEM((planes,), F32),
            vmem((3, 4, LANES), jnp.int32),
            vmem((9, 3, 4, LANES), jnp.int32),
            rows(UNITS * LANES), rows(LANES * PITCH + 16), rows(3 * UNITS * LANES),
            vmem((12, 256, LANES), BF16),
            vmem((12, 256, LANES), F32),
            vmem((3, 8 * LANES, LANES), F32),
            rows(7 * UNITS * BLOCK + 8), rows(8 * UNITS * BLOCK + 8),
            vmem((24, 1, LANES), F32),
            vmem((24, 1, LANES), F32),
            rows(UNITS * LANES), rows(UNITS * LANES),
            rows(2 * UNITS * LANES), rows(2 * UNITS * LANES), rows(UNITS * LANES),
            vmem((planes, cx, cx), BF16),
            vmem((planes, cx, cx), BF16),
            vmem((planes, cy, cy), BF16),
            vmem((planes, cy, cy), BF16),
            vmem((planes, 16, cx), BF16),
            vmem((planes, 16, cy), BF16),
            vmem((2 * planes, cx, LANES), F32),
            vmem((planes, 32, cy), BF16),
            vmem((48, 8, LANES), F32),
            vmem((2, 8, cx), F32),
            vmem((cx, LANES), F32),
            vmem((planes, cx, 2 * cy), BF16),
            vmem((2, 8, LANES), F32),
            vmem((16, LANES), F32),
            vmem((1, 1, LANES), F32),
            vmem((LANES, 1, LANES), F32),
            vmem((8, cy), F32),
            vmem((8, 8, cy), F32),
            vmem((8, cx), F32),
            vmem((16, 8, cx), F32),
            dma((8,)), dma, dma((3,)), dma, dma((UNITS,)),
            dma, dma((UNITS,)), dma((UNITS,)), dma, dma((3,)), dma, dma((UNITS,)),
            dma, dma((UNITS,)),
            dma, dma, dma, dma, dma, dma,
        ],
        compiler_params=pltpu.CompilerParams(collective_id=0, has_side_effects=True, vmem_limit_bytes=40 * 1024 * 1024),
        name="dual_step",
    )(
        *[
            pltpu.with_memory_space_constraint(a, pltpu.HBM)
            for a in (
                source_mass, target_density, potential,
                lanes(dest_device), lanes(dest_tile), lanes(mass_counts), reach,
            )
        ],
    )

    local = pl.BlockSpec(memory_space=vmem)
    return pl.pallas_call(
        store,
        out_shape=(grid, grid),
        in_specs=[local, local],
        out_specs=(hbm, hbm),
        scratch_shapes=[dma((2,))],
        compiler_params=pltpu.CompilerParams(vmem_limit_bytes=4 * 1024 * 1024),
        name="store",
    )(*fields)


def solution(mesh):
    in_specs = (
        P(None, "gx", "gy"),
        P(None, "gx", "gy"),
        P(None, "gx", "gy"),
        P("gx", "gy", None, None),
        P("gx", "gy", None, None),
        P("gx", "gy", None, None),
        P(),
    )
    out_specs = (P(None, "gx", "gy"), P(None, "gx", "gy"))
    return jax.shard_map(
        per_device, mesh=mesh, in_specs=in_specs, out_specs=out_specs, check_vma=False
    )
```

```python
import jax
import jax.numpy as jnp
from jax import lax
from jax.experimental import pallas as pl
from jax.experimental.pallas import tpu as pltpu
from jax.sharding import PartitionSpec as P

MESH = pl.DeviceIdType.MESH
TS = 16
SLOTS = 6
LANES = 128
UNITS = 8
AXES = ((0, 1, 2), (1, 2, 0), (2, 0, 1))
GROUP = SLOTS * 4
BLOCK = 4 * GROUP
LAG = 3
PITCH = 9
F32 = jnp.float32
BF16 = jnp.bfloat16


def split2(a):
    hi = a.astype(BF16)
    return hi, (a - hi.astype(F32)).astype(BF16)


def split3(a):
    hi = a.astype(BF16)
    rest = a - hi.astype(F32)
    mid = rest.astype(BF16)
    return hi, mid, (rest - mid.astype(F32)).astype(BF16)


def dot(a, b, dims=((1,), (0,))):
    return lax.dot_general(a, b, (dims, ((), ())), preferred_element_type=F32)


def dot3(a, b, dims=((1,), (0,))):
    ah, al = a
    bh, bl = b
    return dot(ah, bh, dims) + (dot(ah, bl, dims) + dot(al, bh, dims))


def dot_f32(a, b, dims=((1,), (0,))):
    return lax.dot_general(
        a, b, (dims, ((), ())), precision=lax.Precision.HIGHEST, preferred_element_type=F32
    )


def iota(shape, axis):
    return lax.broadcasted_iota(jnp.int32, shape, axis)


def block_transpose(vectors):
    lane_block = iota((8, LANES), 1) // TS
    vectors = list(vectors)
    for bit in (4, 2, 1):
        low = (lane_block & bit) == 0
        result = [None] * 8
        for a in range(8):
            if a & bit:
                continue
            b = a | bit
            up, down = vectors[a], vectors[b]
            result[a] = jnp.where(low, up, pltpu.roll(down, bit * TS, 1))
            result[b] = jnp.where(low, pltpu.roll(up, LANES - bit * TS, 1), down)
        vectors = result
    return vectors


def powers(logs, exponent):
    return jnp.exp(exponent.astype(F32) * logs)


def whole(ref, first, count, sem):
    part = ref.at[pl.ds(first, count)]
    pltpu.make_async_copy(part, part, sem).wait()


def kernel(
    source_ref, target_ref, potential_ref, device_ref, tile_ref, count_ref, reach_hbm,
    pushed_ref, next_ref,
    natural, target, potential, smooth, reach_ref,
    meta, metas, tiles, regroup, spread_in, picks, weights, places,
    slots_out, slots_in, labels_out, labels_in,
    far_out, far_in, partial_out, partial_in, own_sum,
    xtab_hi, xtab_lo, ytab_hi, ytab_lo, xends_tab, yends_tab, xfill, yfill_tab,
    coef, edge_rows, column_tab, halves, line_coef, corner_coef, corner_out, corners, xmsg, xall, ymsg, yall,
    load_sem, meta_send, meta_recv, spread_send, spread_recv,
    slot_send, slot_recv, own_recv, label_send, label_recv, far_send, far_recv,
    partial_send, partial_recv, x_send, x_recv, y_send, y_recv, corner_send, corner_recv,
):
    p, q = lax.axis_index("gx"), lax.axis_index("gy")
    n_gx, n_gy = 8, 16
    planes, cx, cy = source_ref.shape
    tile_rows, tile_cols = cx // TS, cy // TS
    half = LANES // 2
    here = (q & 3, p >> 1, q >> 2)
    core = p & 1
    stride = (1, 2 * n_gy, 4)

    def device(moves, other):
        x, y, z = [(here[axis] + moves.get(axis, 0)) & 3 for axis in range(3)]
        return y * 2 + (core ^ other), z * 4 + x

    def remote(src, dst, send, recv, to):
        pltpu.make_async_remote_copy(
            src_ref=src, dst_ref=dst, send_sem=send, recv_sem=recv,
            device_id=to, device_id_type=MESH,
        ).start()

    split = [pl.ds(r * (cx // 2), cx // 2) for r in range(2)]
    loads = [
        pltpu.make_async_copy(a, b, load_sem.at[i])
        for i, (a, b) in enumerate([
            (source_ref.at[:, split[0]], natural.at[:, split[0]]),
            (source_ref.at[:, split[1]], natural.at[:, split[1]]),
            (device_ref, meta.at[0]), (tile_ref, meta.at[1]), (count_ref, meta.at[2]),
            (reach_hbm, reach_ref), (target_ref, target), (potential_ref, potential),
        ])
    ]
    for load in loads:
        load.start()

    barrier = pltpu.get_barrier_semaphore()
    peers = [({axis: s}, h) for axis in range(3) for s in range(1, 4) for h in range(2)]
    peers.append(({}, 1))
    for moves, other in peers:
        pl.semaphore_signal(
            barrier, inc=1, device_id=device(moves, other), device_id_type=MESH
        )

    for xo in range(tile_rows):
        if xo % (tile_rows // 2) == 0:
            loads[xo // (tile_rows // 2)].wait()
        parts = [
            natural[g // 2, pl.ds(xo * TS + (g % 2) * 8, 8), :] for g in range(2 * planes)
        ]
        for yo, value in enumerate(block_transpose(parts)):
            regroup[pl.ds((xo * tile_cols + yo) * PITCH, UNITS), :] = value
    for load in loads[2:5]:
        load.wait()
    pl.semaphore_wait(barrier, len(peers))
    for g, (a, _, _) in enumerate(AXES):
        for s in range(1, 4):
            remote(meta, metas.at[g * 3 + s - 1], meta_send, meta_recv.at[g], device({a: s}, 0))
    for c in range(UNITS):
        tiles[pl.ds(c * LANES, LANES), :] = regroup[pl.ds(c, LANES, stride=PITCH), :]
        for s in (2, 1, 3):
            remote(
                tiles.at[pl.ds(c * LANES, LANES)],
                spread_in.at[pl.ds((c * 3 + s - 1) * LANES, LANES)],
                spread_send, spread_recv.at[c], device({AXES[c % 3][0]: s}, 0),
            )

    loads[5].wait()
    decay = [jnp.full((1, 1), 1.0 - 1.0 / reach_ref[z], F32) for z in range(planes)]
    logs = [jnp.log(d) for d in decay]
    scale = [(1.0 - d) ** 2 for d in decay]
    row8 = iota((8, 1), 0)

    def both_rows(values):
        result = jnp.zeros((8, values[0].shape[1]), F32)
        for z, v in enumerate(values):
            result = jnp.where((row8 == z) | (row8 == planes + z), v, result)
        return result

    def stacked(a):
        hi = a.astype(BF16).astype(F32)
        return jnp.concatenate([hi, a - hi], axis=0).astype(BF16)

    logs8, scale8 = both_rows(logs), both_rows(scale)

    def rows_of(n):
        at = iota((8, n), 1)
        squares = powers(2.0 * logs8, at)
        hi = squares.astype(BF16).astype(F32)
        mid = (squares - hi).astype(BF16).astype(F32)
        parts = jnp.concatenate([hi, mid, squares - hi - mid, jnp.zeros_like(hi)], axis=0)
        inside = (iota((n, n), 0) + iota((n, n), 1) < n).astype(BF16)
        sums = dot(parts.astype(BF16), inside)
        sums = sums[0:8] + (sums[8:16] + sums[16:24])
        last = powers(logs8, n - 1 - at)
        fall = powers(logs8, n - at)
        first = scale8 * powers(logs8, at) * sums
        swept = scale8 * powers(logs8, at + 1) * sums
        return sums, last, first, swept, fall

    upper = row8 < planes
    sums_x, last_x, first_x, swept_x, fall_x = rows_of(cx)
    sums_y, last_rows, first_rows, swept_y, fall_y = rows_of(cy)
    edge_rows[0], edge_rows[1] = swept_x, fall_x
    spare = jnp.zeros((cy - 32, cx), F32)
    column_tab[...] = jnp.transpose(
        jnp.concatenate(
            [sums_x, jnp.where(upper, swept_x, fall_x),
             jnp.concatenate([sums_y, sums_y], axis=1),
             jnp.where(upper, last_x, first_x), spare],
            axis=0,
        )
    )
    columns = column_tab[...]
    across_row = iota((cy, cy), 0)
    gap = across_row - iota((cy, cy), 1)
    for z in range(planes):
        near = powers(logs[z], jnp.abs(gap)) * scale[z]
        below = powers(logs[z], gap + cy) * scale[z]
        above = powers(logs[z], cy - gap) * scale[z]

        def column(i, first, count):
            return jnp.broadcast_to(columns[first : first + count, i : i + 1], (count, cy))

        low = gap >= 0
        g0, g1, gy = column(z, 0, cy), column(z, cy, cy), column(16 + z, 0, cy)
        r0, r1, ry = sums_x[z : z + 1, :cy], sums_x[z : z + 1, cy:], sums_y[z : z + 1]
        for r, (left_part, right_part) in enumerate([
            (near * jnp.where(low, g0, r0), above * r1),
            (below * g1, near * jnp.where(low, g1, r1)),
        ]):
            at = pl.ds(r * cy, cy)
            for w, part in enumerate((left_part, right_part)):
                hi, lo = split2(part)
                xtab_hi[z, at, pl.ds(w * cy, cy)] = hi
                xtab_lo[z, at, pl.ds(w * cy, cy)] = lo
        ytab_hi[z], ytab_lo[z] = split2(near * jnp.where(low, gy, ry))
        xfill[z] = jnp.broadcast_to(columns[:, 8 + z : 9 + z], (cx, LANES))
        xfill[planes + z] = jnp.broadcast_to(
            columns[:, 8 + planes + z : 9 + planes + z], (cx, LANES)
        )
        one, two = row8 == z, row8 == planes + z
        xends_tab[z] = stacked(jnp.where(one, last_x, 0.0) + jnp.where(two, first_x, 0.0))
        yends_tab[z] = stacked(jnp.where(one, last_rows, 0.0) + jnp.where(two, first_rows, 0.0))
        fill = jnp.where(one, swept_y, 0.0) + jnp.where(two, fall_y, 0.0)
        hi = fill.astype(BF16).astype(F32)
        yfill_tab[z] = jnp.concatenate([hi, hi, fill - hi, fill - hi], axis=0).astype(BF16)

    def coefficients(base, count, at, n, first):
        across = jnp.exp(float(n) * logs8)
        powers_of = [jnp.ones((8, 1), F32)]
        for _ in range(count - 1):
            powers_of.append(powers_of[-1] * across)
        low = row8 < planes
        before, after = [], []
        for i in range(count):
            coming = jnp.zeros((8, 1), F32)
            going = jnp.zeros((8, 1), F32)
            for m in range(count - 1):
                coming = jnp.where(at - 1 - i == m, powers_of[m], coming)
                going = jnp.where(i - at - 1 == m, powers_of[m], going)
            before.append(coming)
            after.append(going)
        through = jnp.zeros((8, 1), F32)
        crossing = [None] * count
        for i in reversed(range(count)):
            crossing[i] = first * through
            through = after[i] + across * through
        for i in range(count):
            coef[base + i] = jnp.broadcast_to(jnp.where(low, before[i], after[i]), (8, LANES))
            coef[base + count + i] = jnp.broadcast_to(
                jnp.where(low, crossing[i], 0.0), (8, LANES)
            )

    coefficients(0, n_gx, p, cx, swept_x[:, 0:1])
    coefficients(2 * n_gx, n_gy, q, cy, swept_y[:, 0:1])

    earlier = (iota((LANES, LANES), 0) < iota((LANES, LANES), 1)).astype(BF16)
    row = iota((32, LANES), 0)
    row_target, row_j = row >> 2, row & 3
    order = iota((8, LANES), 0).astype(F32)

    def find_slots(g, s, info):
        a, b, e = AXES[g]
        names, spots, counts = info[0], info[1].astype(F32), info[2].astype(F32)
        shares = counts / jnp.sum(counts, axis=0, keepdims=True)
        number = (
            here[a] * stride[a] + ((here[b] + (row_target >> 1)) & 3) * stride[b]
            + (core ^ (row_target & 1)) * n_gy + ((here[e] + row_j) & 3) * stride[e]
        )
        share = jnp.zeros((32, LANES), F32)
        spot = jnp.zeros((32, LANES), F32)
        for f in range(4):
            match = number == names[f : f + 1, :]
            share = jnp.where(match, shares[f : f + 1, :], share)
            spot = jnp.where(match, spots[f : f + 1, :], spot)
        named = share > 0.0
        rank = dot(jnp.where(named, 1.0, 0.0).astype(BF16), earlier)
        rank = jnp.where(named, rank, -1.0)
        found = []
        for r in range(32):
            mine = rank[r : r + 1, :] == order
            found.append(jnp.where(mine, 1.0, 0.0))
            part = jnp.where(mine, share[r : r + 1, :], 0.0)
            weights[g * 4 + s, pl.ds(r * 8, 8), :] = jnp.broadcast_to(
                jnp.sum(part, axis=1, keepdims=True), (8, LANES)
            )
            places[g, pl.ds((r // 4) * LANES + (r % 4) * GROUP + s * SLOTS, SLOTS), :] = (
                jnp.where(mine, spot[r : r + 1, :], 0.0)[:SLOTS]
            )
        picks[g * 4 + s] = jnp.concatenate(found, axis=0).astype(BF16)

    def find_labels(g):
        b = AXES[g][1]
        for ih in range(8):
            places[g, pl.ds(ih * LANES + BLOCK, LANES - BLOCK), :] = jnp.zeros(
                (LANES - BLOCK, LANES), F32
            )
        found = dot(jnp.ones((8, LANES), BF16), places[g].astype(BF16), ((1,), (1,)))
        for ih in range(8):
            line = found[0:1, ih * LANES : (ih + 1) * LANES]
            if ih == 0:
                labels_in[g * 8] = line
            else:
                labels_out[g * 8 + ih - 1] = line
        for ih in range(1, 8):
            remote(
                labels_out.at[g * 8 + ih - 1], labels_in.at[g * 8 + ih],
                label_send, label_recv.at[g], device({b: ih // 2}, ih % 2),
            )

    for g in range(3):
        find_slots(g, 0, meta[...])
    for g in range(3):
        whole(metas, g * 3, 3, meta_recv.at[g])
        for s in range(1, 4):
            find_slots(g, s, metas[g * 3 + s - 1])
        find_labels(g)

    def pack(c):
        g = c % 3
        for s in range(4):
            if s == 1:
                whole(spread_in, c * 3 * LANES, 3 * LANES, spread_recv.at[c])
            if s == 0:
                value = tiles[pl.ds(c * LANES, LANES), :]
            else:
                value = spread_in[pl.ds((c * 3 + s - 1) * LANES, LANES), :]
            pick = picks[g * 4 + s]
            value = dot(
                jnp.concatenate([pick, pick], axis=1), jnp.concatenate(split2(value), axis=0)
            )
            value = value * weights[g * 4 + s]
            for r in range(32):
                ih, j = r // 4, r % 4
                piece = value[r * 8 : r * 8 + SLOTS]
                within = j * GROUP + s * SLOTS
                if ih == 0:
                    slots_in[pl.ds(c * 8 * BLOCK + within, SLOTS), :] = piece
                else:
                    slots_out[pl.ds((c * 7 + ih - 1) * BLOCK + within, SLOTS), :] = piece
        send_slots(c, GROUP, BLOCK - GROUP, slot_recv)

    def send_slots(c, first, count, recv):
        for ih in range(1, 8):
            remote(
                slots_out.at[pl.ds((c * 7 + ih - 1) * BLOCK + first, count)],
                slots_in.at[pl.ds((c * 8 + ih) * BLOCK + first, count)],
                slot_send, recv.at[c], device({AXES[c % 3][1]: ih // 2}, ih % 2),
            )

    for c in range(UNITS):
        pack(c)

    corner_lane = iota((8, LANES), 1)
    corner_row = (corner_lane >> 3) * planes + (corner_lane & 3) == iota((8, LANES), 0)
    for i in range(2 * n_gx):
        corner_coef[pl.ds(i, 1), :] = jnp.sum(
            jnp.where(corner_row, coef[i], 0.0), axis=0, keepdims=True
        )

    for k in range(2):
        value = jnp.zeros((8, LANES), F32)
        for i in range(n_gy):
            value = jnp.where(corner_lane == i, coef[2 * n_gx + k * n_gy + i], value)
        line_coef[k] = value

    def inflow(base, count, all_ref, width):
        columns = []
        for w in range(width // LANES):
            direct, through = [], []
            for i in range(count):
                value = all_ref[i, :, pl.ds(w * LANES, LANES)]
                direct.append(coef[base + i] * value)
                through.append(coef[base + count + i] * value)
            while len(direct) > 1:
                direct = [a + b for a, b in zip(direct[::2], direct[1::2])]
                through = [a + b for a, b in zip(through[::2], through[1::2])]
            columns.append(direct[0] + pltpu.roll(through[0], planes, 0))
        return columns[0] if len(columns) == 1 else jnp.concatenate(columns, axis=1)

    wide = 8 * GROUP
    out_lane = iota((1, wide), 1)
    sender = jnp.zeros((1, wide), jnp.int32)
    for m in range(1, 8):
        sender += (out_lane >= m * GROUP).astype(jnp.int32)
    within = out_lane - sender * GROUP
    in_lane = iota((LANES, wide), 0)
    sender_row = iota((8, wide), 0) == sender
    tile_index = iota((LANES, wide), 0).astype(F32)
    selects = []
    for g in range(3):
        whole(labels_in, g * 8 + 1, 7, label_recv.at[g])
        lines = labels_in[pl.ds(g * 8, 8)].reshape(8, LANES).astype(BF16)
        row_of = []
        for j in range(4):
            choose = in_lane == within + j * GROUP
            named = dot(lines, choose.astype(BF16))
            named = jnp.sum(jnp.where(sender_row, named, 0.0), axis=0, keepdims=True)
            row_of.append((tile_index == named).astype(BF16))
        selects.append(row_of)

    part_lane = iota((LANES, LANES), 1)
    source_lane = iota((LANES, LANES), 0)
    unit_row = iota((LANES, cx), 0)
    cell = iota((LANES, cx), 1)
    unit_weights = []
    for first in (24, 24 + planes):
        expand = (source_lane == first + (part_lane >> 5)).astype(BF16)
        values = sum(dot(part, expand) for part in split3(column_tab[...]))
        values = split3(values)
        rows = []
        for h in range(2):
            pick = (cell == (unit_row & 15) * TS + h * 8 + (unit_row >> 4)).astype(BF16)
            rows.append(sum(dot(pick, part) for part in values))
        unit_weights.append(jnp.where((part_lane & TS) == 0, rows[0], rows[1]))
    loads[6].wait()
    ends = jnp.zeros((8, cy), F32)
    for z in range(planes):
        value = dot(xends_tab[z], jnp.concatenate(split2(target[z]), axis=1))
        ends += value[:8, :cy] + (value[:8, cy:] + value[8:, :cy])
    unit_ends = [jnp.zeros((8, LANES), F32), jnp.zeros((8, LANES), F32)]

    def collect(c, j):
        rows = jnp.concatenate(
            [slots_in[pl.ds((c * 8 + ih) * BLOCK + j * GROUP, GROUP), :] for ih in range(8)],
            axis=0,
        )
        value = dot(selects[c % 3][j], jnp.concatenate(split2(rows), axis=1))
        return value[:, :LANES] + value[:, LANES:]

    def partial_row(c, s):
        return (c * 2 + s) * LANES

    sides = ((0, 1), (1, 3))

    def send_partial(c, s, move, r):
        at = pl.ds(partial_row(c, s) + r * half, half)
        remote(
            partial_out.at[at], partial_in.at[at],
            partial_send, partial_recv.at[c], device({AXES[c % 3][2]: move}, 0),
        )

    for c in range(UNITS):
        whole(slots_in, (c * 8 + 1) * BLOCK, 7 * (BLOCK - GROUP), slot_recv.at[c])
        far_out[pl.ds(c * LANES, LANES), :] = collect(c, 2)
        for s, move in sides:
            at = pl.ds(c * LANES + s * half, half)
            remote(
                far_out.at[at], far_in.at[at],
                far_send, far_recv.at[c], device({AXES[c % 3][2]: move}, 0),
            )
        for s, move in sides:
            partial_out[pl.ds(partial_row(c, s), LANES), :] = collect(c, move)
            send_partial(c, s, move, 1 - s)
        if c >= LAG:
            send_slots(c - LAG, 0, GROUP, own_recv)
    for c in range(UNITS - LAG, UNITS):
        send_slots(c, 0, GROUP, own_recv)
    for c in range(UNITS):
        whole(far_in, c * LANES, LANES, far_recv.at[c])
        for s, move in sides:
            at = pl.ds(partial_row(c, s) + s * half, half)
            partial_out[at, :] = (
                partial_out[at, :] + far_in[pl.ds(c * LANES + s * half, half), :]
            )
            send_partial(c, s, move, s)
    for c in range(UNITS):
        whole(slots_in, (c * 8 + 1) * BLOCK, 7 * GROUP, own_recv.at[c])
        own_sum[pl.ds(c * LANES, LANES), :] = collect(c, 0)
    for c in range(UNITS):
        whole(partial_in, partial_row(c, 0), 2 * LANES, partial_recv.at[c])
        total = (
            own_sum[pl.ds(c * LANES, LANES), :]
            + partial_in[pl.ds(partial_row(c, 0), LANES), :]
            + partial_in[pl.ds(partial_row(c, 1), LANES), :]
        )
        for i in range(2):
            terms = [
                total[xo * 8 : (xo + 1) * 8] * unit_weights[i][c * 16 + xo : c * 16 + xo + 1]
                for xo in range(tile_rows)
            ]
            while len(terms) > 1:
                terms = [a + b for a, b in zip(terms[::2], terms[1::2])]
            unit_ends[i] = unit_ends[i] + terms[0]
        regroup[pl.ds(c, LANES, stride=PITCH), :] = total

    lane = iota((8, LANES), 1)
    last, first = [a + pltpu.roll(a, LANES - TS, 1) for a in unit_ends]
    block = lane >> 4 == iota((8, LANES), 0)
    for i, value in enumerate((last, first)):
        for z in range(planes):
            moved = pltpu.roll(value, (LANES - 2 * TS * z) % LANES, 1) if z else value
            moved = pltpu.roll(moved, 0, 1, stride=TS, stride_axis=0)
            moved = jnp.sum(jnp.where(block, moved, 0.0), axis=0, keepdims=True)
            ends -= jnp.where(row8 == i * planes + z, moved, 0.0)
    xmsg[...] = ends
    for s in range(4):
        for h in range(2):
            if s + h:
                remote(xmsg, xall.at[p], x_send, x_recv, device({1: s}, h))
    xall[p] = ends
    at_last = jnp.sum(ends * last_rows, axis=1, keepdims=True)
    at_first = jnp.sum(ends * first_rows, axis=1, keepdims=True)
    corner = jnp.sum(
        jnp.where(corner_row, jnp.where((corner_lane & 4) == 0, at_last, at_first), 0.0),
        axis=0, keepdims=True,
    )
    here_block = p * n_gy + q
    corner_out[0] = corner
    corners[here_block] = corner
    for far in (2, 1, 3, 0):
        for dz in (2, 1, 3, 0):
            for dx in (2, 1, 3, 0):
                for h in range(2):
                    if far + h + dz + dx:
                        remote(
                            corner_out.at[0], corners.at[here_block], corner_send, corner_recv,
                            device({1: far, 2: dz, 0: dx}, h),
                        )
    for xo in range(tile_rows):
        parts = [
            regroup[pl.ds((xo * tile_cols + yo) * PITCH, UNITS), :] for yo in range(tile_cols)
        ]
        for g, value in enumerate(block_transpose(parts)):
            pushed_ref[g // 2, pl.ds(xo * TS + (g % 2) * 8, 8), :] = value
    for z in range(planes):
        halves[z] = jnp.concatenate(split2(target[z] - pushed_ref[z]), axis=1)
    y_ends = jnp.zeros((8, cx), F32)
    for z in range(planes):
        both = halves[z]
        value = dot(xtab_hi[z], both)
        value = value[:, :cy] + (value[:, cy:] + dot(xtab_lo[z], both[:, :cy]))
        smooth[z] = value
        value = dot(yends_tab[z], jnp.concatenate(split2(value), axis=0), ((1,), (1,)))
        y_ends += value[:8, :cx] + (value[:8, cx:] + value[8:, :cx])
    ymsg[...] = y_ends
    for dz in range(4):
        for dx in range(4):
            if dz + dx:
                remote(ymsg, yall.at[q], y_send, y_recv, device({2: dz, 0: dx}, 0))
    yall[q] = y_ends
    whole(xall, 0, n_gx - 1, x_recv)
    flow = inflow(0, n_gx, xall, cy)

    loads[7].wait()
    for z in range(planes):
        value = smooth[z] + (
            xfill[z] * flow[z : z + 1] + xfill[planes + z] * flow[planes + z : planes + z + 1]
        )
        potential[z] = potential[z] + dot3(split2(value), (ytab_hi[z], ytab_lo[z]))
    whole(corners, 0, n_gx * n_gy - 1, corner_recv)
    direct, through = [], []
    for i in range(n_gx):
        value = corners[pl.ds(i * n_gy, n_gy)].reshape(n_gy, LANES)
        direct.append(value * corner_coef[pl.ds(i, 1), :])
        through.append(value * corner_coef[pl.ds(n_gx + i, 1), :])
    while len(direct) > 1:
        direct = [a + b for a, b in zip(direct[::2], direct[1::2])]
        through = [a + b for a, b in zip(through[::2], through[1::2])]
    crossed = direct[0] + pltpu.roll(through[0], 8, 1)
    crossed = jnp.transpose(
        jnp.concatenate([crossed, jnp.zeros((LANES - n_gy, LANES), F32)], axis=0)
    )

    def crossed_by(k):
        entered = jnp.sum(crossed[0:8] * line_coef[k], axis=1, keepdims=True)
        left = jnp.sum(crossed[8:16] * line_coef[k], axis=1, keepdims=True)
        return edge_rows[0] * entered + edge_rows[1] * left

    crossing, far_crossing = crossed_by(0), crossed_by(1)
    whole(yall, 0, n_gy - 1, y_recv)
    flow = inflow(2 * n_gx, n_gy, yall, cx)
    flow += crossing + pltpu.roll(far_crossing, planes, 0)
    hi = flow.astype(BF16).astype(F32)
    flow = jnp.concatenate([hi, flow - hi, hi, flow - hi], axis=0).astype(BF16)
    for z in range(planes):
        next_ref[z] = potential[z] + dot(flow, yfill_tab[z], ((0,), (0,)))

    whole(metas, 0, 9, meta_send)
    whole(spread_in, 0, 3 * UNITS * LANES, spread_send)
    whole(slots_out, 0, 7 * UNITS * BLOCK, slot_send)
    whole(labels_out, 0, 21, label_send)
    whole(far_out, 0, UNITS * LANES, far_send)
    whole(partial_out, 0, 2 * UNITS * LANES, partial_send)
    whole(xall, 0, n_gx - 1, x_send)
    whole(yall, 0, n_gy - 1, y_send)
    whole(corners, 0, n_gx * n_gy - 1, corner_send)


def store(pushed_ref, next_ref, pushed_out, next_out, sems):
    copies = [
        pltpu.make_async_copy(pushed_ref, pushed_out, sems.at[0]),
        pltpu.make_async_copy(next_ref, next_out, sems.at[1]),
    ]
    for copy in copies:
        copy.start()
    for copy in copies:
        copy.wait()


def per_device(source_mass, target_density, potential, dest_device, dest_tile, mass_counts, reach):
    planes, cx, cy = source_mass.shape

    def lanes(a):
        return jnp.swapaxes(a.reshape(a.shape[2:]), 0, 1)

    hbm = pl.BlockSpec(memory_space=pl.ANY)
    dma = pltpu.SemaphoreType.DMA
    vmem = pltpu.VMEM
    grid = jax.ShapeDtypeStruct((planes, cx, cy), F32)
    field = vmem((planes, cx, cy), F32)

    def rows(count):
        return vmem((count, LANES), F32)

    fields = pl.pallas_call(
        kernel,
        out_shape=(grid, grid),
        in_specs=[hbm] * 7,
        out_specs=(pl.BlockSpec(memory_space=vmem), pl.BlockSpec(memory_space=vmem)),
        scratch_shapes=[
            field, field, field, field,
            pltpu.SMEM((planes,), F32),
            vmem((3, 4, LANES), jnp.int32),
            vmem((9, 3, 4, LANES), jnp.int32),
            rows(UNITS * LANES), rows(LANES * PITCH + 16), rows(3 * UNITS * LANES),
            vmem((12, 256, LANES), BF16),
            vmem((12, 256, LANES), F32),
            vmem((3, 8 * LANES, LANES), F32),
            rows(7 * UNITS * BLOCK + 8), rows(8 * UNITS * BLOCK + 8),
            vmem((24, 1, LANES), F32),
            vmem((24, 1, LANES), F32),
            rows(UNITS * LANES), rows(UNITS * LANES),
            rows(2 * UNITS * LANES), rows(2 * UNITS * LANES), rows(UNITS * LANES),
            vmem((planes, cx, cx), BF16),
            vmem((planes, cx, cx), BF16),
            vmem((planes, cy, cy), BF16),
            vmem((planes, cy, cy), BF16),
            vmem((planes, 16, cx), BF16),
            vmem((planes, 16, cy), BF16),
            vmem((2 * planes, cx, LANES), F32),
            vmem((planes, 32, cy), BF16),
            vmem((48, 8, LANES), F32),
            vmem((2, 8, cx), F32),
            vmem((cx, LANES), F32),
            vmem((planes, cx, 2 * cy), BF16),
            vmem((2, 8, LANES), F32),
            vmem((16, LANES), F32),
            vmem((1, 1, LANES), F32),
            vmem((LANES, 1, LANES), F32),
            vmem((8, cy), F32),
            vmem((8, 8, cy), F32),
            vmem((8, cx), F32),
            vmem((16, 8, cx), F32),
            dma((8,)), dma, dma((3,)), dma, dma((UNITS,)),
            dma, dma((UNITS,)), dma((UNITS,)), dma, dma((3,)), dma, dma((UNITS,)),
            dma, dma((UNITS,)),
            dma, dma, dma, dma, dma, dma,
        ],
        compiler_params=pltpu.CompilerParams(collective_id=0, has_side_effects=True, vmem_limit_bytes=40 * 1024 * 1024),
        name="dual_step",
    )(
        *[
            pltpu.with_memory_space_constraint(a, pltpu.HBM)
            for a in (
                source_mass, target_density, potential,
                lanes(dest_device), lanes(dest_tile), lanes(mass_counts), reach,
            )
        ],
    )

    local = pl.BlockSpec(memory_space=vmem)
    return pl.pallas_call(
        store,
        out_shape=(grid, grid),
        in_specs=[local, local],
        out_specs=(hbm, hbm),
        scratch_shapes=[dma((2,))],
        compiler_params=pltpu.CompilerParams(vmem_limit_bytes=4 * 1024 * 1024),
        name="store",
    )(*fields)


def solution(mesh):
    in_specs = (
        P(None, "gx", "gy"),
        P(None, "gx", "gy"),
        P(None, "gx", "gy"),
        P("gx", "gy", None, None),
        P("gx", "gy", None, None),
        P("gx", "gy", None, None),
        P(),
    )
    out_specs = (P(None, "gx", "gy"), P(None, "gx", "gy"))
    return jax.shard_map(
        per_device, mesh=mesh, in_specs=in_specs, out_specs=out_specs, check_vma=False
    )
```
